32 devices in a mesh: grp: 2 (over y), slab: 8 (over z, x), col: 2 (over core).
Axes of the slice: x: 2, y: 2, z: 4, core: 2. Of those that a mesh axis runs over, the one named last changes fastest.
Arguments:
- states: float32 [4, 64, 128, 1024], P(None, ('grp', 'slab'), 'col'), parts along dimension 1, may hold values from 0 to 1.4, as said below
- cond: float32 [6, 16, 32, 256], P(None, ('grp', 'slab'), 'col'), parts along dimension 1, may hold values from -0.025 to 0.15, as said below
- tension: float32 [32, 64, 512], P(('grp', 'slab'), 'col'), parts along dimension 0, may hold values from 0 to 1
- fiber: int32 [16, 32, 256], P(('grp', 'slab'), 'col'), parts along dimension 0, may hold values from 0 to 63
- disp: float32 [3, 16, 32, 256], P(None, ('grp', 'slab'), 'col'), parts along dimension 1, may hold values from -0.12 to 0.12
Outputs:
- states_next: float32 [4, 64, 128, 1024], P(None, ('grp', 'slab'), 'col'), parts along dimension 1
- tension_next: float32 [32, 64, 512], P(('grp', 'slab'), 'col'), parts along dimension 0
- disp_next: float32 [3, 16, 32, 256], P(None, ('grp', 'slab'), 'col'), parts along dimension 1
- cond_next: float32 [6, 16, 32, 256], P(None, ('grp', 'slab'), 'col'), parts along dimension 1
The draws below stay inside these ranges and needn't reach their ends.
There are 2 independent parts, one for each index of `grp`. The reference program is written for one: setup_inputs(seed, part) draws one part's arguments, and reference() takes and returns one part's arrays. A program takes and returns all parts, laid end to end along the dimension named above; each array names one. Nothing has to cross between parts.
Inputs may be any that keep to these rules, and one draw needn't show every extreme that they name: `states`: component 0 lies in 0 to 1.4, components 1 to 3 in 0 to 1. `cond`: components 0 to 2 lie in 0.05 to 0.15, components 3 to 5 in -0.025 to 0.025.
All inputs are finite; a program needn't handle non-finite values.
Results may differ from the reference program's by a relative error of at most 0.0003.
Values sent between devices are 32-bit elements; how exact they have to be, the bound alone decides.
A program may use at most 192 MiB of HBM per device.

```python
import jax
import jax.numpy as jnp
from jax import lax

NX = 1024
SUB = 4
MECH_STEPS = 2
NFIB = 64
NZ = 32
NY = 128
TZ = 16
TY = 64
TX = 512
MZ = 8
MY = 32
MX = 256


def draw_states(key, part):
    keys = jax.random.split(key, 1)
    rough = jax.random.uniform(keys[0], (4, NZ, NY, NX), jnp.float32)
    scales = jnp.array([1.4, 1.0, 1.0, 1.0], jnp.float32).reshape(4, 1, 1, 1)
    return rough * scales


def draw_cond(key, part):
    keys = jax.random.split(key, 2)
    diagonal = jax.random.uniform(keys[0], (3, MZ, MY, MX), jnp.float32, 0.05, 0.15)
    cross = jax.random.uniform(keys[1], (3, MZ, MY, MX), jnp.float32, -0.025, 0.025)
    return jnp.concatenate([diagonal, cross], 0)


def set_ends(drawn, own_key, least, top_value):
    place = [jax.random.randint(jax.random.fold_in(own_key, axis), (), 0, length) for axis, length in enumerate(drawn.shape)]
    main_axis = drawn.shape.index(max(drawn.shape))
    beside = place[:main_axis] + [(place[main_axis] + 1) % drawn.shape[main_axis]] + place[main_axis + 1:]
    return drawn.at[tuple(place)].set(least).at[tuple(beside)].set(top_value)


def block_levels(own_key, dims, cuts, low, top_value):
    def one(dim, blocks):
        heights = jax.random.uniform(jax.random.fold_in(jax.random.fold_in(own_key, 6), dim), (blocks,), jnp.float32, low / len(cuts), top_value / len(cuts))
        return jnp.repeat(jnp.exp(heights), dims[dim] // blocks).reshape((-1,) + (1,) * (len(dims) - dim - 1))

    level = one(*cuts[0])
    for cut in cuts[1:]:
        level = level * one(*cut)
    return level


def gaussian(stream_key, shape, scale, most, shards=(), kind=jnp.bfloat16):
    drawn = jax.random.normal(stream_key, shape, jnp.float32) * scale
    if len(shards) > 0:
        drawn = block_levels(stream_key, shape, shards, -0.22, 0.18) * drawn
    return jnp.clip(drawn, min=-most, max=most).astype(kind)


def setup_inputs(seed: int = 0, part: int = 0) -> dict:
    key_of = jax.random.split(jax.random.key(seed), 6)
    own_keys = jax.random.split(jax.random.fold_in(key_of[5], part), 6)
    states = draw_states(jax.random.fold_in(jax.random.fold_in(key_of[5], part), 71), part)
    cond = draw_cond(jax.random.fold_in(jax.random.fold_in(key_of[5], part), 71), part)
    tension = jnp.clip(1.0 * jax.random.uniform(own_keys[2], (TZ, TY, TX), jnp.float32) ** block_levels(own_keys[2], (TZ, TY, TX), ((0, 8), (1, 2)), -0.2, 0.2), 0.0, 1.0)
    fiber = set_ends(jax.random.randint(own_keys[3], (MZ, MY, MX), 0, NFIB), jax.random.fold_in(own_keys[3], 1), 0, NFIB - 1).astype(jnp.int32)
    disp = gaussian(own_keys[4], (3, MZ, MY, MX), 0.03, 0.12, ((1, 8), (2, 2)), jnp.float32)
    return dict(states=states, cond=cond, tension=tension, fiber=fiber, disp=disp)


SHARP = 50.0
STEP_TIME = 0.05
LAME_FIRST = 1.0
SHEAR = 0.5
ACTIVE_GAIN = 0.5
MECH_RATE = 0.15
SIGMA_LONG = 0.16
SIGMA_TRANS = 0.04
SMOOTH_WEIGHTS = (0.125, 0.75, 0.125)
SLOPE_WEIGHTS = (-0.5, 0.0, 0.5)
PAIRS = ((0, 0), (1, 1), (2, 2), (0, 1), (0, 2), (1, 2))


def switch(value):
    return 0.5 * (1.0 + jnp.tanh(SHARP * value))


def ionic_rates(volt, gate_v, gate_w, gate_s):
    high_v = switch(volt - 0.3)
    high_w = switch(volt - 0.13)
    high_o = switch(volt - 0.006)
    tau_vminus = (1.0 - high_o) * 60.0 + high_o * 1150.0
    tau_wminus = 60.0 + (15.0 - 60.0) * 0.5 * (1.0 + jnp.tanh(65.0 * (volt - 0.03)))
    tau_soft = 30.0181 + (0.9957 - 30.0181) * 0.5 * (1.0 + jnp.tanh(2.0458 * (volt - 0.65)))
    tau_slow = (1.0 - high_w) * 2.7342 + high_w * 16.0
    tau_open = (1.0 - high_o) * 400.0 + high_o * 6.0
    v_inf = 1.0 - high_o
    w_inf = (1.0 - high_o) * (1.0 - volt / 0.07) + high_o * 0.94
    fast_current = -gate_v * high_v * (volt - 0.3) * (1.55 - volt) / 0.11
    outward = volt * (1.0 - high_w) / tau_open + high_w / tau_soft
    slow_current = -high_w * gate_w * gate_s / 1.8875
    rate_v = (1.0 - high_v) * (v_inf - gate_v) / tau_vminus - high_v * gate_v / 1.4506
    rate_w = (1.0 - high_w) * (w_inf - gate_w) / tau_wminus - high_w * gate_w / 200.0
    rate_s = (0.5 * (1.0 + jnp.tanh(2.0994 * (volt - 0.9087))) - gate_s) / tau_slow
    return -(fast_current + outward + slow_current), rate_v, rate_w, rate_s


def diffusion(padded, coeff):
    centre = padded[1:-1, 1:-1, 1:-1]
    along_z = padded[2:, 1:-1, 1:-1] + padded[:-2, 1:-1, 1:-1] - 2.0 * centre
    along_y = padded[1:-1, 2:, 1:-1] + padded[1:-1, :-2, 1:-1] - 2.0 * centre
    along_x = padded[1:-1, 1:-1, 2:] + padded[1:-1, 1:-1, :-2] - 2.0 * centre
    cross_zy = 0.25 * (padded[2:, 2:, 1:-1] - padded[2:, :-2, 1:-1] - padded[:-2, 2:, 1:-1] + padded[:-2, :-2, 1:-1])
    cross_zx = 0.25 * (padded[2:, 1:-1, 2:] - padded[2:, 1:-1, :-2] - padded[:-2, 1:-1, 2:] + padded[:-2, 1:-1, :-2])
    cross_yx = 0.25 * (padded[1:-1, 2:, 2:] - padded[1:-1, 2:, :-2] - padded[1:-1, :-2, 2:] + padded[1:-1, :-2, :-2])
    return (coeff[0] * along_z + coeff[1] * along_y + coeff[2] * along_x
            + 2.0 * (coeff[3] * cross_zy + coeff[4] * cross_zx + coeff[5] * cross_yx))


def excite_step(padded, volt, gate_v, gate_w, gate_s, coeff):
    ion, rate_v, rate_w, rate_s = ionic_rates(volt, gate_v, gate_w, gate_s)
    new_volt = volt + diffusion(padded, coeff) + STEP_TIME * ion
    return new_volt, gate_v + STEP_TIME * rate_v, gate_w + STEP_TIME * rate_w, gate_s + STEP_TIME * rate_s


def upsample(cond):
    return jnp.repeat(jnp.repeat(jnp.repeat(cond, 4, axis=1), 4, axis=2), 4, axis=3)


def coarsen(field):
    shaped = field.reshape(field.shape[0] // 2, 2, field.shape[1] // 2, 2, field.shape[2] // 2, 2)
    return jnp.mean(shaped, axis=(1, 3, 5))


def fiber_dir(fiber):
    block_index = fiber.astype(jnp.float32)
    theta = -1.0 + 2.0 * block_index / (NFIB - 1)
    tilt = 0.3 * jnp.sin(3.0 * block_index)
    return jnp.stack([jnp.sin(tilt), jnp.cos(tilt) * jnp.sin(theta), jnp.cos(tilt) * jnp.cos(theta)])


def along(field, axis_pos, weights):
    count = field.shape[axis_pos] - 2
    total = weights[0] * lax.slice_in_dim(field, 0, count, axis=axis_pos)
    total = total + weights[1] * lax.slice_in_dim(field, 1, count + 1, axis=axis_pos)
    return total + weights[2] * lax.slice_in_dim(field, 2, count + 2, axis=axis_pos)


def spline_op(padded, direction):
    result = padded
    for dim_pos in range(3):
        result = along(result, dim_pos + 1, SLOPE_WEIGHTS if dim_pos == direction else SMOOTH_WEIGHTS)
    return result


def deformation(padded_disp):
    grads = [spline_op(padded_disp, direction) for direction in range(3)]
    return [[grads[col_pos][row_pos] + (1.0 if row_pos == col_pos else 0.0) for col_pos in range(3)] for row_pos in range(3)]


def first_piola(deform, active, fdir):
    right = [[deform[0][a_pos] * deform[0][b_pos] + deform[1][a_pos] * deform[1][b_pos] + deform[2][a_pos] * deform[2][b_pos]
              for b_pos in range(3)] for a_pos in range(3)]
    strain = [[0.5 * (right[a_pos][b_pos] - (1.0 if a_pos == b_pos else 0.0)) for b_pos in range(3)] for a_pos in range(3)]
    trace_e = strain[0][0] + strain[1][1] + strain[2][2]
    second = []
    for a_pos in range(3):
        row_list = []
        for b_pos in range(3):
            entry = 2.0 * SHEAR * strain[a_pos][b_pos] + ACTIVE_GAIN * active * fdir[a_pos] * fdir[b_pos]
            if a_pos == b_pos:
                entry = LAME_FIRST * trace_e + entry
            row_list.append(entry)
        second.append(row_list)
    pieces = []
    for a_pos in range(3):
        for i_pos in range(3):
            pieces.append(deform[i_pos][0] * second[0][a_pos] + deform[i_pos][1] * second[1][a_pos] + deform[i_pos][2] * second[2][a_pos])
    return jnp.stack(pieces)


def forces(padded_piola):
    total = spline_op(padded_piola[0:3], 0)
    total = total + spline_op(padded_piola[3:6], 1)
    return total + spline_op(padded_piola[6:9], 2)


def metric(deform, fdir):
    det_f = (deform[0][0] * (deform[1][1] * deform[2][2] - deform[1][2] * deform[2][1])
             - deform[0][1] * (deform[1][0] * deform[2][2] - deform[1][2] * deform[2][0])
             + deform[0][2] * (deform[1][0] * deform[2][1] - deform[1][1] * deform[2][0]))
    inverse = [[None, None, None] for row_pos in range(3)]
    for i_pos in range(3):
        for j_pos in range(3):
            cofac = (deform[(i_pos + 1) % 3][(j_pos + 1) % 3] * deform[(i_pos + 2) % 3][(j_pos + 2) % 3]
                     - deform[(i_pos + 1) % 3][(j_pos + 2) % 3] * deform[(i_pos + 2) % 3][(j_pos + 1) % 3])
            inverse[j_pos][i_pos] = cofac / det_f
    along_fiber = [inverse[a_pos][0] * fdir[0] + inverse[a_pos][1] * fdir[1] + inverse[a_pos][2] * fdir[2] for a_pos in range(3)]
    comps = []
    for a_pos, b_pos in PAIRS:
        inv_metric = inverse[a_pos][0] * inverse[b_pos][0] + inverse[a_pos][1] * inverse[b_pos][1] + inverse[a_pos][2] * inverse[b_pos][2]
        comps.append(SIGMA_TRANS * inv_metric + (SIGMA_LONG - SIGMA_TRANS) * along_fiber[a_pos] * along_fiber[b_pos])
    return jnp.stack(comps)


def mechanics(disp, active, fdir, extend):
    for turn_index in range(MECH_STEPS):
        deform = deformation(extend(disp))
        piola = first_piola(deform, active, fdir)
        disp = disp + MECH_RATE * forces(extend(piola))
    deform = deformation(extend(disp))
    return disp, metric(deform, fdir)


def pad_space(field):
    return jnp.pad(field, ((0, 0), (1, 1), (1, 1), (1, 1)))


def reference(states, cond, tension, fiber, disp):
    volt, gate_v, gate_w, gate_s = states[0], states[1], states[2], states[3]
    coeff = upsample(cond)
    for turn_index in range(SUB):
        padded = jnp.pad(volt, 1)
        volt, gate_v, gate_w, gate_s = excite_step(padded, volt, gate_v, gate_w, gate_s, coeff)
    states_next = jnp.stack([volt, gate_v, gate_w, gate_s])
    tension_next = tension + 0.5 * (coarsen(volt) - tension)
    active = coarsen(tension_next)
    fdir = fiber_dir(fiber)
    disp_next, cond_next = mechanics(disp, active, fdir, pad_space)
    return states_next, tension_next, disp_next, cond_next
```

```python
import functools

import jax
import jax.numpy as jnp
from jax import lax
from jax.experimental import pallas as pl
from jax.experimental.pallas import tpu as pltpu
from jax.sharding import PartitionSpec as P

SUB = 4
MECH_STEPS = 2
NFIB = 64
STEP_TIME = 0.05
MECH_RATE = 0.15
SIGMA_LONG = 0.16
SIGMA_TRANS = 0.04
PAIRS = ((0, 0), (1, 1), (2, 2), (0, 1), (0, 2), (1, 2))
MESH = pl.DeviceIdType.MESH
HI = lax.Precision.HIGHEST
F32 = jnp.float32
TILE = 8
CHUNK = 256
RADIUS = 2 * MECH_STEPS + 1
REACH = RADIUS - 1
ALONG = (-4, -2, 2, 4)
BEYOND = (-6, -4, -2, 2, 4, 6)
PEERS = (-6, -4, -3, -2, -1, 0, 1, 2, 3, 4, 6)
JOIN = 12


def ionic(u, v, w, s):
    th_v = jnp.tanh(50.0 * (u - 0.3))
    th_w = jnp.tanh(50.0 * (u - 0.13))
    th_o = jnp.tanh(50.0 * (u - 0.006))
    th_m = jnp.tanh(65.0 * (u - 0.03))
    th_s = jnp.tanh(2.0458 * (u - 0.65))
    th_r = jnp.tanh(2.0994 * (u - 0.9087))
    hv = 0.5 + 0.5 * th_v
    hw = 0.5 + 0.5 * th_w
    ho = 0.5 + 0.5 * th_o
    nv = 1.0 - hv
    nw = 1.0 - hw
    no = 1.0 - ho
    tau_v = 605.0 + 545.0 * th_o
    tau_w = 37.5 - 22.5 * th_m
    tau_so = 15.5069 - 14.5112 * th_s
    tau_s = 9.3671 + 6.6329 * th_w
    tau_o = 203.0 - 197.0 * th_o
    w_inf = no * (1.0 - u * (1.0 / 0.07)) + 0.94 * ho
    fast = v * hv * (u - 0.3) * (1.55 - u) * (STEP_TIME / 0.11)
    slow = hw * (w * s) * (STEP_TIME / 1.8875)
    out = (u * nw * tau_so + hw * tau_o) * (STEP_TIME / (tau_o * tau_so))
    du = fast - out + slow
    inv = STEP_TIME / (tau_v * tau_w)
    v2 = v + nv * (no - v) * (tau_w * inv) - hv * v * (STEP_TIME / 1.4506)
    w2 = w + nw * (w_inf - w) * (tau_v * inv) - hw * w * (STEP_TIME / 200.0)
    s2 = s + (0.5 + 0.5 * th_r - s) * (STEP_TIME / tau_s)
    return du, v2, w2, s2


def iota2(shape, dim):
    return lax.broadcasted_iota(jnp.int32, shape, dim)


def first_piola(f, active=None, fdir=None):
    second = {}
    for a in range(3):
        for b in range(a, 3):
            right = f[0][a] * f[0][b] + f[1][a] * f[1][b] + f[2][a] * f[2][b]
            second[a, b] = 0.5 * (right - (1.0 if a == b else 0.0))
    trace = second[0, 0] + second[1, 1] + second[2, 2]
    for a in range(3):
        if active is not None:
            scaled = 0.5 * active * fdir[a]
            for b in range(a, 3):
                second[a, b] = second[a, b] + scaled * fdir[b]
        second[a, a] = second[a, a] + trace
    for a in range(3):
        for b in range(a):
            second[a, b] = second[b, a]
    return [
        f[i][0] * second[0, a] + f[i][1] * second[1, a] + f[i][2] * second[2, a]
        for a in range(3)
        for i in range(3)
    ]


def metric(f, fdir):
    cof = [[None] * 3 for _ in range(3)]
    for i in range(3):
        for j in range(3):
            cof[i][j] = (
                f[(i + 1) % 3][(j + 1) % 3] * f[(i + 2) % 3][(j + 2) % 3]
                - f[(i + 1) % 3][(j + 2) % 3] * f[(i + 2) % 3][(j + 1) % 3]
            )
    det = f[0][0] * cof[0][0] + f[0][1] * cof[0][1] + f[0][2] * cof[0][2]
    scale = 1.0 / det
    inverse = [[cof[i][j] * scale for i in range(3)] for j in range(3)]
    g = [inverse[a][0] * fdir[0] + inverse[a][1] * fdir[1] + inverse[a][2] * fdir[2] for a in range(3)]
    comps = []
    for a, b in PAIRS:
        inner = (
            inverse[a][0] * inverse[b][0]
            + inverse[a][1] * inverse[b][1]
            + inverse[a][2] * inverse[b][2]
        )
        comps.append(SIGMA_TRANS * inner + (SIGMA_LONG - SIGMA_TRANS) * (g[a] * g[b]))
    return comps


class Stencils:
    def __init__(self, rows, width):
        self.rows, self.width = rows, width
        self.lane = iota2((rows, width), 1)
        self.line = iota2((rows, width), 0)

    def left(self, f):
        return jnp.where(self.lane == 0, 0.0, pltpu.roll(f, 1, 1))

    def right(self, f):
        return jnp.where(self.lane == self.width - 1, 0.0, pltpu.roll(f, self.width - 1, 1))

    def south(self, f):
        return jnp.where(self.line == 0, 0.0, pltpu.roll(f, 1, 0))

    def north(self, f):
        return jnp.where(self.line == self.rows - 1, 0.0, pltpu.roll(f, self.rows - 1, 0))

    def sx(self, f):
        return 0.125 * (self.left(f) + self.right(f)) + 0.75 * f

    def dx(self, f):
        return 0.5 * (self.right(f) - self.left(f))

    def sy(self, f):
        return 0.125 * (self.south(f) + self.north(f)) + 0.75 * f

    def dy(self, f):
        return 0.5 * (self.north(f) - self.south(f))

    def deformation(self, field):
        f = []
        for i in range(3):
            low, mid, high = field(i, -1), field(i, 0), field(i, 1)
            zs = 0.125 * (low + high) + 0.75 * mid
            zd = 0.5 * (high - low)
            f.append([self.sy(self.sx(zd)), self.dy(self.sx(zs)), self.sy(self.dx(zs))])
            f[i][i] = f[i][i] + 1.0
        return f

    def force(self, stress, i):
        zd = 0.5 * (stress(i, 1) - stress(i, -1))
        ys = 0.125 * (stress(3 + i, -1) + stress(3 + i, 1)) + 0.75 * stress(3 + i, 0)
        xs = 0.125 * (stress(6 + i, -1) + stress(6 + i, 1)) + 0.75 * stress(6 + i, 0)
        return self.sy(self.sx(zd) + self.dx(xs)) + self.dy(self.sx(ys))


def sine(x):
    y = x * x
    c = 1.0
    for n in (12, 10, 8, 6, 4, 2):
        c = 1.0 - y * (1.0 / (n * (n + 1))) * c
    return x * c


def cosine(x):
    y = x * x
    c = 1.0
    for n in (13, 11, 9, 7, 5, 3, 1):
        c = 1.0 - y * (1.0 / (n * (n + 1))) * c
    return c


def directions(index):
    theta = -1.0 + index * (2.0 / (NFIB - 1))
    tilt = 0.3 * jnp.sin(3.0 * index)
    flat = cosine(tilt)
    return [sine(tilt), flat * sine(theta), flat * cosine(theta)]


def excite_kernel(
    slabs, states, cond_hbm, ten_hbm, fib_hbm, disp_hbm,
    out_hbm, ten_out, act_hbm, shift_hbm, pull_hbm,
    ubuf, out, cond, tension, coeff, dif, act_win, fix_win, fiber, passive, shifted, pull,
    load_sem, store_sem, sz, rz, sc, rc, sy, ry, sa, ra, sf, rf, sg,
):
    grp = lax.axis_index("grp")
    slab = lax.axis_index("slab")
    col = lax.axis_index("col")
    other = 1 - col
    depth, rows, width = out.shape[1:]
    tiles = rows // TILE
    has_up = slab < slabs - 1
    has_dn = slab > 0
    edge_src = rows - (rows - TILE) * col
    edge_dst = (rows + TILE) * col

    load_u = pltpu.make_async_copy(
        states.at[0], ubuf.at[0, pl.ds(1, depth), pl.ds(TILE, rows), :], load_sem.at[0]
    )
    load_g = pltpu.make_async_copy(
        states.at[pl.ds(1, 3)], out.at[pl.ds(1, 3)], load_sem.at[1]
    )
    load_c = pltpu.make_async_copy(cond_hbm, cond, load_sem.at[2])
    load_t = pltpu.make_async_copy(ten_hbm, tension, load_sem.at[3])
    load_u.start()
    load_c.start()
    load_g.start()
    load_t.start()
    half = rows // 4
    span = half + TILE
    own = pl.ds(pl.multiple_of(TILE * col, TILE), half)
    near = pl.ds(TILE, TILE)
    far = pl.ds(pl.multiple_of(2 * TILE * col, TILE), TILE)
    load_d = pltpu.make_async_copy(
        disp_hbm.at[:, 0], fix_win.at[RADIUS, pl.ds(0, 3), own, :], load_sem.at[4]
    )
    load_f = pltpu.make_async_copy(fib_hbm, fiber, load_sem.at[5])
    load_d.start()
    load_f.start()

    barrier = pltpu.get_barrier_semaphore()

    def greet(where):
        pl.semaphore_signal(barrier, inc=1, device_id=where, device_id_type=MESH)

    def there(d):
        return (slab + d >= 0) & (slab + d < slabs)

    peers = 0
    for d in PEERS:
        valid = there(d)
        wide = abs(d) <= REACH
        count = (0 if d == 0 else 1) + (1 if wide else 0)
        peers = peers + count * valid.astype(jnp.int32)

        @pl.when(valid)
        def _(d=d, wide=wide):
            if wide:
                greet((grp, slab + d, other))
            if d != 0:
                greet((grp, slab + d, col))

    for d in range(-RADIUS, RADIUS + 1):

        @pl.when(jnp.logical_not(there(d)))
        def _(d=d):
            fix_win[d + RADIUS] = jnp.zeros(fix_win.shape[1:], F32)
            if abs(d) <= REACH:
                act_win[d + REACH] = jnp.zeros(act_win.shape[1:], F32)

    blank = jnp.zeros((TILE, width), F32)

    def clear_y(n, c):
        ubuf[n // (depth + 2), n % (depth + 2), pl.ds(pl.multiple_of(edge_dst, TILE), TILE), :] = blank
        return c

    lax.fori_loop(0, SUB * (depth + 2), clear_y, 0)

    def clear_z(layer):
        per = rows // TILE + 2

        def body(n, c):
            ubuf[n // per, layer, pl.ds(pl.multiple_of((n % per) * TILE, TILE), TILE), :] = blank
            return c

        lax.fori_loop(0, SUB * per, body, 0)

    @pl.when(slab == 0)
    def _():
        clear_z(0)

    @pl.when(slab == slabs - 1)
    def _():
        clear_z(depth + 1)

    def row_of(step):
        return jnp.where(col == 1, step, tiles - 1 - step)

    def copy_z(slot, way, step):
        at = pl.ds(pl.multiple_of(TILE + TILE * row_of(step), TILE), TILE)
        src = depth if way == 0 else 1
        dst = 0 if way == 0 else depth + 1
        to = slab + 1 if way == 0 else slab - 1
        return pltpu.make_async_remote_copy(
            src_ref=ubuf.at[slot, src, at, :],
            dst_ref=ubuf.at[slot, dst, at, :],
            send_sem=sz.at[slot, way, step],
            recv_sem=rz.at[slot, way, step],
            device_id=(grp, to, col),
            device_id_type=MESH,
        )

    def copy_c(slot, way):
        at = depth + 1 if way == 0 else 0
        return pltpu.make_async_remote_copy(
            src_ref=ubuf.at[slot, at, pl.ds(pl.multiple_of(edge_src, TILE), TILE), :],
            dst_ref=ubuf.at[slot, at, pl.ds(pl.multiple_of(edge_dst, TILE), TILE), :],
            send_sem=sc.at[slot, way],
            recv_sem=rc.at[slot, way],
            device_id=(grp, slab, other),
            device_id_type=MESH,
        )

    def copy_y(slot):
        return pltpu.make_async_remote_copy(
            src_ref=ubuf.at[slot, pl.ds(1, depth), pl.ds(pl.multiple_of(edge_src, TILE), TILE), :],
            dst_ref=ubuf.at[slot, pl.ds(1, depth), pl.ds(pl.multiple_of(edge_dst, TILE), TILE), :],
            send_sem=sy.at[slot],
            recv_sem=ry.at[slot],
            device_id=(grp, slab, other),
            device_id_type=MESH,
        )

    def both(do_up, do_dn):
        pl.when(has_up)(do_up)
        pl.when(has_dn)(do_dn)

    def send_z(slot, step):
        both(lambda: copy_z(slot, 0, step).start(), lambda: copy_z(slot, 1, step).start())

    def send_c(slot):
        both(lambda: copy_c(slot, 0).start(), lambda: copy_c(slot, 1).start())

    def recv_z(slot, step):
        both(lambda: copy_z(slot, 1, step).wait_recv(), lambda: copy_z(slot, 0, step).wait_recv())

    def recv_c(slot):
        both(lambda: copy_c(slot, 0).wait_recv(), lambda: copy_c(slot, 1).wait_recv())

    beside = 1 - 2 * lax.rem(slab, 2)

    def copy_f(source, d, n):
        slot = RADIUS + source - d
        return pltpu.make_async_remote_copy(
            src_ref=fix_win.at[RADIUS + source, :, own, :],
            dst_ref=fix_win.at[slot, :, own, :],
            send_sem=sf.at[n],
            recv_sem=rf.at[slot],
            device_id=(grp, slab + d, col),
            device_id_type=MESH,
        )

    def come_f(e):
        return pltpu.make_async_remote_copy(
            src_ref=fix_win.at[RADIUS, :, own, :],
            dst_ref=fix_win.at[RADIUS + e, :, own, :],
            send_sem=sf.at[0],
            recv_sem=rf.at[RADIUS + e],
            device_id=(grp, slab + e, col),
            device_id_type=MESH,
        )

    def share_f(whose):
        return pltpu.make_async_remote_copy(
            src_ref=fix_win.at[:, :, near, :],
            dst_ref=fix_win.at[:, :, pl.ds(pl.multiple_of(2 * TILE * whose, TILE), TILE), :],
            send_sem=sg.at[0],
            recv_sem=sg.at[1],
            device_id=(grp, slab, other),
            device_id_type=MESH,
        )

    def forward_f(act):
        for n, d in enumerate(BEYOND):
            ok = there(d) & (jnp.abs(d - beside) <= RADIUS)
            pl.when(ok)(lambda n=n, d=d: act(n, d))

    def relay_f(n, d):
        return copy_f(beside, d, 1 + len(ALONG) + n)

    pl.semaphore_wait(barrier, peers)

    load_u.wait()
    send_z(0, 0)
    copy_y(0).start()
    send_z(0, 1)
    load_d.wait()
    load_f.wait()
    fix_win[RADIUS, 3, own, :] = fiber[0].astype(F32)
    copy_f(0, beside, 0).start()
    for n, d in enumerate(ALONG):
        pl.when(there(d))(lambda n=n, d=d: copy_f(0, d, 1 + n).start())

    def initial(step, c):
        send_z(0, step)
        return c

    lax.fori_loop(2, tiles, initial, 0)
    load_c.wait()

    spread_x = (iota2((128, 512), 0) == iota2((128, 512), 1) // 4).astype(F32)
    spread_y = (iota2((rows, rows // 4), 0) // 4 == iota2((rows, rows // 4), 1)).astype(F32)
    for c in range(6):
        for h in range(width // 512):
            part = jnp.dot(
                cond[c, 0, :, h * 128 : (h + 1) * 128], spread_x, precision=HI,
                preferred_element_type=F32,
            )
            part = jnp.dot(spread_y, part, precision=HI, preferred_element_type=F32)
            coeff[c, :, h * 512 : (h + 1) * 512] = part if c < 3 else 0.5 * part

    load_g.wait()
    load_t.wait()

    lane = iota2((TILE, width), 1)

    def left(f):
        return jnp.where(lane == 0, 0.0, pltpu.roll(f, 1, 1))

    def right(f):
        return jnp.where(lane == width - 1, 0.0, pltpu.roll(f, width - 1, 1))

    def layer(k, z, r):
        base = pl.multiple_of(TILE * r, TILE)
        here = pl.ds(base, TILE)
        tall = pl.ds(base, 3 * TILE)
        below = ubuf[k, z, tall, :]
        mid = ubuf[k, z + 1, tall, :]
        above = ubuf[k, z + 2, tall, :]
        odd = above - below
        centre = mid[TILE : 2 * TILE]
        odd0 = odd[TILE : 2 * TILE]
        north = mid[TILE + 1 : 2 * TILE + 1]
        south = mid[TILE - 1 : 2 * TILE - 1]
        slope = north - south
        twice = 2.0 * centre
        total = coeff[0, here, :] * (
            above[TILE : 2 * TILE] + below[TILE : 2 * TILE] - twice
        )
        total = total + coeff[1, here, :] * (north + south - twice)
        total = total + coeff[2, here, :] * (right(centre) + left(centre) - twice)
        total = total + coeff[3, here, :] * (
            odd[TILE + 1 : 2 * TILE + 1] - odd[TILE - 1 : 2 * TILE - 1]
        )
        total = total + coeff[4, here, :] * (right(odd0) - left(odd0))
        total = total + coeff[5, here, :] * (right(slope) - left(slope))
        dif[...] = total + centre
        up = pl.ds(pl.multiple_of(base + TILE, TILE), TILE)
        for x in range(0, width, CHUNK):
            xs = pl.ds(x, CHUNK)
            du, v2, w2, s2 = ionic(
                ubuf[k, z + 1, up, xs], out[1, z, here, xs], out[2, z, here, xs],
                out[3, z, here, xs],
            )
            u2 = dif[:, xs] + du
            ubuf[k + 1, z + 1, up, xs] = u2
            out[0, z, here, xs] = u2
            out[1, z, here, xs] = v2
            out[2, z, here, xs] = w2
            out[3, z, here, xs] = s2

    def leave(step):
        at = pl.ds(pl.multiple_of(TILE * row_of(step), TILE), TILE)
        return pltpu.make_async_copy(
            out.at[:, :, at, :], out_hbm.at[:, :, at, :], store_sem.at[step]
        )

    pair_x = (iota2((256, 128), 0) // 2 == iota2((256, 128), 1)).astype(F32)
    pair_y = (iota2((TILE, 2 * TILE), 0) == iota2((TILE, 2 * TILE), 1) // 2).astype(F32)
    pair_y2 = (iota2((half, 2 * half), 0) == iota2((half, 2 * half), 1) // 2).astype(F32)

    def tense(p):
        fine = pl.ds(pl.multiple_of(2 * TILE * p, 2 * TILE), 2 * TILE)
        wide = pl.ds(pl.multiple_of(TILE * p, TILE), TILE)
        for q in range(depth // 2):
            layers = out[0, 2 * q, fine, :] + out[0, 2 * q + 1, fine, :]
            pairs = 0.125 * jnp.dot(pair_y, layers, precision=HI, preferred_element_type=F32)
            for h in range(width // 256):
                mean = jnp.dot(
                    pairs[:, h * 256 : (h + 1) * 256], pair_x, precision=HI,
                    preferred_element_type=F32,
                )
                xo = slice(h * 128, (h + 1) * 128)
                before = tension[q, wide, xo]
                ten_out[q, wide, xo] = before + 0.5 * (mean - before)

    pool_x = (iota2((512, 128), 0) // 4 == iota2((512, 128), 1)).astype(F32)
    pool_y = (iota2((TILE, 4 * TILE), 0) == iota2((TILE, 4 * TILE), 1) // 4).astype(F32)

    def activate(part, lines):
        fine = pl.ds(pl.multiple_of(4 * TILE * part, 4 * TILE), 4 * TILE)
        layers = out[0, 0, fine, :]
        for z in range(1, depth):
            layers = layers + out[0, z, fine, :]
        pooled = (0.5 / (16 * depth)) * jnp.dot(
            pool_y, layers, precision=HI, preferred_element_type=F32
        )
        for h in range(width // 512):
            xo = slice(h * 128, (h + 1) * 128)
            act_win[REACH, lines, xo] = act_win[REACH, lines, xo] + jnp.dot(
                pooled[:, h * 512 : (h + 1) * 512], pool_x, precision=HI,
                preferred_element_type=F32,
            )

    def copy_a(d, to, kind, lines, at):
        return pltpu.make_async_remote_copy(
            src_ref=act_win.at[REACH, lines, :],
            dst_ref=act_win.at[REACH - d, at, :],
            send_sem=sa.at[d + REACH, kind],
            recv_sem=ra.at[REACH - d, kind],
            device_id=(grp, slab + d, to),
            device_id_type=MESH,
        )

    def each_a(act, centre):
        for d in sorted(range(-REACH, REACH + 1), key=lambda d: -abs(d)):
            if d != 0 or centre:
                pl.when(there(d))(lambda d=d: act(d))

    mech = Stencils(span, fix_win.shape[3])

    def inside(j):
        return there(j - RADIUS)

    def prepare(j):
        ok = inside(j)
        f = mech.deformation(lambda i, d: fix_win[j + d, i])
        fdir = directions(fix_win[j, 3])
        pieces = first_piola(f)
        for n in range(9):
            passive[n, j - 1] = jnp.where(ok, pieces[n], 0.0)
        for i in range(3):
            g = 0.5 * (f[i][0] * fdir[0] + f[i][1] * fdir[1] + f[i][2] * fdir[2])
            pull[i, j - 1] = jnp.where(ok, g, 0.0)
            pull[3 + i, j - 1] = fdir[i]

        @pl.when(j >= 3)
        def _():
            here = inside(j - 1)
            for i in range(3):
                force = mech.force(lambda n, d: passive[n, j - 2 + d], i)
                moved = fix_win[j - 1, i] + MECH_RATE * force
                shifted[i, j - 3] = jnp.where(here, moved, 0.0)

    hand_shift = pltpu.make_async_copy(shifted, shift_hbm, load_sem.at[0])
    hand_pull = pltpu.make_async_copy(pull, pull_hbm, load_sem.at[1])

    for h in range(width // 512):
        xs = slice(h * 256, (h + 1) * 256)
        layers = tension[0, :, xs] + tension[1, :, xs]
        mean = jnp.dot(layers, pair_x, precision=HI, preferred_element_type=F32)
        mean = 0.0625 * jnp.dot(pair_y2, mean, precision=HI, preferred_element_type=F32)
        act_win[REACH, own, h * 128 : (h + 1) * 128] = mean

    def chunk(n, c):
        k = n // tiles
        step = n % tiles
        r = row_of(step)

        @pl.when(n == tiles // 2)
        def _():
            come_f(beside).wait_recv()
            forward_f(lambda n, d: relay_f(n, d).start())

        @pl.when(n == JOIN)
        def _():
            for d in range(-RADIUS, RADIUS + 1):
                if d != 0:
                    arrives = there(d) if d % 2 == 0 else there(d) & (beside != d)
                    pl.when(arrives)(lambda d=d: come_f(d).wait_recv())
            share_f(col).start()

        @pl.when(n == JOIN + 2)
        def _():
            share_f(col).wait_recv()

        @pl.when(step == 0)
        def _():
            recv_z(k, 0)
            send_c(k)

        @pl.when(step < tiles - 1)
        def _():
            recv_z(k, step + 1)

        @pl.when(step == 0)
        def _():
            copy_y(k).wait_recv()
            recv_c(k)

        def outer(m, c):
            layer(k, m * (depth - 1), r)
            return c

        lax.fori_loop(0, 2, outer, 0)

        @pl.when(k < SUB - 1)
        def _():
            send_z(k + 1, step)

        def inner(m, c):
            layer(k, m, r)
            return c

        lax.fori_loop(1, depth - 1, inner, 0)

        @pl.when((k < SUB - 1) & (step == 0))
        def _():
            copy_y(k + 1).start()

        @pl.when((n >= JOIN + 2) & (n < JOIN + 3 + 2 * REACH))
        def _():
            prepare(n - JOIN - 1)

        @pl.when(n == JOIN + 3 + 2 * REACH)
        def _():
            hand_shift.start()
            hand_pull.start()

        @pl.when(k == SUB - 1)
        def _():
            leave(step).start()

        @pl.when(n == SUB * tiles - 1 - tiles // 2)
        def _():
            activate(other, near)
            each_a(lambda d: copy_a(d, col, 0, near, near).start(), False)
            each_a(lambda d: copy_a(d, other, 1, near, far).start(), True)

        @pl.when((k == SUB - 1) & (step % 2 == 1) & (step < tiles - 1))
        def _():
            tense(r // 2)

        return c

    lax.fori_loop(0, SUB * tiles, chunk, 0)

    activate(col, far)
    each_a(lambda d: copy_a(d, col, 2, far, far).start(), False)
    tense(row_of(tiles - 1) // 2)
    share_f(col).wait_send()
    copy_f(0, beside, 0).wait_send()
    for n, d in enumerate(ALONG):
        pl.when(there(d))(lambda n=n, d=d: copy_f(0, d, 1 + n).wait_send())
    forward_f(lambda n, d: relay_f(n, d).wait_send())
    hand_shift.wait()
    hand_pull.wait()
    copy_y(0).wait_send()

    def drain(slot, c):
        both(lambda: copy_c(slot, 0).wait_send(), lambda: copy_c(slot, 1).wait_send())

        @pl.when(slot > 0)
        def _():
            copy_y(slot).wait_send()

        def tile(step, c):
            both(
                lambda: copy_z(slot, 0, step).wait_send(),
                lambda: copy_z(slot, 1, step).wait_send(),
            )
            return c

        return lax.fori_loop(0, tiles, tile, c)

    lax.fori_loop(0, SUB, drain, 0)

    def left_all(step, c):
        leave(step).wait()
        return c

    lax.fori_loop(0, tiles, left_all, 0)
    each_a(lambda d: copy_a(d, col, 0, near, near).wait_send(), False)
    each_a(lambda d: copy_a(d, other, 1, near, far).wait_send(), True)
    each_a(lambda d: copy_a(d, col, 2, far, far).wait_send(), False)
    each_a(lambda d: copy_a(-d, col, 0, near, near).wait_recv(), False)
    each_a(lambda d: copy_a(-d, other, 1, near, far).wait_recv(), True)
    each_a(lambda d: copy_a(-d, col, 2, far, far).wait_recv(), False)
    hand_act = pltpu.make_async_copy(act_win, act_hbm, load_sem.at[0])
    hand_act.start()
    hand_act.wait()


def excite(slabs, states, cond, tension, fiber, disp):
    _, depth, rows, width = states.shape
    tiles = rows // TILE
    full = rows // 4 + TILE
    across = cond.shape[3]
    vmem = pl.BlockSpec(memory_space=pltpu.VMEM)
    hbm = pl.BlockSpec(memory_space=pltpu.HBM)
    window = (2 * REACH + 1, full, across)
    shifts = (3, 2 * REACH - 1, full, across)
    pulls = (6, 2 * REACH + 1, full, across)
    dma = pltpu.SemaphoreType.DMA
    return pl.pallas_call(
        functools.partial(excite_kernel, slabs),
        out_shape=(
            jax.ShapeDtypeStruct(states.shape, F32),
            jax.ShapeDtypeStruct(tension.shape, F32),
            jax.ShapeDtypeStruct(window, F32),
            jax.ShapeDtypeStruct(shifts, F32),
            jax.ShapeDtypeStruct(pulls, F32),
        ),
        in_specs=[hbm, hbm, hbm, hbm, hbm],
        out_specs=(hbm, vmem, hbm, hbm, hbm),
        scratch_shapes=[
            pltpu.VMEM((SUB + 1, depth + 2, rows + 2 * TILE, width), F32),
            pltpu.VMEM(states.shape, F32),
            pltpu.VMEM(cond.shape, F32),
            pltpu.VMEM(tension.shape, F32),
            pltpu.VMEM((6, rows, width), F32),
            pltpu.VMEM((TILE, width), F32),
            pltpu.VMEM(window, F32),
            pltpu.VMEM((2 * RADIUS + 1, 4, full, across), F32),
            pltpu.VMEM(fiber.shape, jnp.int32),
            pltpu.VMEM((9, *window), F32),
            pltpu.VMEM(shifts, F32),
            pltpu.VMEM(pulls, F32),
            dma((6,)),
            dma((tiles,)),
            dma((SUB, 2, tiles)),
            dma((SUB, 2, tiles)),
            dma((SUB, 2)),
            dma((SUB, 2)),
            dma((SUB,)),
            dma((SUB,)),
            dma((2 * REACH + 1, 3)),
            dma((2 * REACH + 1, 3)),
            dma((1 + len(ALONG) + len(BEYOND),)),
            dma((2 * RADIUS + 1,)),
            dma((2,)),
        ],
        compiler_params=pltpu.CompilerParams(
            collective_id=0, has_side_effects=True, vmem_limit_bytes=61 << 20
        ),
        cost_estimate=pl.CostEstimate(
            flops=200_000_000, bytes_accessed=16 << 20, transcendentals=6_000_000
        ),
        name="excite",
    )(states, cond, tension, fiber, disp)


def mech_kernel(
    slabs, active, shifted, pull, ten_in, states_in,
    disp_out, cond_out, ten_out, states_out, stress, moved, held, sem,
):
    slab = lax.axis_index("slab")
    first = lax.axis_index("col") == 0
    rows, width = active.shape[1:]
    half = rows - TILE
    fetch = pltpu.make_async_copy(states_in, held, sem.at[0])
    hand_on = pltpu.make_async_copy(held, states_out, sem.at[1])
    fetch.start()
    ten_out[...] = ten_in[...]
    mech = Stencils(rows, width)

    def inside(j):
        zz = slab + j - REACH
        return (zz >= 0) & (zz < slabs)

    def tense(j, c):
        for a in range(3):
            t = active[j] * pull[3 + a, j]
            for i in range(3):
                stress[3 * a + i, j] = t * pull[i, j]
        return c

    def move(field):
        def body(j, c):
            ok = inside(j)
            for i in range(3):
                force = mech.force(lambda n, d: stress[n, j + d], i)
                moved[i, j] = jnp.where(ok, field(i, j) + MECH_RATE * force, 0.0)
            return c

        return body

    def strain(j, c):
        ok = inside(j)
        f = mech.deformation(lambda i, d: moved[i, j + d])
        pieces = first_piola(f, active[j], [pull[3 + a, j] for a in range(3)])
        for n in range(9):
            stress[n, j] = jnp.where(ok, pieces[n], 0.0)
        return c

    lax.fori_loop(0, 2 * REACH + 1, tense, 0)
    lax.fori_loop(1, 2 * REACH, move(lambda i, j: shifted[i, j - 1]), 0)
    fetch.wait()
    hand_on.start()
    lax.fori_loop(2, 2 * REACH - 1, strain, 0)
    lax.fori_loop(3, 2 * REACH - 2, move(lambda i, j: moved[i, j]), 0)

    comps = metric(
        mech.deformation(lambda i, d: moved[i, REACH + d]),
        [pull[3 + a, REACH] for a in range(3)],
    )
    for i in range(3):
        whole = moved[i, REACH]
        disp_out[i, 0] = jnp.where(first, whole[:half], whole[TILE:])
    for n in range(6):
        cond_out[n, 0] = jnp.where(first, comps[n][:half], comps[n][TILE:])
    hand_on.wait()


def mechanics(slabs, active, shifted, pull, tension, states):
    _, full, width = active.shape
    rows = full - TILE
    vmem = pl.BlockSpec(memory_space=pltpu.VMEM)
    hbm = pl.BlockSpec(memory_space=pltpu.HBM)
    return pl.pallas_call(
        functools.partial(mech_kernel, slabs),
        out_shape=(
            jax.ShapeDtypeStruct((3, 1, rows, width), F32),
            jax.ShapeDtypeStruct((6, 1, rows, width), F32),
            jax.ShapeDtypeStruct(tension.shape, F32),
            jax.ShapeDtypeStruct(states.shape, F32),
        ),
        in_specs=[vmem, vmem, vmem, vmem, hbm],
        out_specs=(vmem, vmem, vmem, hbm),
        scratch_shapes=[
            pltpu.VMEM((9, 2 * REACH + 1, full, width), F32),
            pltpu.VMEM((3, 2 * REACH + 1, full, width), F32),
            pltpu.VMEM(states.shape, F32),
            pltpu.SemaphoreType.DMA((2,)),
        ],
        compiler_params=pltpu.CompilerParams(vmem_limit_bytes=61 << 20),
        name="mechanics",
    )(active, shifted, pull, tension, states)


def on_device(slabs, states, cond, tension, fiber, disp):
    states_next, tension_next, active, shifted, pull = excite(
        slabs, states, cond, tension, fiber, disp
    )
    disp_next, cond_next, tension_next, states_next = mechanics(
        slabs, active, shifted, pull, tension_next, states_next
    )
    return states_next, tension_next, disp_next, cond_next


def solution(mesh):
    wide = P(None, ("grp", "slab"), "col", None)
    flat = P(("grp", "slab"), "col", None)
    return jax.shard_map(
        functools.partial(on_device, mesh.shape["slab"]),
        mesh=mesh,
        in_specs=(wide, wide, flat, flat, wide),
        out_specs=(wide, flat, wide, wide),
        check_vma=False,
    )
```

```python
import functools

import jax
import jax.numpy as jnp
import numpy as np
from jax import lax
from jax.experimental import pallas as pl
from jax.experimental.pallas import tpu as pltpu
from jax.sharding import PartitionSpec as P

SUB = 4
MECH_STEPS = 2
NFIB = 64
STEP_TIME = 0.05
MECH_RATE = 0.15
SIGMA_LONG = 0.16
SIGMA_TRANS = 0.04
PAIRS = ((0, 0), (1, 1), (2, 2), (0, 1), (0, 2), (1, 2))
MESH = pl.DeviceIdType.MESH
HI = lax.Precision.HIGHEST
F32 = jnp.float32
BF16 = jnp.bfloat16
TILE = 8
CHUNK = 256
RADIUS = 2 * MECH_STEPS + 1
REACH = RADIUS - 1
ALONG = (-4, -2, 2, 4)
BEYOND = (-6, -4, -2, 2, 4, 6)
PEERS = (-6, -4, -3, -2, -1, 0, 1, 2, 3, 4, 6)
JOIN = 14


def ionic(u, v, w, s):
    th_v = jnp.tanh(50.0 * (u - 0.3))
    th_w = jnp.tanh(50.0 * (u - 0.13))
    th_o = jnp.tanh(50.0 * (u - 0.006))
    th_m = jnp.tanh(65.0 * (u - 0.03))
    th_s = jnp.tanh(2.0458 * (u - 0.65))
    th_r = jnp.tanh(2.0994 * (u - 0.9087))
    hv = 0.5 + 0.5 * th_v
    hw = 0.5 + 0.5 * th_w
    ho = 0.5 + 0.5 * th_o
    nv = 1.0 - hv
    nw = 1.0 - hw
    no = 1.0 - ho
    tau_v = 605.0 + 545.0 * th_o
    tau_w = 37.5 - 22.5 * th_m
    tau_so = 15.5069 - 14.5112 * th_s
    tau_s = 9.3671 + 6.6329 * th_w
    tau_o = 203.0 - 197.0 * th_o
    w_inf = no * (1.0 - u * (1.0 / 0.07)) + 0.94 * ho
    fast = v * hv * (u - 0.3) * (1.55 - u) * (STEP_TIME / 0.11)
    slow = hw * (w * s) * (STEP_TIME / 1.8875)
    out = (u * nw * tau_so + hw * tau_o) * (STEP_TIME / (tau_o * tau_so))
    du = fast - out + slow
    inv = STEP_TIME / (tau_v * tau_w)
    v2 = v + nv * (no - v) * (tau_w * inv) - hv * v * (STEP_TIME / 1.4506)
    w2 = w + nw * (w_inf - w) * (tau_v * inv) - hw * w * (STEP_TIME / 200.0)
    s2 = s + (0.5 + 0.5 * th_r - s) * (STEP_TIME / tau_s)
    return du, v2, w2, s2


def iota2(shape, dim):
    return lax.broadcasted_iota(jnp.int32, shape, dim)


def first_piola(f, active=None, fdir=None):
    second = {}
    for a in range(3):
        for b in range(a, 3):
            right = f[0][a] * f[0][b] + f[1][a] * f[1][b] + f[2][a] * f[2][b]
            second[a, b] = 0.5 * (right - (1.0 if a == b else 0.0))
    trace = second[0, 0] + second[1, 1] + second[2, 2]
    for a in range(3):
        if active is not None:
            scaled = 0.5 * active * fdir[a]
            for b in range(a, 3):
                second[a, b] = second[a, b] + scaled * fdir[b]
        second[a, a] = second[a, a] + trace
    for a in range(3):
        for b in range(a):
            second[a, b] = second[b, a]
    return [
        f[i][0] * second[0, a] + f[i][1] * second[1, a] + f[i][2] * second[2, a]
        for a in range(3)
        for i in range(3)
    ]


def metric(f, fdir):
    cof = [[None] * 3 for _ in range(3)]
    for i in range(3):
        for j in range(3):
            cof[i][j] = (
                f[(i + 1) % 3][(j + 1) % 3] * f[(i + 2) % 3][(j + 2) % 3]
                - f[(i + 1) % 3][(j + 2) % 3] * f[(i + 2) % 3][(j + 1) % 3]
            )
    det = f[0][0] * cof[0][0] + f[0][1] * cof[0][1] + f[0][2] * cof[0][2]
    scale = 1.0 / det
    inverse = [[cof[i][j] * scale for i in range(3)] for j in range(3)]
    g = [inverse[a][0] * fdir[0] + inverse[a][1] * fdir[1] + inverse[a][2] * fdir[2] for a in range(3)]
    comps = []
    for a, b in PAIRS:
        inner = (
            inverse[a][0] * inverse[b][0]
            + inverse[a][1] * inverse[b][1]
            + inverse[a][2] * inverse[b][2]
        )
        comps.append(SIGMA_TRANS * inner + (SIGMA_LONG - SIGMA_TRANS) * (g[a] * g[b]))
    return comps


class Stencils:
    def __init__(self, rows, width):
        self.rows, self.width = rows, width
        self.lane = iota2((rows, width), 1)
        self.line = iota2((rows, width), 0)

    def left(self, f):
        return jnp.where(self.lane == 0, 0.0, pltpu.roll(f, 1, 1))

    def right(self, f):
        return jnp.where(self.lane == self.width - 1, 0.0, pltpu.roll(f, self.width - 1, 1))

    def south(self, f):
        return jnp.where(self.line == 0, 0.0, pltpu.roll(f, 1, 0))

    def north(self, f):
        return jnp.where(self.line == self.rows - 1, 0.0, pltpu.roll(f, self.rows - 1, 0))

    def sx(self, f):
        return 0.125 * (self.left(f) + self.right(f)) + 0.75 * f

    def dx(self, f):
        return 0.5 * (self.right(f) - self.left(f))

    def sy(self, f):
        return 0.125 * (self.south(f) + self.north(f)) + 0.75 * f

    def dy(self, f):
        return 0.5 * (self.north(f) - self.south(f))

    def deformation(self, field):
        f = []
        for i in range(3):
            low, mid, high = field(i, -1), field(i, 0), field(i, 1)
            zs = 0.125 * (low + high) + 0.75 * mid
            zd = 0.5 * (high - low)
            f.append([self.sy(self.sx(zd)), self.dy(self.sx(zs)), self.sy(self.dx(zs))])
            f[i][i] = f[i][i] + 1.0
        return f

    def force(self, stress, i):
        zd = 0.5 * (stress(i, 1) - stress(i, -1))
        ys = 0.125 * (stress(3 + i, -1) + stress(3 + i, 1)) + 0.75 * stress(3 + i, 0)
        xs = 0.125 * (stress(6 + i, -1) + stress(6 + i, 1)) + 0.75 * stress(6 + i, 0)
        return self.sy(self.sx(zd) + self.dx(xs)) + self.dy(self.sx(ys))


def sine(x, terms=6):
    y = x * x
    c = 1.0
    for n in range(2 * terms, 0, -2):
        c = 1.0 - y * (1.0 / (n * (n + 1))) * c
    return x * c


def cosine(x):
    y = x * x
    c = 1.0
    for n in (13, 11, 9, 7, 5, 3, 1):
        c = 1.0 - y * (1.0 / (n * (n + 1))) * c
    return c


def directions(index):
    theta = -1.0 + index * (2.0 / (NFIB - 1))
    triple = 3.0 * index
    turns = jnp.floor(triple * (0.5 / np.pi) + 0.5)
    triple = (triple - turns * 6.28125) - turns * (2.0 * np.pi - 6.28125)
    tilt = 0.3 * sine(triple, 10)
    flat = cosine(tilt)
    return [sine(tilt), flat * sine(theta), flat * cosine(theta)]


def halves(x):
    high = x.astype(BF16)
    return high, (x - high.astype(F32)).astype(BF16)


def excite_kernel(
    slabs, states, cond_hbm, ten_hbm, fib_hbm, disp_hbm,
    out_hbm, ten_out, act_hbm, shift_hbm, pull_hbm,
    ubuf, out, cond, tension, coeff, dif, act_win, fix_win, fiber, passive, shifted, pull, pooled,
    load_sem, store_sem, sz, rz, sc, rc, sy, ry, sa, ra, sf, rf, sg,
):
    grp = lax.axis_index("grp")
    slab = lax.axis_index("slab")
    col = lax.axis_index("col")
    other = 1 - col
    depth, rows, width = out.shape[1:]
    tiles = rows // TILE
    has_up = slab < slabs - 1
    has_dn = slab > 0
    edge_src = rows - (rows - TILE) * col
    edge_dst = (rows + TILE) * col

    load_u = pltpu.make_async_copy(
        states.at[0], ubuf.at[0, pl.ds(1, depth), pl.ds(TILE, rows), :], load_sem.at[0]
    )
    load_g = pltpu.make_async_copy(
        states.at[pl.ds(1, 3)], out.at[pl.ds(1, 3)], load_sem.at[1]
    )
    load_c = pltpu.make_async_copy(cond_hbm, cond, load_sem.at[2])
    load_t = pltpu.make_async_copy(ten_hbm, tension, load_sem.at[3])
    load_u.start()
    load_c.start()
    load_g.start()
    load_t.start()
    half = rows // 4
    span = half + TILE
    own = pl.ds(pl.multiple_of(TILE * col, TILE), half)
    near = pl.ds(TILE, TILE)
    far = pl.ds(pl.multiple_of(2 * TILE * col, TILE), TILE)
    load_d = pltpu.make_async_copy(
        disp_hbm.at[:, 0], fix_win.at[RADIUS, pl.ds(0, 3), own, :], load_sem.at[4]
    )
    load_f = pltpu.make_async_copy(fib_hbm, fiber, load_sem.at[5])
    load_d.start()
    load_f.start()

    barrier = pltpu.get_barrier_semaphore()

    def greet(where):
        pl.semaphore_signal(barrier, inc=1, device_id=where, device_id_type=MESH)

    def there(d):
        return (slab + d >= 0) & (slab + d < slabs)

    peers = 0
    for d in PEERS:
        valid = there(d)
        wide = abs(d) <= REACH
        count = (0 if d == 0 else 1) + (1 if wide else 0)
        peers = peers + count * valid.astype(jnp.int32)

        @pl.when(valid)
        def _(d=d, wide=wide):
            if wide:
                greet((grp, slab + d, other))
            if d != 0:
                greet((grp, slab + d, col))

    for d in range(-RADIUS, RADIUS + 1):

        @pl.when(jnp.logical_not(there(d)))
        def _(d=d):
            fix_win[d + RADIUS] = jnp.zeros(fix_win.shape[1:], F32)
            if abs(d) <= REACH:
                act_win[d + REACH] = jnp.zeros(act_win.shape[1:], F32)

    blank = jnp.zeros((TILE, width), F32)

    def clear_y(n, c):
        ubuf[n // (depth + 2), n % (depth + 2), pl.ds(pl.multiple_of(edge_dst, TILE), TILE), :] = blank
        return c

    lax.fori_loop(0, SUB * (depth + 2), clear_y, 0)

    def clear_z(layer):
        per = rows // TILE + 2

        def body(n, c):
            ubuf[n // per, layer, pl.ds(pl.multiple_of((n % per) * TILE, TILE), TILE), :] = blank
            return c

        lax.fori_loop(0, SUB * per, body, 0)

    @pl.when(slab == 0)
    def _():
        clear_z(0)

    @pl.when(slab == slabs - 1)
    def _():
        clear_z(depth + 1)

    def row_of(step):
        return jnp.where(col == 1, step, tiles - 1 - step)

    def copy_z(slot, way, step):
        at = pl.ds(pl.multiple_of(TILE + TILE * row_of(step), TILE), TILE)
        src = depth if way == 0 else 1
        dst = 0 if way == 0 else depth + 1
        to = slab + 1 if way == 0 else slab - 1
        return pltpu.make_async_remote_copy(
            src_ref=ubuf.at[slot, src, at, :],
            dst_ref=ubuf.at[slot, dst, at, :],
            send_sem=sz.at[slot, way, step],
            recv_sem=rz.at[slot, way, step],
            device_id=(grp, to, col),
            device_id_type=MESH,
        )

    def copy_c(slot, way):
        at = depth + 1 if way == 0 else 0
        return pltpu.make_async_remote_copy(
            src_ref=ubuf.at[slot, at, pl.ds(pl.multiple_of(edge_src, TILE), TILE), :],
            dst_ref=ubuf.at[slot, at, pl.ds(pl.multiple_of(edge_dst, TILE), TILE), :],
            send_sem=sc.at[slot, way],
            recv_sem=rc.at[slot, way],
            device_id=(grp, slab, other),
            device_id_type=MESH,
        )

    def copy_y(slot):
        return pltpu.make_async_remote_copy(
            src_ref=ubuf.at[slot, pl.ds(1, depth), pl.ds(pl.multiple_of(edge_src, TILE), TILE), :],
            dst_ref=ubuf.at[slot, pl.ds(1, depth), pl.ds(pl.multiple_of(edge_dst, TILE), TILE), :],
            send_sem=sy.at[slot],
            recv_sem=ry.at[slot],
            device_id=(grp, slab, other),
            device_id_type=MESH,
        )

    def both(do_up, do_dn):
        pl.when(has_up)(do_up)
        pl.when(has_dn)(do_dn)

    def send_z(slot, step):
        both(lambda: copy_z(slot, 0, step).start(), lambda: copy_z(slot, 1, step).start())

    def send_c(slot):
        both(lambda: copy_c(slot, 0).start(), lambda: copy_c(slot, 1).start())

    def recv_z(slot, step):
        both(lambda: copy_z(slot, 1, step).wait_recv(), lambda: copy_z(slot, 0, step).wait_recv())

    def recv_c(slot):
        both(lambda: copy_c(slot, 0).wait_recv(), lambda: copy_c(slot, 1).wait_recv())

    beside = 1 - 2 * lax.rem(slab, 2)

    def copy_f(source, d, n):
        slot = RADIUS + source - d
        return pltpu.make_async_remote_copy(
            src_ref=fix_win.at[RADIUS + source, :, own, :],
            dst_ref=fix_win.at[slot, :, own, :],
            send_sem=sf.at[n],
            recv_sem=rf.at[slot],
            device_id=(grp, slab + d, col),
            device_id_type=MESH,
        )

    def come_f(e):
        return pltpu.make_async_remote_copy(
            src_ref=fix_win.at[RADIUS, :, own, :],
            dst_ref=fix_win.at[RADIUS + e, :, own, :],
            send_sem=sf.at[0],
            recv_sem=rf.at[RADIUS + e],
            device_id=(grp, slab + e, col),
            device_id_type=MESH,
        )

    def share_f(whose):
        return pltpu.make_async_remote_copy(
            src_ref=fix_win.at[:, :, near, :],
            dst_ref=fix_win.at[:, :, pl.ds(pl.multiple_of(2 * TILE * whose, TILE), TILE), :],
            send_sem=sg.at[0],
            recv_sem=sg.at[1],
            device_id=(grp, slab, other),
            device_id_type=MESH,
        )

    def forward_f(act):
        for n, d in enumerate(BEYOND):
            ok = there(d) & (jnp.abs(d - beside) <= RADIUS)
            pl.when(ok)(lambda n=n, d=d: act(n, d))

    def relay_f(n, d):
        return copy_f(beside, d, 1 + len(ALONG) + n)

    pl.semaphore_wait(barrier, peers)

    load_u.wait()
    send_z(0, 0)
    copy_y(0).start()
    send_z(0, 1)
    load_d.wait()
    load_f.wait()
    fix_win[RADIUS, 3, own, :] = fiber[0].astype(F32)
    copy_f(0, beside, 0).start()
    for n, d in enumerate(ALONG):
        pl.when(there(d))(lambda n=n, d=d: copy_f(0, d, 1 + n).start())

    def initial(step, c):
        send_z(0, step)
        return c

    lax.fori_loop(2, tiles, initial, 0)
    load_c.wait()

    spread_x = (iota2((256, 512), 0) % 128 == iota2((256, 512), 1) // 4).astype(BF16)
    spread_y = (iota2((rows, rows // 4), 0) // 4 == iota2((rows, rows // 4), 1)).astype(BF16)
    for c in range(6):
        tall = [
            jnp.dot(spread_y, part, preferred_element_type=F32).astype(BF16)
            for part in halves(cond[c, 0])
        ]
        for h in range(width // 512):
            part = jnp.concatenate([t[:, h * 128 : (h + 1) * 128] for t in tall], axis=1)
            part = jnp.dot(part, spread_x, preferred_element_type=F32)
            coeff[c, :, h * 512 : (h + 1) * 512] = part if c < 3 else 0.5 * part

    load_g.wait()
    load_t.wait()

    lane = iota2((TILE, width), 1)

    def left(f):
        return jnp.where(lane == 0, 0.0, pltpu.roll(f, 1, 1))

    def right(f):
        return jnp.where(lane == width - 1, 0.0, pltpu.roll(f, width - 1, 1))

    def layer(k, z, r):
        base = pl.multiple_of(TILE * r, TILE)
        here = pl.ds(base, TILE)
        tall = pl.ds(base, 3 * TILE)
        below = ubuf[k, z, tall, :]
        mid = ubuf[k, z + 1, tall, :]
        above = ubuf[k, z + 2, tall, :]
        odd = above - below
        centre = mid[TILE : 2 * TILE]
        odd0 = odd[TILE : 2 * TILE]
        north = mid[TILE + 1 : 2 * TILE + 1]
        south = mid[TILE - 1 : 2 * TILE - 1]
        slope = north - south
        twice = 2.0 * centre
        total = coeff[0, here, :] * (
            above[TILE : 2 * TILE] + below[TILE : 2 * TILE] - twice
        )
        total = total + coeff[1, here, :] * (north + south - twice)
        total = total + coeff[2, here, :] * (right(centre) + left(centre) - twice)
        total = total + coeff[3, here, :] * (
            odd[TILE + 1 : 2 * TILE + 1] - odd[TILE - 1 : 2 * TILE - 1]
        )
        total = total + coeff[4, here, :] * (right(odd0) - left(odd0))
        total = total + coeff[5, here, :] * (right(slope) - left(slope))
        dif[...] = total + centre
        up = pl.ds(pl.multiple_of(base + TILE, TILE), TILE)
        for x in range(0, width, CHUNK):
            xs = pl.ds(x, CHUNK)
            du, v2, w2, s2 = ionic(
                ubuf[k, z + 1, up, xs], out[1, z, here, xs], out[2, z, here, xs],
                out[3, z, here, xs],
            )
            u2 = dif[:, xs] + du
            ubuf[k + 1, z + 1, up, xs] = u2
            out[0, z, here, xs] = u2
            out[1, z, here, xs] = v2
            out[2, z, here, xs] = w2
            out[3, z, here, xs] = s2

    def leave(step):
        at = pl.ds(pl.multiple_of(TILE * row_of(step), TILE), TILE)
        return pltpu.make_async_copy(
            out.at[:, :, at, :], out_hbm.at[:, :, at, :], store_sem.at[step]
        )

    pair_x = (iota2((256, 128), 0) // 2 == iota2((256, 128), 1)).astype(F32)
    pair_2 = (iota2((512, 128), 0) % 256 // 2 == iota2((512, 128), 1)).astype(BF16)
    pair_y2 = (iota2((half, 2 * half), 0) == iota2((half, 2 * half), 1) // 2).astype(F32)

    def pool_lanes(rows_in, weights, size, chunk):
        parts = halves(rows_in)
        for h in range(width // chunk):
            both_halves = jnp.concatenate(
                [part[:, h * chunk : (h + 1) * chunk] for part in parts], axis=1
            )
            pooled[h, 0:size] = jnp.dot(both_halves, weights, preferred_element_type=F32)

    def tense(p):
        fine = pl.ds(pl.multiple_of(2 * TILE * p, 2 * TILE), 2 * TILE)
        wide = pl.ds(pl.multiple_of(TILE * p, TILE), TILE)
        sums = []
        for q in range(depth // 2):
            layers = out[0, 2 * q, fine, :] + out[0, 2 * q + 1, fine, :]
            sums.append(layers + pltpu.roll(layers, 2 * TILE - 1, 0))
        pool_lanes(0.125 * jnp.concatenate(sums, axis=0), pair_2, TILE * depth, 256)
        for h in range(width // 256):
            xo = slice(h * 128, (h + 1) * 128)
            for q in range(depth // 2):
                mean = pooled[h, pl.ds(2 * TILE * q, TILE, 2), :]
                before = tension[q, wide, xo]
                ten_out[q, wide, xo] = before + 0.5 * (mean - before)

    pool_x = (iota2((1024, 128), 0) % 512 // 4 == iota2((1024, 128), 1)).astype(BF16)

    def activate(part, lines):
        fine = pl.ds(pl.multiple_of(4 * TILE * part, 4 * TILE), 4 * TILE)
        layers = out[0, 0, fine, :]
        for z in range(1, depth):
            layers = layers + out[0, z, fine, :]
        layers = layers + pltpu.roll(layers, 4 * TILE - 1, 0)
        layers = layers + pltpu.roll(layers, 4 * TILE - 2, 0)
        pool_lanes((0.5 / (16 * depth)) * layers, pool_x, 4 * TILE, 512)
        for h in range(width // 512):
            xo = slice(h * 128, (h + 1) * 128)
            act_win[REACH, lines, xo] = act_win[REACH, lines, xo] + pooled[h, pl.ds(0, TILE, 4), :]

    def copy_a(d, to, kind, lines, at):
        return pltpu.make_async_remote_copy(
            src_ref=act_win.at[REACH, lines, :],
            dst_ref=act_win.at[REACH - d, at, :],
            send_sem=sa.at[d + REACH, kind],
            recv_sem=ra.at[REACH - d, kind],
            device_id=(grp, slab + d, to),
            device_id_type=MESH,
        )

    def each_a(act, centre):
        for d in sorted(range(-REACH, REACH + 1), key=lambda d: -abs(d)):
            if d != 0 or centre:
                pl.when(there(d))(lambda d=d: act(d))

    mech = Stencils(span, fix_win.shape[3])

    def inside(j):
        return there(j - RADIUS)

    def prepare(j):
        ok = inside(j)
        f = mech.deformation(lambda i, d: fix_win[j + d, i])
        fdir = directions(fix_win[j, 3])
        pieces = first_piola(f)
        for n in range(9):
            passive[n, j - 1] = jnp.where(ok, pieces[n], 0.0)
        for i in range(3):
            g = 0.5 * (f[i][0] * fdir[0] + f[i][1] * fdir[1] + f[i][2] * fdir[2])
            pull[i, j - 1] = jnp.where(ok, g, 0.0)
            pull[3 + i, j - 1] = fdir[i]

        @pl.when(j >= 3)
        def _():
            here = inside(j - 1)
            for i in range(3):
                force = mech.force(lambda n, d: passive[n, j - 2 + d], i)
                moved = fix_win[j - 1, i] + MECH_RATE * force
                shifted[i, j - 3] = jnp.where(here, moved, 0.0)

    hand_shift = pltpu.make_async_copy(shifted, shift_hbm, load_sem.at[0])
    hand_pull = pltpu.make_async_copy(pull, pull_hbm, load_sem.at[1])

    for h in range(width // 512):
        xs = slice(h * 256, (h + 1) * 256)
        layers = tension[0, :, xs] + tension[1, :, xs]
        mean = jnp.dot(layers, pair_x, precision=HI, preferred_element_type=F32)
        mean = 0.0625 * jnp.dot(pair_y2, mean, precision=HI, preferred_element_type=F32)
        act_win[REACH, own, h * 128 : (h + 1) * 128] = mean

    def within(n):
        k = n // tiles
        r = row_of(n % tiles)

        def inner(m, c):
            layer(k, m, r)
            return c

        lax.fori_loop(1, depth - 1, inner, 0)

    recv_z(0, 0)
    send_c(0)
    copy_y(0).wait_recv()
    within(0)

    def chunk(n, c):
        k = n // tiles
        step = n % tiles
        r = row_of(step)

        @pl.when(n == tiles // 2)
        def _():
            come_f(beside).wait_recv()
            forward_f(lambda n, d: relay_f(n, d).start())

        @pl.when(n == JOIN)
        def _():
            for d in range(-RADIUS, RADIUS + 1):
                if d != 0:
                    arrives = there(d) if d % 2 == 0 else there(d) & (beside != d)
                    pl.when(arrives)(lambda d=d: come_f(d).wait_recv())
            share_f(col).start()

        @pl.when(n == JOIN + 2)
        def _():
            share_f(col).wait_recv()

        @pl.when(step < tiles - 1)
        def _():
            recv_z(k, step + 1)

        @pl.when(step == 0)
        def _():
            recv_c(k)

        def outer(m, c):
            layer(k, m * (depth - 1), r)
            return c

        lax.fori_loop(0, 2, outer, 0)

        @pl.when(k < SUB - 1)
        def _():
            send_z(k + 1, step)

        @pl.when((k < SUB - 1) & (step == 0))
        def _():
            copy_y(k + 1).start()

        @pl.when((k < SUB - 1) & (step == tiles - 1))
        def _():
            recv_z(k + 1, 0)
            send_c(k + 1)
            copy_y(k + 1).wait_recv()

        @pl.when(n < SUB * tiles - 1)
        def _():
            within(n + 1)

        @pl.when((n >= JOIN + 2) & (n < JOIN + 3 + 2 * REACH))
        def _():
            prepare(n - JOIN - 1)

        @pl.when(n == JOIN + 3 + 2 * REACH)
        def _():
            hand_shift.start()
            hand_pull.start()

        @pl.when(k == SUB - 1)
        def _():
            leave(step).start()

        @pl.when(n == SUB * tiles - 1 - tiles // 2)
        def _():
            activate(other, near)
            each_a(lambda d: copy_a(d, col, 0, near, near).start(), False)
            each_a(lambda d: copy_a(d, other, 1, near, far).start(), True)

        @pl.when((k == SUB - 1) & (step % 2 == 1) & (step < tiles - 1))
        def _():
            tense(r // 2)

        return c

    lax.fori_loop(0, SUB * tiles, chunk, 0)

    activate(col, far)
    each_a(lambda d: copy_a(d, col, 2, far, far).start(), False)
    tense(row_of(tiles - 1) // 2)
    share_f(col).wait_send()
    copy_f(0, beside, 0).wait_send()
    for n, d in enumerate(ALONG):
        pl.when(there(d))(lambda n=n, d=d: copy_f(0, d, 1 + n).wait_send())
    forward_f(lambda n, d: relay_f(n, d).wait_send())
    hand_shift.wait()
    hand_pull.wait()
    copy_y(0).wait_send()

    def drain(slot, c):
        both(lambda: copy_c(slot, 0).wait_send(), lambda: copy_c(slot, 1).wait_send())

        @pl.when(slot > 0)
        def _():
            copy_y(slot).wait_send()

        def tile(step, c):
            both(
                lambda: copy_z(slot, 0, step).wait_send(),
                lambda: copy_z(slot, 1, step).wait_send(),
            )
            return c

        return lax.fori_loop(0, tiles, tile, c)

    lax.fori_loop(0, SUB, drain, 0)

    def left_all(step, c):
        leave(step).wait()
        return c

    lax.fori_loop(0, tiles, left_all, 0)
    each_a(lambda d: copy_a(d, col, 0, near, near).wait_send(), False)
    each_a(lambda d: copy_a(d, other, 1, near, far).wait_send(), True)
    each_a(lambda d: copy_a(d, col, 2, far, far).wait_send(), False)
    each_a(lambda d: copy_a(-d, col, 0, near, near).wait_recv(), False)
    each_a(lambda d: copy_a(-d, other, 1, near, far).wait_recv(), True)
    each_a(lambda d: copy_a(-d, col, 2, far, far).wait_recv(), False)
    hand_act = pltpu.make_async_copy(act_win, act_hbm, load_sem.at[0])
    hand_act.start()
    hand_act.wait()


def excite(slabs, states, cond, tension, fiber, disp):
    _, depth, rows, width = states.shape
    tiles = rows // TILE
    full = rows // 4 + TILE
    across = cond.shape[3]
    vmem = pl.BlockSpec(memory_space=pltpu.VMEM)
    hbm = pl.BlockSpec(memory_space=pltpu.HBM)
    window = (2 * REACH + 1, full, across)
    shifts = (3, 2 * REACH - 1, full, across)
    pulls = (6, 2 * REACH + 1, full, across)
    dma = pltpu.SemaphoreType.DMA
    return pl.pallas_call(
        functools.partial(excite_kernel, slabs),
        out_shape=(
            jax.ShapeDtypeStruct(states.shape, F32),
            jax.ShapeDtypeStruct(tension.shape, F32),
            jax.ShapeDtypeStruct(window, F32),
            jax.ShapeDtypeStruct(shifts, F32),
            jax.ShapeDtypeStruct(pulls, F32),
        ),
        in_specs=[hbm, hbm, hbm, hbm, hbm],
        out_specs=(hbm, vmem, hbm, hbm, hbm),
        scratch_shapes=[
            pltpu.VMEM((SUB + 1, depth + 2, rows + 2 * TILE, width), F32),
            pltpu.VMEM(states.shape, F32),
            pltpu.VMEM(cond.shape, F32),
            pltpu.VMEM(tension.shape, F32),
            pltpu.VMEM((6, rows, width), F32),
            pltpu.VMEM((TILE, width), F32),
            pltpu.VMEM(window, F32),
            pltpu.VMEM((2 * RADIUS + 1, 4, full, across), F32),
            pltpu.VMEM(fiber.shape, jnp.int32),
            pltpu.VMEM((9, *window), F32),
            pltpu.VMEM(shifts, F32),
            pltpu.VMEM(pulls, F32),
            pltpu.VMEM((width // 256, 4 * TILE, 128), F32),
            dma((6,)),
            dma((tiles,)),
            dma((SUB, 2, tiles)),
            dma((SUB, 2, tiles)),
            dma((SUB, 2)),
            dma((SUB, 2)),
            dma((SUB,)),
            dma((SUB,)),
            dma((2 * REACH + 1, 3)),
            dma((2 * REACH + 1, 3)),
            dma((1 + len(ALONG) + len(BEYOND),)),
            dma((2 * RADIUS + 1,)),
            dma((2,)),
        ],
        compiler_params=pltpu.CompilerParams(
            collective_id=0, has_side_effects=True, vmem_limit_bytes=61 << 20
        ),
        cost_estimate=pl.CostEstimate(
            flops=200_000_000, bytes_accessed=16 << 20, transcendentals=6_000_000
        ),
        name="excite",
    )(states, cond, tension, fiber, disp)


def mech_kernel(
    slabs, active, shifted, pull, ten_in, states_in,
    disp_out, cond_out, ten_out, states_out, stress, moved, held, sem,
):
    slab = lax.axis_index("slab")
    first = lax.axis_index("col") == 0
    rows, width = active.shape[1:]
    half = rows - TILE
    fetch = pltpu.make_async_copy(states_in, held, sem.at[0])
    hand_on = pltpu.make_async_copy(held, states_out, sem.at[1])
    fetch.start()
    ten_out[...] = ten_in[...]
    mech = Stencils(rows, width)

    def inside(j):
        zz = slab + j - REACH
        return (zz >= 0) & (zz < slabs)

    def tense(j, c):
        for a in range(3):
            t = active[j] * pull[3 + a, j]
            for i in range(3):
                stress[3 * a + i, j] = t * pull[i, j]
        return c

    def move(field):
        def body(j, c):
            ok = inside(j)
            for i in range(3):
                force = mech.force(lambda n, d: stress[n, j + d], i)
                moved[i, j] = jnp.where(ok, field(i, j) + MECH_RATE * force, 0.0)
            return c

        return body

    def strain(j, c):
        ok = inside(j)
        f = mech.deformation(lambda i, d: moved[i, j + d])
        pieces = first_piola(f, active[j], [pull[3 + a, j] for a in range(3)])
        for n in range(9):
            stress[n, j] = jnp.where(ok, pieces[n], 0.0)
        return c

    lax.fori_loop(0, 2 * REACH + 1, tense, 0)
    lax.fori_loop(1, 2 * REACH, move(lambda i, j: shifted[i, j - 1]), 0)
    fetch.wait()
    hand_on.start()
    lax.fori_loop(2, 2 * REACH - 1, strain, 0)
    lax.fori_loop(3, 2 * REACH - 2, move(lambda i, j: moved[i, j]), 0)

    comps = metric(
        mech.deformation(lambda i, d: moved[i, REACH + d]),
        [pull[3 + a, REACH] for a in range(3)],
    )
    for i in range(3):
        whole = moved[i, REACH]
        disp_out[i, 0] = jnp.where(first, whole[:half], whole[TILE:])
    for n in range(6):
        cond_out[n, 0] = jnp.where(first, comps[n][:half], comps[n][TILE:])
    hand_on.wait()


def mechanics(slabs, active, shifted, pull, tension, states):
    _, full, width = active.shape
    rows = full - TILE
    vmem = pl.BlockSpec(memory_space=pltpu.VMEM)
    hbm = pl.BlockSpec(memory_space=pltpu.HBM)
    return pl.pallas_call(
        functools.partial(mech_kernel, slabs),
        out_shape=(
            jax.ShapeDtypeStruct((3, 1, rows, width), F32),
            jax.ShapeDtypeStruct((6, 1, rows, width), F32),
            jax.ShapeDtypeStruct(tension.shape, F32),
            jax.ShapeDtypeStruct(states.shape, F32),
        ),
        in_specs=[vmem, vmem, vmem, vmem, hbm],
        out_specs=(vmem, vmem, vmem, hbm),
        scratch_shapes=[
            pltpu.VMEM((9, 2 * REACH + 1, full, width), F32),
            pltpu.VMEM((3, 2 * REACH + 1, full, width), F32),
            pltpu.VMEM(states.shape, F32),
            pltpu.SemaphoreType.DMA((2,)),
        ],
        compiler_params=pltpu.CompilerParams(vmem_limit_bytes=61 << 20),
        name="mechanics",
    )(active, shifted, pull, tension, states)


def on_device(slabs, states, cond, tension, fiber, disp):
    states_next, tension_next, active, shifted, pull = excite(
        slabs, states, cond, tension, fiber, disp
    )
    disp_next, cond_next, tension_next, states_next = mechanics(
        slabs, active, shifted, pull, tension_next, states_next
    )
    return states_next, tension_next, disp_next, cond_next


def solution(mesh):
    wide = P(None, ("grp", "slab"), "col", None)
    flat = P(("grp", "slab"), "col", None)
    return jax.shard_map(
        functools.partial(on_device, mesh.shape["slab"]),
        mesh=mesh,
        in_specs=(wide, wide, flat, flat, wide),
        out_specs=(wide, flat, wide, wide),
        check_vma=False,
    )
```

```python
import functools

import jax
import jax.numpy as jnp
import numpy as np
from jax import lax
from jax.experimental import pallas as pl
from jax.experimental.pallas import tpu as pltpu
from jax.sharding import PartitionSpec as P

SUB = 4
MECH_STEPS = 2
NFIB = 64
STEP_TIME = 0.05
MECH_RATE = 0.15
SIGMA_LONG = 0.16
SIGMA_TRANS = 0.04
PAIRS = ((0, 0), (1, 1), (2, 2), (0, 1), (0, 2), (1, 2))
MESH = pl.DeviceIdType.MESH
HI = lax.Precision.HIGHEST
F32 = jnp.float32
BF16 = jnp.bfloat16
TILE = 8
CHUNK = 256
RADIUS = 2 * MECH_STEPS + 1
REACH = RADIUS - 1
ALONG = (-4, -2, 2, 4)
BEYOND = (-6, -4, -2, 2, 4, 6)
PEERS = (-6, -4, -3, -2, -1, 0, 1, 2, 3, 4, 6)
JOIN = 10
LAST = 4 * REACH
LAG = 4


def ionic(u, v, w, s):
    per = 2.0 / STEP_TIME
    steep = 50.0 * u
    th_v = jnp.tanh(steep - 50.0 * 0.3)
    th_w = jnp.tanh(steep - 50.0 * 0.13)
    th_o = jnp.tanh(steep - 50.0 * 0.006)
    th_m = jnp.tanh(65.0 * u - 65.0 * 0.03)
    th_s = jnp.tanh(2.0458 * u - 2.0458 * 0.65)
    th_r = jnp.tanh(2.0994 * u - 2.0994 * 0.9087)
    hv2 = 1.0 + th_v
    nv2 = 1.0 - th_v
    hw2 = 1.0 + th_w
    nw2 = 1.0 - th_w
    no = 0.5 - 0.5 * th_o
    rate_v = 1.0 / (605.0 * per + (545.0 * per) * th_o)
    rate_w = 1.0 / (37.5 * per - (22.5 * per) * th_m)
    rate_so = 1.0 / (15.5069 * per - (14.5112 * per) * th_s)
    rate_s = 1.0 / (9.3671 * per + (6.6329 * per) * th_w)
    rate_o = 1.0 / (203.0 * per - (197.0 * per) * th_o)
    lead = STEP_TIME / 0.22
    open_v = hv2 * v
    w_inf = no * (0.06 - u * (1.0 / 0.07)) + 0.94
    du = (
        open_v * ((u - 0.3) * (1.55 * lead - lead * u))
        + hw2 * ((w * s) * (STEP_TIME / 3.775) - rate_so)
        - (u * nw2) * rate_o
    )
    v2 = v - open_v * (STEP_TIME / 2.9012) + (nv2 * rate_v) * (no - v)
    w2 = w - (hw2 * w) * (STEP_TIME / 400.0) + (nw2 * rate_w) * (w_inf - w)
    s2 = s + ((1.0 + th_r) - 2.0 * s) * rate_s
    return du, v2, w2, s2


def iota2(shape, dim):
    return lax.broadcasted_iota(jnp.int32, shape, dim)


def first_piola(f, active=None, fdir=None):
    second = {}
    for a in range(3):
        for b in range(a, 3):
            right = f[0][a] * f[0][b] + f[1][a] * f[1][b] + f[2][a] * f[2][b]
            second[a, b] = 0.5 * (right - (1.0 if a == b else 0.0))
    trace = second[0, 0] + second[1, 1] + second[2, 2]
    for a in range(3):
        if active is not None:
            scaled = 0.5 * active * fdir[a]
            for b in range(a, 3):
                second[a, b] = second[a, b] + scaled * fdir[b]
        second[a, a] = second[a, a] + trace
    for a in range(3):
        for b in range(a):
            second[a, b] = second[b, a]
    return [
        f[i][0] * second[0, a] + f[i][1] * second[1, a] + f[i][2] * second[2, a]
        for a in range(3)
        for i in range(3)
    ]


def metric(f, fdir):
    cof = [[None] * 3 for _ in range(3)]
    for i in range(3):
        for j in range(3):
            cof[i][j] = (
                f[(i + 1) % 3][(j + 1) % 3] * f[(i + 2) % 3][(j + 2) % 3]
                - f[(i + 1) % 3][(j + 2) % 3] * f[(i + 2) % 3][(j + 1) % 3]
            )
    det = f[0][0] * cof[0][0] + f[0][1] * cof[0][1] + f[0][2] * cof[0][2]
    scale = 1.0 / det
    inverse = [[cof[i][j] * scale for i in range(3)] for j in range(3)]
    g = [inverse[a][0] * fdir[0] + inverse[a][1] * fdir[1] + inverse[a][2] * fdir[2] for a in range(3)]
    comps = []
    for a, b in PAIRS:
        inner = (
            inverse[a][0] * inverse[b][0]
            + inverse[a][1] * inverse[b][1]
            + inverse[a][2] * inverse[b][2]
        )
        comps.append(SIGMA_TRANS * inner + (SIGMA_LONG - SIGMA_TRANS) * (g[a] * g[b]))
    return comps


class Stencils:
    def __init__(self, rows, width):
        self.rows, self.width = rows, width
        self.lane = iota2((rows, width), 1)
        self.line = iota2((rows, width), 0)

    def left(self, f):
        return jnp.where(self.lane == 0, 0.0, pltpu.roll(f, 1, 1))

    def right(self, f):
        return jnp.where(self.lane == self.width - 1, 0.0, pltpu.roll(f, self.width - 1, 1))

    def south(self, f):
        return jnp.where(self.line == 0, 0.0, pltpu.roll(f, 1, 0))

    def north(self, f):
        return jnp.where(self.line == self.rows - 1, 0.0, pltpu.roll(f, self.rows - 1, 0))


    def sx(self, f):
        return self.left(f) + self.right(f) + 6.0 * f

    def dx(self, f):
        return self.right(f) - self.left(f)

    def sy(self, f):
        return self.south(f) + self.north(f) + 6.0 * f

    def dy(self, f):
        return self.north(f) - self.south(f)

    def deformation(self, field):
        f = []
        for i in range(3):
            low, mid, high = field(i, -1), field(i, 0), field(i, 1)
            zs = low + high + 6.0 * mid
            zd = high - low
            grads = [self.sy(self.sx(zd)), self.dy(self.sx(zs)), self.sy(self.dx(zs))]
            f.append([(1.0 / 128.0) * g for g in grads])
            f[i][i] = f[i][i] + 1.0
        return f

    def force(self, stress, i):
        zd = stress(i, 1) - stress(i, -1)
        ys = stress(3 + i, -1) + stress(3 + i, 1) + 6.0 * stress(3 + i, 0)
        xs = stress(6 + i, -1) + stress(6 + i, 1) + 6.0 * stress(6 + i, 0)
        return self.sy(self.sx(zd) + self.dx(xs)) + self.dy(self.sx(ys))


def sine(x, terms=6):
    y = x * x
    c = 1.0
    for n in range(2 * terms, 0, -2):
        c = 1.0 - y * (1.0 / (n * (n + 1))) * c
    return x * c


def cosine(x):
    y = x * x
    c = 1.0
    for n in (13, 11, 9, 7, 5, 3, 1):
        c = 1.0 - y * (1.0 / (n * (n + 1))) * c
    return c


def directions(index):
    theta = -1.0 + index * (2.0 / (NFIB - 1))
    triple = 3.0 * index
    turns = jnp.floor(triple * (0.5 / np.pi) + 0.5)
    triple = (triple - turns * 6.28125) - turns * (2.0 * np.pi - 6.28125)
    tilt = 0.3 * sine(triple, 10)
    flat = cosine(tilt)
    return [sine(tilt), flat * sine(theta), flat * cosine(theta)]


def halves(x):
    high = x.astype(BF16)
    return high, (x - high.astype(F32)).astype(BF16)


def excite_kernel(
    slabs, states, cond_hbm, ten_hbm, fib_hbm, disp_hbm,
    out_hbm, ten_out, act_hbm, shift_hbm, pull_hbm,
    ubuf, out, cond, tension, coeff, dif, act_win, fix_win, fiber, passive, shifted, pull, pooled,
    load_sem, store_sem, sz, rz, sc, rc, sy, ry, sa, ra, sf, rf, sg, relay, sv, rv,
):
    grp = lax.axis_index("grp")
    slab = lax.axis_index("slab")
    col = lax.axis_index("col")
    other = 1 - col
    depth, rows, width = out.shape[1:]
    tiles = rows // TILE
    has_up = slab < slabs - 1
    has_dn = slab > 0
    edge_src = rows - (rows - TILE) * col
    edge_dst = (rows + TILE) * col

    load_u = pltpu.make_async_copy(
        states.at[0], ubuf.at[0, pl.ds(1, depth), pl.ds(TILE, rows), :], load_sem.at[0]
    )
    load_g = pltpu.make_async_copy(
        states.at[pl.ds(1, 3)], out.at[pl.ds(1, 3)], load_sem.at[1]
    )
    load_c = pltpu.make_async_copy(cond_hbm, cond, load_sem.at[2])
    load_t = pltpu.make_async_copy(ten_hbm, tension, load_sem.at[3])
    load_u.start()
    load_c.start()
    load_g.start()
    load_t.start()
    half = rows // 4
    span = half + TILE
    own = pl.ds(pl.multiple_of(TILE * col, TILE), half)
    near = pl.ds(TILE, TILE)
    far = pl.ds(pl.multiple_of(2 * TILE * col, TILE), TILE)
    load_d = pltpu.make_async_copy(
        disp_hbm.at[:, 0], fix_win.at[RADIUS, pl.ds(0, 3), own, :], load_sem.at[4]
    )
    load_f = pltpu.make_async_copy(fib_hbm, fiber, load_sem.at[5])
    load_d.start()
    load_f.start()

    barrier = pltpu.get_barrier_semaphore()

    def greet(where):
        pl.semaphore_signal(barrier, inc=1, device_id=where, device_id_type=MESH)

    def there(d):
        return (slab + d >= 0) & (slab + d < slabs)

    peers = 0
    for d in PEERS:
        valid = there(d)
        wide = abs(d) <= REACH
        count = (0 if d == 0 else 1) + (1 if wide else 0)
        peers = peers + count * valid.astype(jnp.int32)

        @pl.when(valid)
        def _(d=d, wide=wide):
            if wide:
                greet((grp, slab + d, other))
            if d != 0:
                greet((grp, slab + d, col))

    for d in range(-RADIUS, RADIUS + 1):

        @pl.when(jnp.logical_not(there(d)))
        def _(d=d):
            fix_win[d + RADIUS] = jnp.zeros(fix_win.shape[1:], F32)
            if abs(d) <= REACH:
                act_win[d + REACH] = jnp.zeros(act_win.shape[1:], F32)

    blank = jnp.zeros((TILE, width), F32)

    def clear_y(n, c):
        ubuf[n // (depth + 2), n % (depth + 2), pl.ds(pl.multiple_of(edge_dst, TILE), TILE), :] = blank
        return c

    lax.fori_loop(0, SUB * (depth + 2), clear_y, 0)

    def clear_z(layer):
        per = rows // TILE + 2

        def body(n, c):
            ubuf[n // per, layer, pl.ds(pl.multiple_of((n % per) * TILE, TILE), TILE), :] = blank
            return c

        lax.fori_loop(0, SUB * per, body, 0)

    @pl.when(slab == 0)
    def _():
        clear_z(0)

    @pl.when(slab == slabs - 1)
    def _():
        clear_z(depth + 1)

    def row_of(step):
        return jnp.where(col == 1, step, tiles - 1 - step)

    def copy_z(slot, way, step):
        at = pl.ds(pl.multiple_of(TILE + TILE * row_of(step), TILE), TILE)
        src = depth if way == 0 else 1
        dst = 0 if way == 0 else depth + 1
        to = slab + 1 if way == 0 else slab - 1
        return pltpu.make_async_remote_copy(
            src_ref=ubuf.at[slot, src, at, :],
            dst_ref=ubuf.at[slot, dst, at, :],
            send_sem=sz.at[slot, way, step],
            recv_sem=rz.at[slot, way, step],
            device_id=(grp, to, col),
            device_id_type=MESH,
        )

    def carried(step, count):
        return lax.rem((step + 1) * count, tiles) < count

    beside = 1 - 2 * lax.rem(slab, 2)
    chips = slabs // 2
    upper = tiles * (chips - 1 - slab // 2) // chips
    lower = tiles * (slab // 2) // chips
    even = beside == 1
    mine = jnp.where(even, lower, upper)
    others = jnp.where(even, upper, lower)
    onward = 1 - lax.rem(slab + 1, 2)

    def copy_via(slot, way, step):
        at = pl.ds(pl.multiple_of(TILE + TILE * row_of(step), TILE), TILE)
        to = pl.ds(pl.multiple_of(TILE * row_of(step), TILE), TILE)
        return pltpu.make_async_remote_copy(
            src_ref=ubuf.at[slot, depth if way == 0 else 1, at, :],
            dst_ref=relay.at[slot, to, :],
            send_sem=sz.at[slot, way, step],
            recv_sem=rv.at[slot, step],
            device_id=(grp, slab + beside, col),
            device_id_type=MESH,
        )

    def copy_on(slot, step):
        at = pl.ds(pl.multiple_of(TILE * row_of(step), TILE), TILE)
        to = pl.ds(pl.multiple_of(TILE + TILE * row_of(step), TILE), TILE)
        return pltpu.make_async_remote_copy(
            src_ref=relay.at[slot, at, :],
            dst_ref=ubuf.at[slot, onward * (depth + 1), to, :],
            send_sem=sv.at[slot, step],
            recv_sem=rz.at[slot, onward, step],
            device_id=(grp, slab + 2 * beside, col),
            device_id_type=MESH,
        )

    def hand_on(n):
        @pl.when((n < SUB * tiles) & carried(n % tiles, others))
        def _():
            copy_via(n // tiles, 0, n % tiles).wait_recv()
            copy_on(n // tiles, n % tiles).start()

    def copy_c(slot, way):
        at = depth + 1 if way == 0 else 0
        return pltpu.make_async_remote_copy(
            src_ref=ubuf.at[slot, at, pl.ds(pl.multiple_of(edge_src, TILE), TILE), :],
            dst_ref=ubuf.at[slot, at, pl.ds(pl.multiple_of(edge_dst, TILE), TILE), :],
            send_sem=sc.at[slot, way],
            recv_sem=rc.at[slot, way],
            device_id=(grp, slab, other),
            device_id_type=MESH,
        )

    def copy_y(slot):
        return pltpu.make_async_remote_copy(
            src_ref=ubuf.at[slot, pl.ds(1, depth), pl.ds(pl.multiple_of(edge_src, TILE), TILE), :],
            dst_ref=ubuf.at[slot, pl.ds(1, depth), pl.ds(pl.multiple_of(edge_dst, TILE), TILE), :],
            send_sem=sy.at[slot],
            recv_sem=ry.at[slot],
            device_id=(grp, slab, other),
            device_id_type=MESH,
        )

    def both(do_up, do_dn):
        pl.when(has_up)(do_up)
        pl.when(has_dn)(do_dn)

    def send_z(slot, step):
        via = carried(step, mine)

        def send(way):
            far_row = jnp.logical_not(even) if way == 0 else even
            pl.when(far_row & via)(lambda: copy_via(slot, way, step).start())
            pl.when(jnp.logical_not(far_row & via))(lambda: copy_z(slot, way, step).start())

        both(lambda: send(0), lambda: send(1))

    def send_c(slot):
        both(lambda: copy_c(slot, 0).start(), lambda: copy_c(slot, 1).start())

    def recv_z(slot, step):
        both(lambda: copy_z(slot, 1, step).wait_recv(), lambda: copy_z(slot, 0, step).wait_recv())

    def recv_c(slot):
        both(lambda: copy_c(slot, 0).wait_recv(), lambda: copy_c(slot, 1).wait_recv())

    def copy_f(source, d, n):
        slot = RADIUS + source - d
        return pltpu.make_async_remote_copy(
            src_ref=fix_win.at[RADIUS + source, :, own, :],
            dst_ref=fix_win.at[slot, :, own, :],
            send_sem=sf.at[n],
            recv_sem=rf.at[slot],
            device_id=(grp, slab + d, col),
            device_id_type=MESH,
        )

    def come_f(e):
        return pltpu.make_async_remote_copy(
            src_ref=fix_win.at[RADIUS, :, own, :],
            dst_ref=fix_win.at[RADIUS + e, :, own, :],
            send_sem=sf.at[0],
            recv_sem=rf.at[RADIUS + e],
            device_id=(grp, slab + e, col),
            device_id_type=MESH,
        )

    def share_f(whose):
        return pltpu.make_async_remote_copy(
            src_ref=fix_win.at[:, :, near, :],
            dst_ref=fix_win.at[:, :, pl.ds(pl.multiple_of(2 * TILE * whose, TILE), TILE), :],
            send_sem=sg.at[0],
            recv_sem=sg.at[1],
            device_id=(grp, slab, other),
            device_id_type=MESH,
        )

    def forward_f(act):
        for n, d in enumerate(BEYOND):
            ok = there(d) & (jnp.abs(d - beside) <= RADIUS)
            pl.when(ok)(lambda n=n, d=d: act(n, d))

    def relay_f(n, d):
        return copy_f(beside, d, 1 + len(ALONG) + n)

    pl.semaphore_wait(barrier, peers)

    load_u.wait()
    send_z(0, 0)
    copy_y(0).start()
    send_z(0, 1)
    load_d.wait()
    load_f.wait()
    fix_win[RADIUS, 3, own, :] = fiber[0].astype(F32)
    copy_f(0, beside, 0).start()
    for n, d in enumerate(ALONG):
        pl.when(there(d))(lambda n=n, d=d: copy_f(0, d, 1 + n).start())

    def initial(step, c):
        send_z(0, step)
        return c

    lax.fori_loop(2, tiles, initial, 0)
    load_c.wait()

    spread_x = (iota2((256, 512), 0) % 128 == iota2((256, 512), 1) // 4).astype(BF16)
    spread_y = (iota2((rows, rows // 4), 0) // 4 == iota2((rows, rows // 4), 1)).astype(BF16)
    for c in range(6):
        tall = [
            jnp.dot(spread_y, part, preferred_element_type=F32).astype(BF16)
            for part in halves(cond[c, 0])
        ]
        for h in range(width // 512):
            part = jnp.concatenate([t[:, h * 128 : (h + 1) * 128] for t in tall], axis=1)
            part = jnp.dot(part, spread_x, preferred_element_type=F32)
            coeff[c, :, h * 512 : (h + 1) * 512] = part if c < 3 else 0.5 * part

    def centre_weight(t, c):
        at = pl.ds(pl.multiple_of(TILE * t, TILE), TILE)
        coeff[6, at, :] = 1.0 - 2.0 * (coeff[0, at, :] + coeff[1, at, :] + coeff[2, at, :])
        return c

    lax.fori_loop(0, tiles, centre_weight, 0)

    load_g.wait()
    load_t.wait()

    lane = iota2((TILE, width), 1)

    def left(f):
        return jnp.where(lane == 0, 0.0, pltpu.roll(f, 1, 1))

    def right(f):
        return jnp.where(lane == width - 1, 0.0, pltpu.roll(f, width - 1, 1))

    line = iota2((TILE, width), 0)

    def north_south(tall):
        here = tall[TILE : 2 * TILE]
        return (
            pltpu.roll(jnp.where(line == 0, tall[2 * TILE :], here), TILE - 1, 0),
            pltpu.roll(jnp.where(line == TILE - 1, tall[:TILE], here), 1, 0),
        )

    def layer(k, z, r):
        base = pl.multiple_of(TILE * r, TILE)
        here = pl.ds(base, TILE)
        tall = pl.ds(base, 3 * TILE)
        below = ubuf[k, z, tall, :]
        mid = ubuf[k, z + 1, tall, :]
        above = ubuf[k, z + 2, tall, :]
        odd = above - below
        centre = mid[TILE : 2 * TILE]
        odd0 = odd[TILE : 2 * TILE]
        north, south = north_south(mid)
        odd_north, odd_south = north_south(odd)
        slope = north - south
        total = coeff[6, here, :] * centre
        total = total + coeff[0, here, :] * (above[TILE : 2 * TILE] + below[TILE : 2 * TILE])
        total = total + coeff[1, here, :] * (north + south)
        total = total + coeff[2, here, :] * (right(centre) + left(centre))
        total = total + coeff[3, here, :] * (odd_north - odd_south)
        total = total + coeff[4, here, :] * (right(odd0) - left(odd0))
        total = total + coeff[5, here, :] * (right(slope) - left(slope))
        dif[...] = total
        up = pl.ds(pl.multiple_of(base + TILE, TILE), TILE)
        for x in range(0, width, CHUNK):
            xs = pl.ds(x, CHUNK)
            du, v2, w2, s2 = ionic(
                ubuf[k, z + 1, up, xs], out[1, z, here, xs], out[2, z, here, xs],
                out[3, z, here, xs],
            )
            u2 = dif[:, xs] + du
            ubuf[k + 1, z + 1, up, xs] = u2
            out[0, z, here, xs] = u2
            out[1, z, here, xs] = v2
            out[2, z, here, xs] = w2
            out[3, z, here, xs] = s2

    def leave(step):
        at = pl.ds(pl.multiple_of(TILE * row_of(step), TILE), TILE)
        return pltpu.make_async_copy(
            out.at[:, :, at, :], out_hbm.at[:, :, at, :], store_sem.at[step]
        )

    pair_x = (iota2((256, 128), 0) // 2 == iota2((256, 128), 1)).astype(F32)
    pair_2 = (iota2((512, 128), 0) % 256 // 2 == iota2((512, 128), 1)).astype(BF16)
    pair_y2 = (iota2((half, 2 * half), 0) == iota2((half, 2 * half), 1) // 2).astype(F32)

    def pool_lanes(rows_in, weights, size, chunk):
        parts = halves(rows_in)
        for h in range(width // chunk):
            both_halves = jnp.concatenate(
                [part[:, h * chunk : (h + 1) * chunk] for part in parts], axis=1
            )
            pooled[h, 0:size] = jnp.dot(both_halves, weights, preferred_element_type=F32)

    def tense(p):
        fine = pl.ds(pl.multiple_of(2 * TILE * p, 2 * TILE), 2 * TILE)
        wide = pl.ds(pl.multiple_of(TILE * p, TILE), TILE)
        sums = []
        for q in range(depth // 2):
            layers = out[0, 2 * q, fine, :] + out[0, 2 * q + 1, fine, :]
            sums.append(layers + pltpu.roll(layers, 2 * TILE - 1, 0))
        pool_lanes(0.125 * jnp.concatenate(sums, axis=0), pair_2, TILE * depth, 256)
        for h in range(width // 256):
            xo = slice(h * 128, (h + 1) * 128)
            for q in range(depth // 2):
                mean = pooled[h, pl.ds(2 * TILE * q, TILE, 2), :]
                before = tension[q, wide, xo]
                ten_out[q, wide, xo] = before + 0.5 * (mean - before)

    pool_x = (iota2((1024, 128), 0) % 512 // 4 == iota2((1024, 128), 1)).astype(BF16)

    def activate(part, lines):
        fine = pl.ds(pl.multiple_of(4 * TILE * part, 4 * TILE), 4 * TILE)
        layers = out[0, 0, fine, :]
        for z in range(1, depth):
            layers = layers + out[0, z, fine, :]
        layers = layers + pltpu.roll(layers, 4 * TILE - 1, 0)
        layers = layers + pltpu.roll(layers, 4 * TILE - 2, 0)
        pool_lanes((0.5 / (16 * depth)) * layers, pool_x, 4 * TILE, 512)
        for h in range(width // 512):
            xo = slice(h * 128, (h + 1) * 128)
            act_win[REACH, lines, xo] = act_win[REACH, lines, xo] + pooled[h, pl.ds(0, TILE, 4), :]

    def copy_a(d, to, kind, lines, at):
        return pltpu.make_async_remote_copy(
            src_ref=act_win.at[REACH, lines, :],
            dst_ref=act_win.at[REACH - d, at, :],
            send_sem=sa.at[d + REACH, kind],
            recv_sem=ra.at[REACH - d, kind],
            device_id=(grp, slab + d, to),
            device_id_type=MESH,
        )

    def each_a(act, centre):
        for d in sorted(range(-REACH, REACH + 1), key=lambda d: -abs(d)):
            if d != 0 or centre:
                pl.when(there(d))(lambda d=d: act(d))

    mech = Stencils(span, fix_win.shape[3])

    def inside(j):
        return there(j - RADIUS)

    def prepare(j):
        ok = inside(j)
        f = mech.deformation(lambda i, d: fix_win[j + d, i])
        fdir = directions(fix_win[j, 3])
        pieces = first_piola(f)
        for n in range(9):
            passive[n, j - 1] = jnp.where(ok, pieces[n], 0.0)
        for i in range(3):
            g = 0.5 * (f[i][0] * fdir[0] + f[i][1] * fdir[1] + f[i][2] * fdir[2])
            pull[i, j - 1] = jnp.where(ok, g, 0.0)
            pull[3 + i, j - 1] = fdir[i]

    def shift(j):
        ok = inside(j)
        for i in range(3):
            force = mech.force(lambda n, d: passive[n, j - 1 + d], i)
            moved = fix_win[j, i] + (MECH_RATE / 128.0) * force
            shifted[i, j - 2] = jnp.where(ok, moved, 0.0)

    hand_shift = pltpu.make_async_copy(shifted, shift_hbm, load_sem.at[0])
    hand_pull = pltpu.make_async_copy(pull, pull_hbm, load_sem.at[1])

    for h in range(width // 512):
        xs = slice(h * 256, (h + 1) * 256)
        layers = tension[0, :, xs] + tension[1, :, xs]
        mean = jnp.dot(layers, pair_x, precision=HI, preferred_element_type=F32)
        mean = 0.0625 * jnp.dot(pair_y2, mean, precision=HI, preferred_element_type=F32)
        act_win[REACH, own, h * 128 : (h + 1) * 128] = mean

    def within(n):
        k = n // tiles
        r = row_of(n % tiles)

        def inner(m, c):
            layer(k, m, r)
            return c

        lax.fori_loop(1, depth - 1, inner, 0)

    recv_z(0, 0)
    send_c(0)
    copy_y(0).wait_recv()
    within(0)
    for n in range(1, LAG):
        hand_on(n)

    def chunk(n, c):
        k = n // tiles
        step = n % tiles
        r = row_of(step)
        hand_on(n + LAG)

        @pl.when(n == tiles // 2)
        def _():
            come_f(beside).wait_recv()

        for far_by in (2, 4, 6):

            @pl.when(n == tiles // 2 + far_by // 2 - 1)
            def _(far_by=far_by):
                forward_f(lambda n, d: relay_f(n, d).start() if abs(d) == far_by else None)

        @pl.when(n == JOIN)
        def _():
            for d in range(-RADIUS, RADIUS + 1):
                if d != 0:
                    arrives = there(d) if d % 2 == 0 else there(d) & (beside != d)
                    pl.when(arrives)(lambda d=d: come_f(d).wait_recv())
            share_f(col).start()

        @pl.when(n == JOIN + 2)
        def _():
            share_f(col).wait_recv()

        @pl.when(step < tiles - 1)
        def _():
            recv_z(k, step + 1)

        @pl.when(step == 0)
        def _():
            recv_c(k)

        def outer(m, c):
            layer(k, m * (depth - 1), r)
            return c

        lax.fori_loop(0, 2, outer, 0)

        @pl.when(k < SUB - 1)
        def _():
            send_z(k + 1, step)

        @pl.when((k < SUB - 1) & (step == 0))
        def _():
            copy_y(k + 1).start()

        @pl.when((k < SUB - 1) & (step == tiles - 1))
        def _():
            recv_z(k + 1, 0)
            send_c(k + 1)
            copy_y(k + 1).wait_recv()

        @pl.when(n < SUB * tiles - 1)
        def _():
            within(n + 1)

        turn = n - JOIN - 2
        stress_turn = (turn < 2) | (turn % 2 == 0)

        @pl.when((turn >= 0) & (turn < LAST) & stress_turn)
        def _():
            prepare(jnp.where(turn < 2, turn + 1, turn // 2 + 2))

        @pl.when((turn >= 3) & (turn < LAST) & jnp.logical_not(stress_turn))
        def _():
            shift((turn + 1) // 2)

        @pl.when(turn == LAST)
        def _():
            hand_shift.start()
            hand_pull.start()

        @pl.when(k == SUB - 1)
        def _():
            leave(step).start()

        @pl.when(n == SUB * tiles - 1 - tiles // 2)
        def _():
            activate(other, near)
            each_a(lambda d: copy_a(d, col, 0, near, near).start(), False)
            each_a(lambda d: copy_a(d, other, 1, near, far).start(), True)

        @pl.when((k == SUB - 1) & (step % 2 == 1) & (step < tiles - 1))
        def _():
            tense(r // 2)

        return c

    lax.fori_loop(0, SUB * tiles, chunk, 0)

    activate(col, far)
    each_a(lambda d: copy_a(d, col, 2, far, far).start(), False)
    tense(row_of(tiles - 1) // 2)
    share_f(col).wait_send()
    copy_f(0, beside, 0).wait_send()
    for n, d in enumerate(ALONG):
        pl.when(there(d))(lambda n=n, d=d: copy_f(0, d, 1 + n).wait_send())
    forward_f(lambda n, d: relay_f(n, d).wait_send())
    hand_shift.wait()
    hand_pull.wait()
    copy_y(0).wait_send()

    def drain(slot, c):
        both(lambda: copy_c(slot, 0).wait_send(), lambda: copy_c(slot, 1).wait_send())

        @pl.when(slot > 0)
        def _():
            copy_y(slot).wait_send()

        def tile(step, c):
            both(
                lambda: copy_z(slot, 0, step).wait_send(),
                lambda: copy_z(slot, 1, step).wait_send(),
            )
            pl.when(carried(step, others))(lambda: copy_on(slot, step).wait_send())
            return c

        return lax.fori_loop(0, tiles, tile, c)

    lax.fori_loop(0, SUB, drain, 0)

    def left_all(step, c):
        leave(step).wait()
        return c

    lax.fori_loop(0, tiles, left_all, 0)
    each_a(lambda d: copy_a(d, col, 0, near, near).wait_send(), False)
    each_a(lambda d: copy_a(d, other, 1, near, far).wait_send(), True)
    each_a(lambda d: copy_a(d, col, 2, far, far).wait_send(), False)
    each_a(lambda d: copy_a(-d, col, 0, near, near).wait_recv(), False)
    each_a(lambda d: copy_a(-d, other, 1, near, far).wait_recv(), True)
    each_a(lambda d: copy_a(-d, col, 2, far, far).wait_recv(), False)
    hand_act = pltpu.make_async_copy(act_win, act_hbm, load_sem.at[0])
    hand_act.start()
    hand_act.wait()


def excite(slabs, states, cond, tension, fiber, disp):
    _, depth, rows, width = states.shape
    tiles = rows // TILE
    full = rows // 4 + TILE
    across = cond.shape[3]
    vmem = pl.BlockSpec(memory_space=pltpu.VMEM)
    hbm = pl.BlockSpec(memory_space=pltpu.HBM)
    window = (2 * REACH + 1, full, across)
    shifts = (3, 2 * REACH - 1, full, across)
    pulls = (6, 2 * REACH + 1, full, across)
    dma = pltpu.SemaphoreType.DMA
    return pl.pallas_call(
        functools.partial(excite_kernel, slabs),
        out_shape=(
            jax.ShapeDtypeStruct(states.shape, F32),
            jax.ShapeDtypeStruct(tension.shape, F32),
            jax.ShapeDtypeStruct(window, F32),
            jax.ShapeDtypeStruct(shifts, F32),
            jax.ShapeDtypeStruct(pulls, F32),
        ),
        in_specs=[hbm, hbm, hbm, hbm, hbm],
        out_specs=(hbm, vmem, hbm, hbm, hbm),
        scratch_shapes=[
            pltpu.VMEM((SUB + 1, depth + 2, rows + 2 * TILE, width), F32),
            pltpu.VMEM(states.shape, F32),
            pltpu.VMEM(cond.shape, F32),
            pltpu.VMEM(tension.shape, F32),
            pltpu.VMEM((7, rows, width), F32),
            pltpu.VMEM((TILE, width), F32),
            pltpu.VMEM(window, F32),
            pltpu.VMEM((2 * RADIUS + 1, 4, full, across), F32),
            pltpu.VMEM(fiber.shape, jnp.int32),
            pltpu.VMEM((9, *window), F32),
            pltpu.VMEM(shifts, F32),
            pltpu.VMEM(pulls, F32),
            pltpu.VMEM((width // 256, 4 * TILE, 128), F32),
            dma((6,)),
            dma((tiles,)),
            dma((SUB, 2, tiles)),
            dma((SUB, 2, tiles)),
            dma((SUB, 2)),
            dma((SUB, 2)),
            dma((SUB,)),
            dma((SUB,)),
            dma((2 * REACH + 1, 3)),
            dma((2 * REACH + 1, 3)),
            dma((1 + len(ALONG) + len(BEYOND),)),
            dma((2 * RADIUS + 1,)),
            dma((2,)),
            pltpu.VMEM((SUB, rows, width), F32),
            dma((SUB, tiles)),
            dma((SUB, tiles)),
        ],
        compiler_params=pltpu.CompilerParams(
            collective_id=0, has_side_effects=True, vmem_limit_bytes=61 << 20
        ),
        cost_estimate=pl.CostEstimate(
            flops=200_000_000, bytes_accessed=16 << 20, transcendentals=6_000_000
        ),
        name="excite",
    )(states, cond, tension, fiber, disp)


def mech_kernel(
    slabs, active, shifted, pull, ten_in, states_in,
    disp_out, cond_out, ten_out, states_out, stress, moved, held, sem,
):
    slab = lax.axis_index("slab")
    first = lax.axis_index("col") == 0
    rows, width = active.shape[1:]
    half = rows - TILE
    fetch = pltpu.make_async_copy(states_in, held, sem.at[0])
    hand_on = pltpu.make_async_copy(held, states_out, sem.at[1])
    fetch.start()
    ten_out[...] = ten_in[...]
    mech = Stencils(rows, width)

    def inside(j):
        zz = slab + j - REACH
        return (zz >= 0) & (zz < slabs)

    def tense(j, c):
        for a in range(3):
            t = active[j] * pull[3 + a, j]
            for i in range(3):
                stress[3 * a + i, j] = t * pull[i, j]
        return c

    def move(field):
        def body(j, c):
            ok = inside(j)
            for i in range(3):
                force = mech.force(lambda n, d: stress[n, j + d], i)
                moved[i, j] = jnp.where(ok, field(i, j) + (MECH_RATE / 128.0) * force, 0.0)
            return c

        return body

    def strain(j, c):
        ok = inside(j)
        f = mech.deformation(lambda i, d: moved[i, j + d])
        pieces = first_piola(f, active[j], [pull[3 + a, j] for a in range(3)])
        for n in range(9):
            stress[n, j] = jnp.where(ok, pieces[n], 0.0)
        return c

    lax.fori_loop(0, 2 * REACH + 1, tense, 0)
    lax.fori_loop(1, 2 * REACH, move(lambda i, j: shifted[i, j - 1]), 0)
    fetch.wait()
    hand_on.start()
    lax.fori_loop(2, 2 * REACH - 1, strain, 0)
    lax.fori_loop(3, 2 * REACH - 2, move(lambda i, j: moved[i, j]), 0)

    comps = metric(
        mech.deformation(lambda i, d: moved[i, REACH + d]),
        [pull[3 + a, REACH] for a in range(3)],
    )
    for i in range(3):
        whole = moved[i, REACH]
        disp_out[i, 0] = jnp.where(first, whole[:half], whole[TILE:])
    for n in range(6):
        cond_out[n, 0] = jnp.where(first, comps[n][:half], comps[n][TILE:])
    hand_on.wait()


def mechanics(slabs, active, shifted, pull, tension, states):
    _, full, width = active.shape
    rows = full - TILE
    vmem = pl.BlockSpec(memory_space=pltpu.VMEM)
    hbm = pl.BlockSpec(memory_space=pltpu.HBM)
    return pl.pallas_call(
        functools.partial(mech_kernel, slabs),
        out_shape=(
            jax.ShapeDtypeStruct((3, 1, rows, width), F32),
            jax.ShapeDtypeStruct((6, 1, rows, width), F32),
            jax.ShapeDtypeStruct(tension.shape, F32),
            jax.ShapeDtypeStruct(states.shape, F32),
        ),
        in_specs=[vmem, vmem, vmem, vmem, hbm],
        out_specs=(vmem, vmem, vmem, hbm),
        scratch_shapes=[
            pltpu.VMEM((9, 2 * REACH + 1, full, width), F32),
            pltpu.VMEM((3, 2 * REACH + 1, full, width), F32),
            pltpu.VMEM(states.shape, F32),
            pltpu.SemaphoreType.DMA((2,)),
        ],
        compiler_params=pltpu.CompilerParams(vmem_limit_bytes=61 << 20),
        name="mechanics",
    )(active, shifted, pull, tension, states)


def on_device(slabs, states, cond, tension, fiber, disp):
    states_next, tension_next, active, shifted, pull = excite(
        slabs, states, cond, tension, fiber, disp
    )
    disp_next, cond_next, tension_next, states_next = mechanics(
        slabs, active, shifted, pull, tension_next, states_next
    )
    return states_next, tension_next, disp_next, cond_next


def solution(mesh):
    wide = P(None, ("grp", "slab"), "col", None)
    flat = P(("grp", "slab"), "col", None)
    return jax.shard_map(
        functools.partial(on_device, mesh.shape["slab"]),
        mesh=mesh,
        in_specs=(wide, wide, flat, flat, wide),
        out_specs=(wide, flat, wide, wide),
        check_vma=False,
    )
```

```python
import functools

import jax
import jax.numpy as jnp
import numpy as np
from jax import lax
from jax.experimental import pallas as pl
from jax.experimental.pallas import tpu as pltpu
from jax.sharding import PartitionSpec as P

SUB = 4
MECH_STEPS = 2
NFIB = 64
STEP_TIME = 0.05
MECH_RATE = 0.15
SIGMA_LONG = 0.16
SIGMA_TRANS = 0.04
PAIRS = ((0, 0), (1, 1), (2, 2), (0, 1), (0, 2), (1, 2))
MESH = pl.DeviceIdType.MESH
HI = lax.Precision.HIGHEST
F32 = jnp.float32
BF16 = jnp.bfloat16
TILE = 8
CHUNK = 256
RADIUS = 2 * MECH_STEPS + 1
REACH = RADIUS - 1
ALONG = (-4, -2, 2, 4)
BEYOND = (-6, -4, -2, 2, 4, 6)
PEERS = (-6, -4, -3, -2, -1, 0, 1, 2, 3, 4, 6)
JOIN = 10
LAST = 4 * REACH
LAG = 4
HOLD = 2


def ionic(u, v, w, s):
    per = 2.0 / STEP_TIME
    steep = 50.0 * u
    th_v = jnp.tanh(steep - 50.0 * 0.3)
    th_w = jnp.tanh(steep - 50.0 * 0.13)
    th_o = jnp.tanh(steep - 50.0 * 0.006)
    th_m = jnp.tanh(65.0 * u - 65.0 * 0.03)
    th_s = jnp.tanh(2.0458 * u - 2.0458 * 0.65)
    th_r = jnp.tanh(2.0994 * u - 2.0994 * 0.9087)
    hv2 = 1.0 + th_v
    nv2 = 1.0 - th_v
    hw2 = 1.0 + th_w
    nw2 = 1.0 - th_w
    no = 0.5 - 0.5 * th_o
    rate_v = 1.0 / (605.0 * per + (545.0 * per) * th_o)
    rate_w = 1.0 / (37.5 * per - (22.5 * per) * th_m)
    rate_so = 1.0 / (15.5069 * per - (14.5112 * per) * th_s)
    rate_s = 1.0 / (9.3671 * per + (6.6329 * per) * th_w)
    rate_o = 1.0 / (203.0 * per - (197.0 * per) * th_o)
    lead = STEP_TIME / 0.22
    open_v = hv2 * v
    w_inf = no * (0.06 - u * (1.0 / 0.07)) + 0.94
    du = (
        open_v * ((u - 0.3) * (1.55 * lead - lead * u))
        + hw2 * ((w * s) * (STEP_TIME / 3.775) - rate_so)
        - (u * nw2) * rate_o
    )
    v2 = v - open_v * (STEP_TIME / 2.9012) + (nv2 * rate_v) * (no - v)
    w2 = w - (hw2 * w) * (STEP_TIME / 400.0) + (nw2 * rate_w) * (w_inf - w)
    s2 = s + ((1.0 + th_r) - 2.0 * s) * rate_s
    return du, v2, w2, s2


def iota2(shape, dim):
    return lax.broadcasted_iota(jnp.int32, shape, dim)


def first_piola(f, active=None, fdir=None):
    second = {}
    for a in range(3):
        for b in range(a, 3):
            right = f[0][a] * f[0][b] + f[1][a] * f[1][b] + f[2][a] * f[2][b]
            second[a, b] = 0.5 * (right - (1.0 if a == b else 0.0))
    trace = second[0, 0] + second[1, 1] + second[2, 2]
    for a in range(3):
        if active is not None:
            scaled = 0.5 * active * fdir[a]
            for b in range(a, 3):
                second[a, b] = second[a, b] + scaled * fdir[b]
        second[a, a] = second[a, a] + trace
    for a in range(3):
        for b in range(a):
            second[a, b] = second[b, a]
    return [
        f[i][0] * second[0, a] + f[i][1] * second[1, a] + f[i][2] * second[2, a]
        for a in range(3)
        for i in range(3)
    ]


def metric(f, fdir):
    cof = [[None] * 3 for _ in range(3)]
    for i in range(3):
        for j in range(3):
            cof[i][j] = (
                f[(i + 1) % 3][(j + 1) % 3] * f[(i + 2) % 3][(j + 2) % 3]
                - f[(i + 1) % 3][(j + 2) % 3] * f[(i + 2) % 3][(j + 1) % 3]
            )
    det = f[0][0] * cof[0][0] + f[0][1] * cof[0][1] + f[0][2] * cof[0][2]
    scale = 1.0 / det
    inverse = [[cof[i][j] * scale for i in range(3)] for j in range(3)]
    g = [inverse[a][0] * fdir[0] + inverse[a][1] * fdir[1] + inverse[a][2] * fdir[2] for a in range(3)]
    comps = []
    for a, b in PAIRS:
        inner = (
            inverse[a][0] * inverse[b][0]
            + inverse[a][1] * inverse[b][1]
            + inverse[a][2] * inverse[b][2]
        )
        comps.append(SIGMA_TRANS * inner + (SIGMA_LONG - SIGMA_TRANS) * (g[a] * g[b]))
    return comps


class Stencils:
    def __init__(self, rows, width):
        self.rows, self.width = rows, width
        self.lane = iota2((rows, width), 1)
        self.line = iota2((rows, width), 0)

    def left(self, f):
        return jnp.where(self.lane == 0, 0.0, pltpu.roll(f, 1, 1))

    def right(self, f):
        return jnp.where(self.lane == self.width - 1, 0.0, pltpu.roll(f, self.width - 1, 1))

    def south(self, f):
        return jnp.where(self.line == 0, 0.0, pltpu.roll(f, 1, 0))

    def north(self, f):
        return jnp.where(self.line == self.rows - 1, 0.0, pltpu.roll(f, self.rows - 1, 0))


    def sx(self, f):
        return self.left(f) + self.right(f) + 6.0 * f

    def dx(self, f):
        return self.right(f) - self.left(f)

    def sy(self, f):
        return self.south(f) + self.north(f) + 6.0 * f

    def dy(self, f):
        return self.north(f) - self.south(f)

    def deformation(self, field):
        f = []
        for i in range(3):
            low, mid, high = field(i, -1), field(i, 0), field(i, 1)
            zs = low + high + 6.0 * mid
            zd = high - low
            grads = [self.sy(self.sx(zd)), self.dy(self.sx(zs)), self.sy(self.dx(zs))]
            f.append([(1.0 / 128.0) * g for g in grads])
            f[i][i] = f[i][i] + 1.0
        return f

    def force(self, stress, i):
        zd = stress(i, 1) - stress(i, -1)
        ys = stress(3 + i, -1) + stress(3 + i, 1) + 6.0 * stress(3 + i, 0)
        xs = stress(6 + i, -1) + stress(6 + i, 1) + 6.0 * stress(6 + i, 0)
        return self.sy(self.sx(zd) + self.dx(xs)) + self.dy(self.sx(ys))


def sine(x, terms=6):
    y = x * x
    c = 1.0
    for n in range(2 * terms, 0, -2):
        c = 1.0 - y * (1.0 / (n * (n + 1))) * c
    return x * c


def cosine(x):
    y = x * x
    c = 1.0
    for n in (13, 11, 9, 7, 5, 3, 1):
        c = 1.0 - y * (1.0 / (n * (n + 1))) * c
    return c


def directions(index):
    theta = -1.0 + index * (2.0 / (NFIB - 1))
    triple = 3.0 * index
    turns = jnp.floor(triple * (0.5 / np.pi) + 0.5)
    triple = (triple - turns * 6.28125) - turns * (2.0 * np.pi - 6.28125)
    tilt = 0.3 * sine(triple, 10)
    flat = cosine(tilt)
    return [sine(tilt), flat * sine(theta), flat * cosine(theta)]


def halves(x):
    high = x.astype(BF16)
    return high, (x - high.astype(F32)).astype(BF16)


def excite_kernel(
    slabs, states, cond_hbm, ten_hbm, fib_hbm, disp_hbm,
    out_hbm, ten_out, act_hbm, shift_hbm, pull_hbm,
    ubuf, out, cond, tension, coeff, dif, act_win, fix_win, fiber, passive, shifted, pull, pooled,
    load_sem, store_sem, sz, rz, sc, rc, sy, ry, sa, ra, sf, rf, sg, relay, sv, rv,
):
    grp = lax.axis_index("grp")
    slab = lax.axis_index("slab")
    col = lax.axis_index("col")
    other = 1 - col
    depth, rows, width = out.shape[1:]
    tiles = rows // TILE
    has_up = slab < slabs - 1
    has_dn = slab > 0
    edge_src = rows - (rows - TILE) * col
    edge_dst = (rows + TILE) * col

    load_u = pltpu.make_async_copy(
        states.at[0], ubuf.at[0, pl.ds(1, depth), pl.ds(TILE, rows), :], load_sem.at[0]
    )
    load_g = pltpu.make_async_copy(
        states.at[pl.ds(1, 3)], out.at[pl.ds(1, 3)], load_sem.at[1]
    )
    load_c = pltpu.make_async_copy(cond_hbm, cond, load_sem.at[2])
    load_t = pltpu.make_async_copy(ten_hbm, tension, load_sem.at[3])
    load_u.start()
    load_c.start()
    load_g.start()
    load_t.start()
    half = rows // 4
    span = half + TILE
    own = pl.ds(pl.multiple_of(TILE * col, TILE), half)
    near = pl.ds(TILE, TILE)
    far = pl.ds(pl.multiple_of(2 * TILE * col, TILE), TILE)
    load_d = pltpu.make_async_copy(
        disp_hbm.at[:, 0], fix_win.at[RADIUS, pl.ds(0, 3), own, :], load_sem.at[4]
    )
    load_f = pltpu.make_async_copy(fib_hbm, fiber, load_sem.at[5])
    load_d.start()
    load_f.start()

    barrier = pltpu.get_barrier_semaphore()

    def greet(where):
        pl.semaphore_signal(barrier, inc=1, device_id=where, device_id_type=MESH)

    def there(d):
        return (slab + d >= 0) & (slab + d < slabs)

    peers = 0
    for d in PEERS:
        valid = there(d)
        wide = abs(d) <= REACH
        count = (0 if d == 0 else 1) + (1 if wide else 0)
        peers = peers + count * valid.astype(jnp.int32)

        @pl.when(valid)
        def _(d=d, wide=wide):
            if wide:
                greet((grp, slab + d, other))
            if d != 0:
                greet((grp, slab + d, col))

    for d in range(-RADIUS, RADIUS + 1):

        @pl.when(jnp.logical_not(there(d)))
        def _(d=d):
            fix_win[d + RADIUS] = jnp.zeros(fix_win.shape[1:], F32)
            if abs(d) <= REACH:
                act_win[d + REACH] = jnp.zeros(act_win.shape[1:], F32)

    blank = jnp.zeros((TILE, width), F32)

    def clear_y(n, c):
        ubuf[n // (depth + 2), n % (depth + 2), pl.ds(pl.multiple_of(edge_dst, TILE), TILE), :] = blank
        return c

    lax.fori_loop(0, SUB * (depth + 2), clear_y, 0)

    def clear_z(layer):
        per = rows // TILE + 2

        def body(n, c):
            ubuf[n // per, layer, pl.ds(pl.multiple_of((n % per) * TILE, TILE), TILE), :] = blank
            return c

        lax.fori_loop(0, SUB * per, body, 0)

    @pl.when(slab == 0)
    def _():
        clear_z(0)

    @pl.when(slab == slabs - 1)
    def _():
        clear_z(depth + 1)

    def row_of(step):
        return jnp.where(col == 1, step, tiles - 1 - step)

    def copy_z(slot, way, step):
        at = pl.ds(pl.multiple_of(TILE + TILE * row_of(step), TILE), TILE)
        src = depth if way == 0 else 1
        dst = 0 if way == 0 else depth + 1
        to = slab + 1 if way == 0 else slab - 1
        return pltpu.make_async_remote_copy(
            src_ref=ubuf.at[slot, src, at, :],
            dst_ref=ubuf.at[slot, dst, at, :],
            send_sem=sz.at[slot, way, step],
            recv_sem=rz.at[slot, way, step],
            device_id=(grp, to, col),
            device_id_type=MESH,
        )

    def carried(step, count):
        return lax.rem((step + 1) * count, tiles) < count

    beside = 1 - 2 * lax.rem(slab, 2)
    chips = slabs // 2
    upper = tiles * (chips - 1 - slab // 2) // chips
    lower = tiles * (slab // 2) // chips
    even = beside == 1
    mine = jnp.where(even, lower, upper)
    others = jnp.where(even, upper, lower)
    onward = 1 - lax.rem(slab + 1, 2)

    def copy_via(slot, way, step):
        at = pl.ds(pl.multiple_of(TILE + TILE * row_of(step), TILE), TILE)
        to = pl.ds(pl.multiple_of(TILE * row_of(step), TILE), TILE)
        return pltpu.make_async_remote_copy(
            src_ref=ubuf.at[slot, depth if way == 0 else 1, at, :],
            dst_ref=relay.at[slot, to, :],
            send_sem=sz.at[slot, way, step],
            recv_sem=rv.at[slot, step],
            device_id=(grp, slab + beside, col),
            device_id_type=MESH,
        )

    def copy_on(slot, step):
        at = pl.ds(pl.multiple_of(TILE * row_of(step), TILE), TILE)
        to = pl.ds(pl.multiple_of(TILE + TILE * row_of(step), TILE), TILE)
        return pltpu.make_async_remote_copy(
            src_ref=relay.at[slot, at, :],
            dst_ref=ubuf.at[slot, onward * (depth + 1), to, :],
            send_sem=sv.at[slot, step],
            recv_sem=rz.at[slot, onward, step],
            device_id=(grp, slab + 2 * beside, col),
            device_id_type=MESH,
        )

    def hand_on(n):
        @pl.when((n < SUB * tiles) & carried(n % tiles, others))
        def _():
            copy_via(n // tiles, 0, n % tiles).wait_recv()
            copy_on(n // tiles, n % tiles).start()

    def copy_c(slot, way):
        at = depth + 1 if way == 0 else 0
        return pltpu.make_async_remote_copy(
            src_ref=ubuf.at[slot, at, pl.ds(pl.multiple_of(edge_src, TILE), TILE), :],
            dst_ref=ubuf.at[slot, at, pl.ds(pl.multiple_of(edge_dst, TILE), TILE), :],
            send_sem=sc.at[slot, way],
            recv_sem=rc.at[slot, way],
            device_id=(grp, slab, other),
            device_id_type=MESH,
        )

    def copy_y(slot):
        return pltpu.make_async_remote_copy(
            src_ref=ubuf.at[slot, pl.ds(1, depth), pl.ds(pl.multiple_of(edge_src, TILE), TILE), :],
            dst_ref=ubuf.at[slot, pl.ds(1, depth), pl.ds(pl.multiple_of(edge_dst, TILE), TILE), :],
            send_sem=sy.at[slot],
            recv_sem=ry.at[slot],
            device_id=(grp, slab, other),
            device_id_type=MESH,
        )

    def both(do_up, do_dn):
        pl.when(has_up)(do_up)
        pl.when(has_dn)(do_dn)

    def send_z(n, by_partner):
        slot = n // tiles
        step = n % tiles
        via = carried(step, mine)

        def send(way):
            through = via & (jnp.logical_not(even) if way == 0 else even)
            if by_partner:
                pl.when(through)(lambda: copy_via(slot, way, step).start())
            else:
                pl.when(jnp.logical_not(through))(lambda: copy_z(slot, way, step).start())

        @pl.when(n < SUB * tiles)
        def _():
            both(lambda: send(0), lambda: send(1))

    def send_c(slot):
        both(lambda: copy_c(slot, 0).start(), lambda: copy_c(slot, 1).start())

    def recv_z(slot, step):
        both(lambda: copy_z(slot, 1, step).wait_recv(), lambda: copy_z(slot, 0, step).wait_recv())

    def recv_c(slot):
        both(lambda: copy_c(slot, 0).wait_recv(), lambda: copy_c(slot, 1).wait_recv())

    def copy_f(source, d, n):
        slot = RADIUS + source - d
        return pltpu.make_async_remote_copy(
            src_ref=fix_win.at[RADIUS + source, :, own, :],
            dst_ref=fix_win.at[slot, :, own, :],
            send_sem=sf.at[n],
            recv_sem=rf.at[slot],
            device_id=(grp, slab + d, col),
            device_id_type=MESH,
        )

    def come_f(e):
        return pltpu.make_async_remote_copy(
            src_ref=fix_win.at[RADIUS, :, own, :],
            dst_ref=fix_win.at[RADIUS + e, :, own, :],
            send_sem=sf.at[0],
            recv_sem=rf.at[RADIUS + e],
            device_id=(grp, slab + e, col),
            device_id_type=MESH,
        )

    def share_f(whose):
        return pltpu.make_async_remote_copy(
            src_ref=fix_win.at[:, :, near, :],
            dst_ref=fix_win.at[:, :, pl.ds(pl.multiple_of(2 * TILE * whose, TILE), TILE), :],
            send_sem=sg.at[0],
            recv_sem=sg.at[1],
            device_id=(grp, slab, other),
            device_id_type=MESH,
        )

    def forward_f(act):
        for n, d in enumerate(BEYOND):
            ok = there(d) & (jnp.abs(d - beside) <= RADIUS)
            pl.when(ok)(lambda n=n, d=d: act(n, d))

    def relay_f(n, d):
        return copy_f(beside, d, 1 + len(ALONG) + n)

    pl.semaphore_wait(barrier, peers)

    load_u.wait()
    send_z(0, True)
    send_z(0, False)
    copy_y(0).start()
    send_z(1, True)
    send_z(1, False)
    load_d.wait()
    load_f.wait()
    fix_win[RADIUS, 3, own, :] = fiber[0].astype(F32)
    copy_f(0, beside, 0).start()
    for n, d in enumerate(ALONG):
        pl.when(there(d))(lambda n=n, d=d: copy_f(0, d, 1 + n).start())

    def initial(step, c):
        send_z(step, True)
        pl.when(step < tiles - HOLD)(lambda: send_z(step, False))
        return c

    lax.fori_loop(2, tiles, initial, 0)
    load_c.wait()

    spread_x = (iota2((256, 512), 0) % 128 == iota2((256, 512), 1) // 4).astype(BF16)
    spread_y = (iota2((rows, rows // 4), 0) // 4 == iota2((rows, rows // 4), 1)).astype(BF16)
    for c in range(6):
        tall = [
            jnp.dot(spread_y, part, preferred_element_type=F32).astype(BF16)
            for part in halves(cond[c, 0])
        ]
        for h in range(width // 512):
            part = jnp.concatenate([t[:, h * 128 : (h + 1) * 128] for t in tall], axis=1)
            part = jnp.dot(part, spread_x, preferred_element_type=F32)
            coeff[c, :, h * 512 : (h + 1) * 512] = part if c < 3 else 0.5 * part

    def centre_weight(t, c):
        at = pl.ds(pl.multiple_of(TILE * t, TILE), TILE)
        coeff[6, at, :] = 1.0 - 2.0 * (coeff[0, at, :] + coeff[1, at, :] + coeff[2, at, :])
        return c

    lax.fori_loop(0, tiles, centre_weight, 0)

    load_g.wait()
    load_t.wait()

    lane = iota2((TILE, width), 1)

    def left(f):
        return jnp.where(lane == 0, 0.0, pltpu.roll(f, 1, 1))

    def right(f):
        return jnp.where(lane == width - 1, 0.0, pltpu.roll(f, width - 1, 1))

    line = iota2((TILE, width), 0)

    def north_south(tall):
        here = tall[TILE : 2 * TILE]
        return (
            pltpu.roll(jnp.where(line == 0, tall[2 * TILE :], here), TILE - 1, 0),
            pltpu.roll(jnp.where(line == TILE - 1, tall[:TILE], here), 1, 0),
        )

    def layer(k, z, r):
        base = pl.multiple_of(TILE * r, TILE)
        here = pl.ds(base, TILE)
        tall = pl.ds(base, 3 * TILE)
        below = ubuf[k, z, tall, :]
        mid = ubuf[k, z + 1, tall, :]
        above = ubuf[k, z + 2, tall, :]
        odd = above - below
        centre = mid[TILE : 2 * TILE]
        odd0 = odd[TILE : 2 * TILE]
        north, south = north_south(mid)
        odd_north, odd_south = north_south(odd)
        slope = north - south
        total = coeff[6, here, :] * centre
        total = total + coeff[0, here, :] * (above[TILE : 2 * TILE] + below[TILE : 2 * TILE])
        total = total + coeff[1, here, :] * (north + south)
        total = total + coeff[2, here, :] * (right(centre) + left(centre))
        total = total + coeff[3, here, :] * (odd_north - odd_south)
        total = total + coeff[4, here, :] * (right(odd0) - left(odd0))
        total = total + coeff[5, here, :] * (right(slope) - left(slope))
        dif[...] = total
        up = pl.ds(pl.multiple_of(base + TILE, TILE), TILE)
        for x in range(0, width, CHUNK):
            xs = pl.ds(x, CHUNK)
            du, v2, w2, s2 = ionic(
                ubuf[k, z + 1, up, xs], out[1, z, here, xs], out[2, z, here, xs],
                out[3, z, here, xs],
            )
            u2 = dif[:, xs] + du
            ubuf[k + 1, z + 1, up, xs] = u2
            out[0, z, here, xs] = u2
            out[1, z, here, xs] = v2
            out[2, z, here, xs] = w2
            out[3, z, here, xs] = s2

    def leave(step):
        at = pl.ds(pl.multiple_of(TILE * row_of(step), TILE), TILE)
        return pltpu.make_async_copy(
            out.at[:, :, at, :], out_hbm.at[:, :, at, :], store_sem.at[step]
        )

    pair_x = (iota2((256, 128), 0) // 2 == iota2((256, 128), 1)).astype(F32)
    pair_2 = (iota2((512, 128), 0) % 256 // 2 == iota2((512, 128), 1)).astype(BF16)
    pair_y2 = (iota2((half, 2 * half), 0) == iota2((half, 2 * half), 1) // 2).astype(F32)

    def pool_lanes(rows_in, weights, size, chunk):
        parts = halves(rows_in)
        for h in range(width // chunk):
            both_halves = jnp.concatenate(
                [part[:, h * chunk : (h + 1) * chunk] for part in parts], axis=1
            )
            pooled[h, 0:size] = jnp.dot(both_halves, weights, preferred_element_type=F32)

    def tense(p):
        fine = pl.ds(pl.multiple_of(2 * TILE * p, 2 * TILE), 2 * TILE)
        wide = pl.ds(pl.multiple_of(TILE * p, TILE), TILE)
        sums = []
        for q in range(depth // 2):
            layers = out[0, 2 * q, fine, :] + out[0, 2 * q + 1, fine, :]
            sums.append(layers + pltpu.roll(layers, 2 * TILE - 1, 0))
        pool_lanes(0.125 * jnp.concatenate(sums, axis=0), pair_2, TILE * depth, 256)
        for h in range(width // 256):
            xo = slice(h * 128, (h + 1) * 128)
            for q in range(depth // 2):
                mean = pooled[h, pl.ds(2 * TILE * q, TILE, 2), :]
                before = tension[q, wide, xo]
                ten_out[q, wide, xo] = before + 0.5 * (mean - before)

    pool_x = (iota2((1024, 128), 0) % 512 // 4 == iota2((1024, 128), 1)).astype(BF16)

    def activate(part, lines):
        fine = pl.ds(pl.multiple_of(4 * TILE * part, 4 * TILE), 4 * TILE)
        layers = out[0, 0, fine, :]
        for z in range(1, depth):
            layers = layers + out[0, z, fine, :]
        layers = layers + pltpu.roll(layers, 4 * TILE - 1, 0)
        layers = layers + pltpu.roll(layers, 4 * TILE - 2, 0)
        pool_lanes((0.5 / (16 * depth)) * layers, pool_x, 4 * TILE, 512)
        for h in range(width // 512):
            xo = slice(h * 128, (h + 1) * 128)
            act_win[REACH, lines, xo] = act_win[REACH, lines, xo] + pooled[h, pl.ds(0, TILE, 4), :]

    def copy_a(d, to, kind, lines, at):
        return pltpu.make_async_remote_copy(
            src_ref=act_win.at[REACH, lines, :],
            dst_ref=act_win.at[REACH - d, at, :],
            send_sem=sa.at[d + REACH, kind],
            recv_sem=ra.at[REACH - d, kind],
            device_id=(grp, slab + d, to),
            device_id_type=MESH,
        )

    def each_a(act, centre):
        for d in sorted(range(-REACH, REACH + 1), key=lambda d: -abs(d)):
            if d != 0 or centre:
                pl.when(there(d))(lambda d=d: act(d))

    mech = Stencils(span, fix_win.shape[3])

    def inside(j):
        return there(j - RADIUS)

    def prepare(j):
        ok = inside(j)
        f = mech.deformation(lambda i, d: fix_win[j + d, i])
        fdir = directions(fix_win[j, 3])
        pieces = first_piola(f)
        for n in range(9):
            passive[n, j - 1] = jnp.where(ok, pieces[n], 0.0)
        for i in range(3):
            g = 0.5 * (f[i][0] * fdir[0] + f[i][1] * fdir[1] + f[i][2] * fdir[2])
            pull[i, j - 1] = jnp.where(ok, g, 0.0)
            pull[3 + i, j - 1] = fdir[i]

    def shift(j):
        ok = inside(j)
        for i in range(3):
            force = mech.force(lambda n, d: passive[n, j - 1 + d], i)
            moved = fix_win[j, i] + (MECH_RATE / 128.0) * force
            shifted[i, j - 2] = jnp.where(ok, moved, 0.0)

    hand_shift = pltpu.make_async_copy(shifted, shift_hbm, load_sem.at[0])
    hand_pull = pltpu.make_async_copy(pull, pull_hbm, load_sem.at[1])

    for h in range(width // 512):
        xs = slice(h * 256, (h + 1) * 256)
        layers = tension[0, :, xs] + tension[1, :, xs]
        mean = jnp.dot(layers, pair_x, precision=HI, preferred_element_type=F32)
        mean = 0.0625 * jnp.dot(pair_y2, mean, precision=HI, preferred_element_type=F32)
        act_win[REACH, own, h * 128 : (h + 1) * 128] = mean

    def within(n):
        k = n // tiles
        r = row_of(n % tiles)

        def inner(m, c):
            layer(k, m, r)
            return c

        lax.fori_loop(1, depth - 1, inner, 0)

    recv_z(0, 0)
    send_c(0)
    copy_y(0).wait_recv()
    within(0)

    def chunk(n, c):
        k = n // tiles
        step = n % tiles
        r = row_of(step)

        @pl.when(n < LAG - 1)
        def _():
            hand_on(2 * n + 1)
            hand_on(2 * n + 2)

        pl.when(n >= LAG - 1)(lambda: hand_on(n + LAG))

        @pl.when(n == tiles // 2)
        def _():
            come_f(beside).wait_recv()

        for far_by in (2, 4, 6):

            @pl.when(n == tiles // 2 + far_by // 2 - 1)
            def _(far_by=far_by):
                forward_f(lambda n, d: relay_f(n, d).start() if abs(d) == far_by else None)

        @pl.when(n == JOIN)
        def _():
            for d in range(-RADIUS, RADIUS + 1):
                if d != 0:
                    arrives = there(d) if d % 2 == 0 else there(d) & (beside != d)
                    pl.when(arrives)(lambda d=d: come_f(d).wait_recv())
            share_f(col).start()

        @pl.when(n == JOIN + 2)
        def _():
            share_f(col).wait_recv()

        @pl.when(step < tiles - 1)
        def _():
            recv_z(k, step + 1)

        @pl.when(step == 0)
        def _():
            recv_c(k)

        def outer(m, c):
            layer(k, m * (depth - 1), r)
            return c

        lax.fori_loop(0, 2, outer, 0)

        send_z(n + tiles, True)
        send_z(n + tiles - HOLD, False)

        @pl.when((k < SUB - 1) & (step == 0))
        def _():
            copy_y(k + 1).start()

        @pl.when((k < SUB - 1) & (step == tiles - 1))
        def _():
            recv_z(k + 1, 0)
            send_c(k + 1)
            copy_y(k + 1).wait_recv()

        @pl.when(n < SUB * tiles - 1)
        def _():
            within(n + 1)

        turn = n - JOIN - 2
        stress_turn = (turn < 2) | (turn % 2 == 0)

        @pl.when((turn >= 0) & (turn < LAST) & stress_turn)
        def _():
            prepare(jnp.where(turn < 2, turn + 1, turn // 2 + 2))

        @pl.when((turn >= 3) & (turn < LAST) & jnp.logical_not(stress_turn))
        def _():
            shift((turn + 1) // 2)

        @pl.when(turn == LAST)
        def _():
            hand_shift.start()
            hand_pull.start()

        @pl.when(k == SUB - 1)
        def _():
            leave(step).start()

        @pl.when(n == SUB * tiles - 1 - tiles // 2)
        def _():
            activate(other, near)
            each_a(lambda d: copy_a(d, col, 0, near, near).start(), False)
            each_a(lambda d: copy_a(d, other, 1, near, far).start(), True)

        @pl.when((k == SUB - 1) & (step % 2 == 1) & (step < tiles - 1))
        def _():
            tense(r // 2)

        return c

    lax.fori_loop(0, SUB * tiles, chunk, 0)

    activate(col, far)
    each_a(lambda d: copy_a(d, col, 2, far, far).start(), False)
    tense(row_of(tiles - 1) // 2)
    share_f(col).wait_send()
    copy_f(0, beside, 0).wait_send()
    for n, d in enumerate(ALONG):
        pl.when(there(d))(lambda n=n, d=d: copy_f(0, d, 1 + n).wait_send())
    forward_f(lambda n, d: relay_f(n, d).wait_send())
    hand_shift.wait()
    hand_pull.wait()
    copy_y(0).wait_send()

    def drain(slot, c):
        both(lambda: copy_c(slot, 0).wait_send(), lambda: copy_c(slot, 1).wait_send())

        @pl.when(slot > 0)
        def _():
            copy_y(slot).wait_send()

        def tile(step, c):
            both(
                lambda: copy_z(slot, 0, step).wait_send(),
                lambda: copy_z(slot, 1, step).wait_send(),
            )
            pl.when(carried(step, others))(lambda: copy_on(slot, step).wait_send())
            return c

        return lax.fori_loop(0, tiles, tile, c)

    lax.fori_loop(0, SUB, drain, 0)

    def left_all(step, c):
        leave(step).wait()
        return c

    lax.fori_loop(0, tiles, left_all, 0)
    each_a(lambda d: copy_a(d, col, 0, near, near).wait_send(), False)
    each_a(lambda d: copy_a(d, other, 1, near, far).wait_send(), True)
    each_a(lambda d: copy_a(d, col, 2, far, far).wait_send(), False)
    each_a(lambda d: copy_a(-d, col, 0, near, near).wait_recv(), False)
    each_a(lambda d: copy_a(-d, other, 1, near, far).wait_recv(), True)
    each_a(lambda d: copy_a(-d, col, 2, far, far).wait_recv(), False)
    hand_act = pltpu.make_async_copy(act_win, act_hbm, load_sem.at[0])
    hand_act.start()
    hand_act.wait()


def excite(slabs, states, cond, tension, fiber, disp):
    _, depth, rows, width = states.shape
    tiles = rows // TILE
    full = rows // 4 + TILE
    across = cond.shape[3]
    vmem = pl.BlockSpec(memory_space=pltpu.VMEM)
    hbm = pl.BlockSpec(memory_space=pltpu.HBM)
    window = (2 * REACH + 1, full, across)
    shifts = (3, 2 * REACH - 1, full, across)
    pulls = (6, 2 * REACH + 1, full, across)
    dma = pltpu.SemaphoreType.DMA
    return pl.pallas_call(
        functools.partial(excite_kernel, slabs),
        out_shape=(
            jax.ShapeDtypeStruct(states.shape, F32),
            jax.ShapeDtypeStruct(tension.shape, F32),
            jax.ShapeDtypeStruct(window, F32),
            jax.ShapeDtypeStruct(shifts, F32),
            jax.ShapeDtypeStruct(pulls, F32),
        ),
        in_specs=[hbm, hbm, hbm, hbm, hbm],
        out_specs=(hbm, vmem, hbm, hbm, hbm),
        scratch_shapes=[
            pltpu.VMEM((SUB + 1, depth + 2, rows + 2 * TILE, width), F32),
            pltpu.VMEM(states.shape, F32),
            pltpu.VMEM(cond.shape, F32),
            pltpu.VMEM(tension.shape, F32),
            pltpu.VMEM((7, rows, width), F32),
            pltpu.VMEM((TILE, width), F32),
            pltpu.VMEM(window, F32),
            pltpu.VMEM((2 * RADIUS + 1, 4, full, across), F32),
            pltpu.VMEM(fiber.shape, jnp.int32),
            pltpu.VMEM((9, *window), F32),
            pltpu.VMEM(shifts, F32),
            pltpu.VMEM(pulls, F32),
            pltpu.VMEM((width // 256, 4 * TILE, 128), F32),
            dma((6,)),
            dma((tiles,)),
            dma((SUB, 2, tiles)),
            dma((SUB, 2, tiles)),
            dma((SUB, 2)),
            dma((SUB, 2)),
            dma((SUB,)),
            dma((SUB,)),
            dma((2 * REACH + 1, 3)),
            dma((2 * REACH + 1, 3)),
            dma((1 + len(ALONG) + len(BEYOND),)),
            dma((2 * RADIUS + 1,)),
            dma((2,)),
            pltpu.VMEM((SUB, rows, width), F32),
            dma((SUB, tiles)),
            dma((SUB, tiles)),
        ],
        compiler_params=pltpu.CompilerParams(
            collective_id=0, has_side_effects=True, vmem_limit_bytes=61 << 20
        ),
        cost_estimate=pl.CostEstimate(
            flops=200_000_000, bytes_accessed=16 << 20, transcendentals=6_000_000
        ),
        name="excite",
    )(states, cond, tension, fiber, disp)


def mech_kernel(
    slabs, active, shifted, pull, ten_in, states_in,
    disp_out, cond_out, ten_out, states_out, stress, moved, held, sem,
):
    slab = lax.axis_index("slab")
    first = lax.axis_index("col") == 0
    rows, width = active.shape[1:]
    half = rows - TILE
    fetch = pltpu.make_async_copy(states_in, held, sem.at[0])
    hand_on = pltpu.make_async_copy(held, states_out, sem.at[1])
    fetch.start()
    ten_out[...] = ten_in[...]
    mech = Stencils(rows, width)

    def inside(j):
        zz = slab + j - REACH
        return (zz >= 0) & (zz < slabs)

    def tense(j, c):
        for a in range(3):
            t = active[j] * pull[3 + a, j]
            for i in range(3):
                stress[3 * a + i, j] = t * pull[i, j]
        return c

    def move(field):
        def body(j, c):
            ok = inside(j)
            for i in range(3):
                force = mech.force(lambda n, d: stress[n, j + d], i)
                moved[i, j] = jnp.where(ok, field(i, j) + (MECH_RATE / 128.0) * force, 0.0)
            return c

        return body

    def strain(j, c):
        ok = inside(j)
        f = mech.deformation(lambda i, d: moved[i, j + d])
        pieces = first_piola(f, active[j], [pull[3 + a, j] for a in range(3)])
        for n in range(9):
            stress[n, j] = jnp.where(ok, pieces[n], 0.0)
        return c

    lax.fori_loop(0, 2 * REACH + 1, tense, 0)
    lax.fori_loop(1, 2 * REACH, move(lambda i, j: shifted[i, j - 1]), 0)
    fetch.wait()
    hand_on.start()
    lax.fori_loop(2, 2 * REACH - 1, strain, 0)
    lax.fori_loop(3, 2 * REACH - 2, move(lambda i, j: moved[i, j]), 0)

    comps = metric(
        mech.deformation(lambda i, d: moved[i, REACH + d]),
        [pull[3 + a, REACH] for a in range(3)],
    )
    for i in range(3):
        whole = moved[i, REACH]
        disp_out[i, 0] = jnp.where(first, whole[:half], whole[TILE:])
    for n in range(6):
        cond_out[n, 0] = jnp.where(first, comps[n][:half], comps[n][TILE:])
    hand_on.wait()


def mechanics(slabs, active, shifted, pull, tension, states):
    _, full, width = active.shape
    rows = full - TILE
    vmem = pl.BlockSpec(memory_space=pltpu.VMEM)
    hbm = pl.BlockSpec(memory_space=pltpu.HBM)
    return pl.pallas_call(
        functools.partial(mech_kernel, slabs),
        out_shape=(
            jax.ShapeDtypeStruct((3, 1, rows, width), F32),
            jax.ShapeDtypeStruct((6, 1, rows, width), F32),
            jax.ShapeDtypeStruct(tension.shape, F32),
            jax.ShapeDtypeStruct(states.shape, F32),
        ),
        in_specs=[vmem, vmem, vmem, vmem, hbm],
        out_specs=(vmem, vmem, vmem, hbm),
        scratch_shapes=[
            pltpu.VMEM((9, 2 * REACH + 1, full, width), F32),
            pltpu.VMEM((3, 2 * REACH + 1, full, width), F32),
            pltpu.VMEM(states.shape, F32),
            pltpu.SemaphoreType.DMA((2,)),
        ],
        compiler_params=pltpu.CompilerParams(vmem_limit_bytes=61 << 20),
        name="mechanics",
    )(active, shifted, pull, tension, states)


def on_device(slabs, states, cond, tension, fiber, disp):
    states_next, tension_next, active, shifted, pull = excite(
        slabs, states, cond, tension, fiber, disp
    )
    disp_next, cond_next, tension_next, states_next = mechanics(
        slabs, active, shifted, pull, tension_next, states_next
    )
    return states_next, tension_next, disp_next, cond_next


def solution(mesh):
    wide = P(None, ("grp", "slab"), "col", None)
    flat = P(("grp", "slab"), "col", None)
    return jax.shard_map(
        functools.partial(on_device, mesh.shape["slab"]),
        mesh=mesh,
        in_specs=(wide, wide, flat, flat, wide),
        out_specs=(wide, flat, wide, wide),
        check_vma=False,
    )
```

```python
import functools

import jax
import jax.numpy as jnp
import numpy as np
from jax import lax
from jax.experimental import pallas as pl
from jax.experimental.pallas import tpu as pltpu
from jax.sharding import PartitionSpec as P

SUB = 4
MECH_STEPS = 2
NFIB = 64
STEP_TIME = 0.05
MECH_RATE = 0.15
SIGMA_LONG = 0.16
SIGMA_TRANS = 0.04
PAIRS = ((0, 0), (1, 1), (2, 2), (0, 1), (0, 2), (1, 2))
MESH = pl.DeviceIdType.MESH
HI = lax.Precision.HIGHEST
F32 = jnp.float32
BF16 = jnp.bfloat16
TILE = 8
LANES = 128
CHUNK = 256
RADIUS = 2 * MECH_STEPS + 1
REACH = RADIUS - 1
ALONG = (-4, -2, 2, 4)
BEYOND = (-6, -4, -2, 2, 4, 6)
PEERS = (-6, -4, -3, -2, -1, 0, 1, 2, 3, 4, 6)
JOIN = 10
LAST = 4 * REACH
LAG = 4
HOLD = 2


def ionic(u, v, w, s):
    per = 2.0 / STEP_TIME
    steep = 50.0 * u
    th_v = jnp.tanh(steep - 50.0 * 0.3)
    th_w = jnp.tanh(steep - 50.0 * 0.13)
    th_o = jnp.tanh(steep - 50.0 * 0.006)
    th_m = jnp.tanh(65.0 * u - 65.0 * 0.03)
    th_s = jnp.tanh(2.0458 * u - 2.0458 * 0.65)
    th_r = jnp.tanh(2.0994 * u - 2.0994 * 0.9087)
    hv2 = 1.0 + th_v
    nv2 = 1.0 - th_v
    hw2 = 1.0 + th_w
    nw2 = 1.0 - th_w
    no = 0.5 - 0.5 * th_o
    rate_v = 1.0 / (605.0 * per + (545.0 * per) * th_o)
    rate_w = 1.0 / (37.5 * per - (22.5 * per) * th_m)
    rate_so = 1.0 / (15.5069 * per - (14.5112 * per) * th_s)
    rate_s = 1.0 / (9.3671 * per + (6.6329 * per) * th_w)
    rate_o = 1.0 / (203.0 * per - (197.0 * per) * th_o)
    lead = STEP_TIME / 0.22
    open_v = hv2 * v
    w_inf = no * (0.06 - u * (1.0 / 0.07)) + 0.94
    du = (
        open_v * ((u - 0.3) * (1.55 * lead - lead * u))
        + hw2 * ((w * s) * (STEP_TIME / 3.775) - rate_so)
        - (u * nw2) * rate_o
    )
    v2 = v - open_v * (STEP_TIME / 2.9012) + (nv2 * rate_v) * (no - v)
    w2 = w - (hw2 * w) * (STEP_TIME / 400.0) + (nw2 * rate_w) * (w_inf - w)
    s2 = s + ((1.0 + th_r) - 2.0 * s) * rate_s
    return du, v2, w2, s2


def iota2(shape, dim):
    return lax.broadcasted_iota(jnp.int32, shape, dim)


def first_piola(f, active=None, fdir=None):
    second = {}
    for a in range(3):
        for b in range(a, 3):
            right = f[0][a] * f[0][b] + f[1][a] * f[1][b] + f[2][a] * f[2][b]
            second[a, b] = 0.5 * (right - (1.0 if a == b else 0.0))
    trace = second[0, 0] + second[1, 1] + second[2, 2]
    for a in range(3):
        if active is not None:
            scaled = 0.5 * active * fdir[a]
            for b in range(a, 3):
                second[a, b] = second[a, b] + scaled * fdir[b]
        second[a, a] = second[a, a] + trace
    for a in range(3):
        for b in range(a):
            second[a, b] = second[b, a]
    return [
        f[i][0] * second[0, a] + f[i][1] * second[1, a] + f[i][2] * second[2, a]
        for a in range(3)
        for i in range(3)
    ]


def metric(f, fdir):
    cof = [[None] * 3 for _ in range(3)]
    for i in range(3):
        for j in range(3):
            cof[i][j] = (
                f[(i + 1) % 3][(j + 1) % 3] * f[(i + 2) % 3][(j + 2) % 3]
                - f[(i + 1) % 3][(j + 2) % 3] * f[(i + 2) % 3][(j + 1) % 3]
            )
    det = f[0][0] * cof[0][0] + f[0][1] * cof[0][1] + f[0][2] * cof[0][2]
    scale = 1.0 / det
    inverse = [[cof[i][j] * scale for i in range(3)] for j in range(3)]
    g = [inverse[a][0] * fdir[0] + inverse[a][1] * fdir[1] + inverse[a][2] * fdir[2] for a in range(3)]
    comps = []
    for a, b in PAIRS:
        inner = (
            inverse[a][0] * inverse[b][0]
            + inverse[a][1] * inverse[b][1]
            + inverse[a][2] * inverse[b][2]
        )
        comps.append(SIGMA_TRANS * inner + (SIGMA_LONG - SIGMA_TRANS) * (g[a] * g[b]))
    return comps


class Stencils:
    def __init__(self, rows, width):
        self.rows, self.width = rows, width
        self.lane = iota2((rows, LANES), 1)
        self.line = iota2((TILE, width), 0)

    def left(self, f):
        parts, before = [], 0.0
        for x in range(0, self.width, LANES):
            here = f[:, x : x + LANES]
            parts.append(pltpu.roll(jnp.where(self.lane == LANES - 1, before, here), 1, 1))
            before = here
        return jnp.concatenate(parts, axis=1)

    def right(self, f):
        parts, after = [], 0.0
        for x in reversed(range(0, self.width, LANES)):
            here = f[:, x : x + LANES]
            parts.append(pltpu.roll(jnp.where(self.lane == 0, after, here), LANES - 1, 1))
            after = here
        return jnp.concatenate(parts[::-1], axis=1)

    def south(self, f):
        parts, before = [], 0.0
        for y in range(0, self.rows, TILE):
            here = f[y : y + TILE]
            parts.append(pltpu.roll(jnp.where(self.line == TILE - 1, before, here), 1, 0))
            before = here
        return jnp.concatenate(parts, axis=0)

    def north(self, f):
        parts, after = [], 0.0
        for y in reversed(range(0, self.rows, TILE)):
            here = f[y : y + TILE]
            parts.append(pltpu.roll(jnp.where(self.line == 0, after, here), TILE - 1, 0))
            after = here
        return jnp.concatenate(parts[::-1], axis=0)


    def sx(self, f):
        return self.left(f) + self.right(f) + 6.0 * f

    def dx(self, f):
        return self.right(f) - self.left(f)

    def sy(self, f):
        return self.south(f) + self.north(f) + 6.0 * f

    def dy(self, f):
        return self.north(f) - self.south(f)

    def deformation(self, field):
        f = []
        for i in range(3):
            low, mid, high = field(i, -1), field(i, 0), field(i, 1)
            zs = low + high + 6.0 * mid
            zd = high - low
            grads = [self.sy(self.sx(zd)), self.dy(self.sx(zs)), self.sy(self.dx(zs))]
            f.append([(1.0 / 128.0) * g for g in grads])
            f[i][i] = f[i][i] + 1.0
        return f

    def force(self, stress, i):
        zd = stress(i, 1) - stress(i, -1)
        ys = stress(3 + i, -1) + stress(3 + i, 1) + 6.0 * stress(3 + i, 0)
        xs = stress(6 + i, -1) + stress(6 + i, 1) + 6.0 * stress(6 + i, 0)
        return self.sy(self.sx(zd) + self.dx(xs)) + self.dy(self.sx(ys))


def sine(x, terms=6):
    y = x * x
    c = 1.0
    for n in range(2 * terms, 0, -2):
        c = 1.0 - y * (1.0 / (n * (n + 1))) * c
    return x * c


def cosine(x):
    y = x * x
    c = 1.0
    for n in (13, 11, 9, 7, 5, 3, 1):
        c = 1.0 - y * (1.0 / (n * (n + 1))) * c
    return c


def directions(index):
    theta = -1.0 + index * (2.0 / (NFIB - 1))
    triple = 3.0 * index
    turns = jnp.floor(triple * (0.5 / np.pi) + 0.5)
    triple = (triple - turns * 6.28125) - turns * (2.0 * np.pi - 6.28125)
    tilt = 0.3 * sine(triple, 10)
    flat = cosine(tilt)
    return [sine(tilt), flat * sine(theta), flat * cosine(theta)]


def halves(x):
    high = x.astype(BF16)
    return high, (x - high.astype(F32)).astype(BF16)


def excite_kernel(
    slabs, states, cond_hbm, ten_hbm, fib_hbm, disp_hbm,
    out_hbm, ten_out, act_hbm, shift_hbm, pull_hbm,
    ubuf, out, cond, tension, coeff, dif, act_win, zeros, fix_win, fiber, passive, shifted, pull, pooled,
    load_sem, store_sem, sz, rz, sc, rc, sy, ry, sa, ra, sf, rf, sg, relay, sv, rv,
):
    grp = lax.axis_index("grp")
    slab = lax.axis_index("slab")
    col = lax.axis_index("col")
    other = 1 - col
    depth, rows, width = out.shape[1:]
    tiles = rows // TILE
    has_up = slab < slabs - 1
    has_dn = slab > 0
    edge_src = rows - (rows - TILE) * col
    edge_dst = (rows + TILE) * col

    load_u = pltpu.make_async_copy(
        states.at[0], ubuf.at[0, pl.ds(1, depth), pl.ds(TILE, rows), :], load_sem.at[0]
    )
    load_g = pltpu.make_async_copy(
        states.at[pl.ds(1, 3)], out.at[pl.ds(1, 3)], load_sem.at[1]
    )
    load_c = pltpu.make_async_copy(cond_hbm, cond, load_sem.at[2])
    load_t = pltpu.make_async_copy(ten_hbm, tension, load_sem.at[3])
    load_u.start()
    load_c.start()
    load_g.start()
    load_t.start()
    half = rows // 4
    span = half + TILE
    own = pl.ds(pl.multiple_of(TILE * col, TILE), half)
    near = pl.ds(TILE, TILE)
    far = pl.ds(pl.multiple_of(2 * TILE * col, TILE), TILE)
    load_d = pltpu.make_async_copy(
        disp_hbm.at[:, 0], fix_win.at[RADIUS, pl.ds(0, 3), own, :], load_sem.at[4]
    )
    load_f = pltpu.make_async_copy(fib_hbm, fiber, load_sem.at[5])
    load_d.start()
    load_f.start()

    barrier = pltpu.get_barrier_semaphore()

    def greet(where):
        pl.semaphore_signal(barrier, inc=1, device_id=where, device_id_type=MESH)

    def there(d):
        return (slab + d >= 0) & (slab + d < slabs)

    peers = 0
    for d in PEERS:
        valid = there(d)
        wide = abs(d) <= REACH
        count = (0 if d == 0 else 1) + (1 if wide else 0)
        peers = peers + count * valid.astype(jnp.int32)

        @pl.when(valid)
        def _(d=d, wide=wide):
            if wide:
                greet((grp, slab + d, other))
            if d != 0:
                greet((grp, slab + d, col))

    zeros[...] = jnp.zeros(zeros.shape, F32)

    def blank_a(d):
        return pltpu.make_async_copy(zeros, act_hbm.at[d + REACH], ra.at[d + REACH, 0])

    for d in range(-RADIUS, RADIUS + 1):

        @pl.when(jnp.logical_not(there(d)))
        def _(d=d):
            fix_win[d + RADIUS] = jnp.zeros(fix_win.shape[1:], F32)
            if abs(d) <= REACH:
                blank_a(d).start()

    blank = jnp.zeros((TILE, width), F32)

    def clear_y(n, c):
        ubuf[n // (depth + 2), n % (depth + 2), pl.ds(pl.multiple_of(edge_dst, TILE), TILE), :] = blank
        return c

    lax.fori_loop(0, SUB * (depth + 2), clear_y, 0)

    def clear_z(layer):
        per = rows // TILE + 2

        def body(n, c):
            ubuf[n // per, layer, pl.ds(pl.multiple_of((n % per) * TILE, TILE), TILE), :] = blank
            return c

        lax.fori_loop(0, SUB * per, body, 0)

    @pl.when(slab == 0)
    def _():
        clear_z(0)

    @pl.when(slab == slabs - 1)
    def _():
        clear_z(depth + 1)

    def row_of(step):
        return jnp.where(col == 1, step, tiles - 1 - step)

    def copy_z(slot, way, step):
        at = pl.ds(pl.multiple_of(TILE + TILE * row_of(step), TILE), TILE)
        src = depth if way == 0 else 1
        dst = 0 if way == 0 else depth + 1
        to = slab + 1 if way == 0 else slab - 1
        return pltpu.make_async_remote_copy(
            src_ref=ubuf.at[slot, src, at, :],
            dst_ref=ubuf.at[slot, dst, at, :],
            send_sem=sz.at[slot, way, step],
            recv_sem=rz.at[slot, way, step],
            device_id=(grp, to, col),
            device_id_type=MESH,
        )

    def carried(step, count):
        return lax.rem((step + 1) * count, tiles) < count

    beside = 1 - 2 * lax.rem(slab, 2)
    chips = slabs // 2
    upper = tiles * (chips - 1 - slab // 2) // chips
    lower = tiles * (slab // 2) // chips
    even = beside == 1
    mine = jnp.where(even, lower, upper)
    others = jnp.where(even, upper, lower)
    onward = 1 - lax.rem(slab + 1, 2)

    def copy_via(slot, way, step):
        at = pl.ds(pl.multiple_of(TILE + TILE * row_of(step), TILE), TILE)
        to = pl.ds(pl.multiple_of(TILE * row_of(step), TILE), TILE)
        return pltpu.make_async_remote_copy(
            src_ref=ubuf.at[slot, depth if way == 0 else 1, at, :],
            dst_ref=relay.at[slot, to, :],
            send_sem=sz.at[slot, way, step],
            recv_sem=rv.at[slot, step],
            device_id=(grp, slab + beside, col),
            device_id_type=MESH,
        )

    def copy_on(slot, step):
        at = pl.ds(pl.multiple_of(TILE * row_of(step), TILE), TILE)
        to = pl.ds(pl.multiple_of(TILE + TILE * row_of(step), TILE), TILE)
        return pltpu.make_async_remote_copy(
            src_ref=relay.at[slot, at, :],
            dst_ref=ubuf.at[slot, onward * (depth + 1), to, :],
            send_sem=sv.at[slot, step],
            recv_sem=rz.at[slot, onward, step],
            device_id=(grp, slab + 2 * beside, col),
            device_id_type=MESH,
        )

    def hand_on(n):
        @pl.when((n < SUB * tiles) & carried(n % tiles, others))
        def _():
            copy_via(n // tiles, 0, n % tiles).wait_recv()
            copy_on(n // tiles, n % tiles).start()

    def copy_c(slot, way):
        at = depth + 1 if way == 0 else 0
        return pltpu.make_async_remote_copy(
            src_ref=ubuf.at[slot, at, pl.ds(pl.multiple_of(edge_src, TILE), TILE), :],
            dst_ref=ubuf.at[slot, at, pl.ds(pl.multiple_of(edge_dst, TILE), TILE), :],
            send_sem=sc.at[slot, way],
            recv_sem=rc.at[slot, way],
            device_id=(grp, slab, other),
            device_id_type=MESH,
        )

    def copy_y(slot):
        return pltpu.make_async_remote_copy(
            src_ref=ubuf.at[slot, pl.ds(1, depth), pl.ds(pl.multiple_of(edge_src, TILE), TILE), :],
            dst_ref=ubuf.at[slot, pl.ds(1, depth), pl.ds(pl.multiple_of(edge_dst, TILE), TILE), :],
            send_sem=sy.at[slot],
            recv_sem=ry.at[slot],
            device_id=(grp, slab, other),
            device_id_type=MESH,
        )

    def both(do_up, do_dn):
        pl.when(has_up)(do_up)
        pl.when(has_dn)(do_dn)

    def send_z(n, by_partner):
        slot = n // tiles
        step = n % tiles
        via = carried(step, mine)

        def send(way):
            through = via & (jnp.logical_not(even) if way == 0 else even)
            if by_partner:
                pl.when(through)(lambda: copy_via(slot, way, step).start())
            else:
                pl.when(jnp.logical_not(through))(lambda: copy_z(slot, way, step).start())

        @pl.when(n < SUB * tiles)
        def _():
            both(lambda: send(0), lambda: send(1))

    def send_c(slot):
        both(lambda: copy_c(slot, 0).start(), lambda: copy_c(slot, 1).start())

    def recv_z(slot, step):
        both(lambda: copy_z(slot, 1, step).wait_recv(), lambda: copy_z(slot, 0, step).wait_recv())

    def recv_c(slot):
        both(lambda: copy_c(slot, 0).wait_recv(), lambda: copy_c(slot, 1).wait_recv())

    def copy_f(source, d, n):
        slot = RADIUS + source - d
        return pltpu.make_async_remote_copy(
            src_ref=fix_win.at[RADIUS + source, :, own, :],
            dst_ref=fix_win.at[slot, :, own, :],
            send_sem=sf.at[n],
            recv_sem=rf.at[slot],
            device_id=(grp, slab + d, col),
            device_id_type=MESH,
        )

    def come_f(e):
        return pltpu.make_async_remote_copy(
            src_ref=fix_win.at[RADIUS, :, own, :],
            dst_ref=fix_win.at[RADIUS + e, :, own, :],
            send_sem=sf.at[0],
            recv_sem=rf.at[RADIUS + e],
            device_id=(grp, slab + e, col),
            device_id_type=MESH,
        )

    def share_f(whose):
        return pltpu.make_async_remote_copy(
            src_ref=fix_win.at[:, :, near, :],
            dst_ref=fix_win.at[:, :, pl.ds(pl.multiple_of(2 * TILE * whose, TILE), TILE), :],
            send_sem=sg.at[0],
            recv_sem=sg.at[1],
            device_id=(grp, slab, other),
            device_id_type=MESH,
        )

    def forward_f(act):
        for n, d in enumerate(BEYOND):
            ok = there(d) & (jnp.abs(d - beside) <= RADIUS)
            pl.when(ok)(lambda n=n, d=d: act(n, d))

    def relay_f(n, d):
        return copy_f(beside, d, 1 + len(ALONG) + n)

    pl.semaphore_wait(barrier, peers)

    load_u.wait()
    send_z(0, True)
    send_z(0, False)
    copy_y(0).start()
    send_z(1, True)
    send_z(1, False)
    load_d.wait()
    load_f.wait()
    fix_win[RADIUS, 3, own, :] = fiber[0].astype(F32)
    copy_f(0, beside, 0).start()
    for n, d in enumerate(ALONG):
        pl.when(there(d))(lambda n=n, d=d: copy_f(0, d, 1 + n).start())

    def initial(step, c):
        send_z(step, True)
        pl.when(step < tiles - HOLD)(lambda: send_z(step, False))
        return c

    lax.fori_loop(2, tiles, initial, 0)
    load_c.wait()

    spread_x = (iota2((256, 512), 0) % 128 == iota2((256, 512), 1) // 4).astype(BF16)
    spread_y = (iota2((rows, rows // 4), 0) // 4 == iota2((rows, rows // 4), 1)).astype(BF16)
    for c in range(6):
        tall = [
            jnp.dot(spread_y, part, preferred_element_type=F32).astype(BF16)
            for part in halves(cond[c, 0])
        ]
        for h in range(width // 512):
            part = jnp.concatenate([t[:, h * 128 : (h + 1) * 128] for t in tall], axis=1)
            part = jnp.dot(part, spread_x, preferred_element_type=F32)
            coeff[c, :, h * 512 : (h + 1) * 512] = part if c < 3 else 0.5 * part

    def centre_weight(t, c):
        at = pl.ds(pl.multiple_of(TILE * t, TILE), TILE)
        coeff[6, at, :] = 1.0 - 2.0 * (coeff[0, at, :] + coeff[1, at, :] + coeff[2, at, :])
        return c

    lax.fori_loop(0, tiles, centre_weight, 0)

    load_g.wait()
    load_t.wait()

    lane = iota2((TILE, width), 1)

    def left(f):
        return jnp.where(lane == 0, 0.0, pltpu.roll(f, 1, 1))

    def right(f):
        return jnp.where(lane == width - 1, 0.0, pltpu.roll(f, width - 1, 1))

    line = iota2((TILE, width), 0)

    def north_south(tall):
        here = tall[TILE : 2 * TILE]
        return (
            pltpu.roll(jnp.where(line == 0, tall[2 * TILE :], here), TILE - 1, 0),
            pltpu.roll(jnp.where(line == TILE - 1, tall[:TILE], here), 1, 0),
        )

    def layer(k, z, r):
        base = pl.multiple_of(TILE * r, TILE)
        here = pl.ds(base, TILE)
        tall = pl.ds(base, 3 * TILE)
        below = ubuf[k, z, tall, :]
        mid = ubuf[k, z + 1, tall, :]
        above = ubuf[k, z + 2, tall, :]
        odd = above - below
        centre = mid[TILE : 2 * TILE]
        odd0 = odd[TILE : 2 * TILE]
        north, south = north_south(mid)
        odd_north, odd_south = north_south(odd)
        slope = north - south
        total = coeff[6, here, :] * centre
        total = total + coeff[0, here, :] * (above[TILE : 2 * TILE] + below[TILE : 2 * TILE])
        total = total + coeff[1, here, :] * (north + south)
        total = total + coeff[2, here, :] * (right(centre) + left(centre))
        total = total + coeff[3, here, :] * (odd_north - odd_south)
        total = total + coeff[4, here, :] * (right(odd0) - left(odd0))
        total = total + coeff[5, here, :] * (right(slope) - left(slope))
        dif[...] = total
        up = pl.ds(pl.multiple_of(base + TILE, TILE), TILE)
        for x in range(0, width, CHUNK):
            xs = pl.ds(x, CHUNK)
            du, v2, w2, s2 = ionic(
                ubuf[k, z + 1, up, xs], out[1, z, here, xs], out[2, z, here, xs],
                out[3, z, here, xs],
            )
            u2 = dif[:, xs] + du
            ubuf[k + 1, z + 1, up, xs] = u2
            out[0, z, here, xs] = u2
            out[1, z, here, xs] = v2
            out[2, z, here, xs] = w2
            out[3, z, here, xs] = s2

    def leave(step):
        at = pl.ds(pl.multiple_of(TILE * row_of(step), TILE), TILE)
        return pltpu.make_async_copy(
            out.at[:, :, at, :], out_hbm.at[:, :, at, :], store_sem.at[step]
        )

    pair_x = (iota2((256, 128), 0) // 2 == iota2((256, 128), 1)).astype(F32)
    pair_2 = (iota2((512, 128), 0) % 256 // 2 == iota2((512, 128), 1)).astype(BF16)
    pair_y2 = (iota2((half, 2 * half), 0) == iota2((half, 2 * half), 1) // 2).astype(F32)

    def pool_lanes(rows_in, weights, size, chunk):
        parts = halves(rows_in)
        for h in range(width // chunk):
            both_halves = jnp.concatenate(
                [part[:, h * chunk : (h + 1) * chunk] for part in parts], axis=1
            )
            pooled[h, 0:size] = jnp.dot(both_halves, weights, preferred_element_type=F32)

    def tense(p):
        fine = pl.ds(pl.multiple_of(2 * TILE * p, 2 * TILE), 2 * TILE)
        wide = pl.ds(pl.multiple_of(TILE * p, TILE), TILE)
        sums = []
        for q in range(depth // 2):
            layers = out[0, 2 * q, fine, :] + out[0, 2 * q + 1, fine, :]
            sums.append(layers + pltpu.roll(layers, 2 * TILE - 1, 0))
        pool_lanes(0.125 * jnp.concatenate(sums, axis=0), pair_2, TILE * depth, 256)
        for h in range(width // 256):
            xo = slice(h * 128, (h + 1) * 128)
            for q in range(depth // 2):
                mean = pooled[h, pl.ds(2 * TILE * q, TILE, 2), :]
                before = tension[q, wide, xo]
                ten_out[q, wide, xo] = before + 0.5 * (mean - before)

    pool_x = (iota2((1024, 128), 0) % 512 // 4 == iota2((1024, 128), 1)).astype(BF16)

    def activate(part, lines):
        fine = pl.ds(pl.multiple_of(4 * TILE * part, 4 * TILE), 4 * TILE)
        layers = out[0, 0, fine, :]
        for z in range(1, depth):
            layers = layers + out[0, z, fine, :]
        layers = layers + pltpu.roll(layers, 4 * TILE - 1, 0)
        layers = layers + pltpu.roll(layers, 4 * TILE - 2, 0)
        pool_lanes((0.5 / (16 * depth)) * layers, pool_x, 4 * TILE, 512)
        for h in range(width // 512):
            xo = slice(h * 128, (h + 1) * 128)
            act_win[lines, xo] = act_win[lines, xo] + pooled[h, pl.ds(0, TILE, 4), :]

    def copy_a(d, to, kind, lines, at):
        return pltpu.make_async_remote_copy(
            src_ref=act_win.at[lines, :],
            dst_ref=act_hbm.at[REACH - d, at, :],
            send_sem=sa.at[d + REACH, kind],
            recv_sem=ra.at[REACH - d, kind],
            device_id=(grp, slab + d, to),
            device_id_type=MESH,
        )

    def keep_a(kind, lines):
        return pltpu.make_async_copy(
            act_win.at[lines, :], act_hbm.at[REACH, lines, :], sa.at[REACH, kind]
        )

    def each_a(act, centre):
        for d in sorted(range(-REACH, REACH + 1), key=lambda d: -abs(d)):
            if d != 0 or centre:
                pl.when(there(d))(lambda d=d: act(d))

    mech = Stencils(span, fix_win.shape[3])

    def inside(j):
        return there(j - RADIUS)

    def prepare(j):
        ok = inside(j)
        f = mech.deformation(lambda i, d: fix_win[j + d, i])
        fdir = directions(fix_win[j, 3])
        pieces = first_piola(f)
        for n in range(9):
            passive[n, j - 1] = jnp.where(ok, pieces[n], 0.0)
        for i in range(3):
            g = 0.5 * (f[i][0] * fdir[0] + f[i][1] * fdir[1] + f[i][2] * fdir[2])
            pull[i, j - 1] = jnp.where(ok, g, 0.0)
            pull[3 + i, j - 1] = fdir[i]

    def shift(j):
        ok = inside(j)
        for i in range(3):
            force = mech.force(lambda n, d: passive[n, j - 1 + d], i)
            moved = fix_win[j, i] + (MECH_RATE / 128.0) * force
            shifted[i, j - 2] = jnp.where(ok, moved, 0.0)

    hand_shift = pltpu.make_async_copy(shifted, shift_hbm, load_sem.at[0])
    hand_pull = pltpu.make_async_copy(pull, pull_hbm, load_sem.at[1])

    for h in range(width // 512):
        xs = slice(h * 256, (h + 1) * 256)
        layers = tension[0, :, xs] + tension[1, :, xs]
        mean = jnp.dot(layers, pair_x, precision=HI, preferred_element_type=F32)
        mean = 0.0625 * jnp.dot(pair_y2, mean, precision=HI, preferred_element_type=F32)
        act_win[own, h * 128 : (h + 1) * 128] = mean

    def within(n):
        k = n // tiles
        r = row_of(n % tiles)

        def inner(m, c):
            layer(k, m, r)
            return c

        lax.fori_loop(1, depth - 1, inner, 0)

    recv_z(0, 0)
    send_c(0)
    copy_y(0).wait_recv()
    within(0)

    def chunk(n, c):
        k = n // tiles
        step = n % tiles
        r = row_of(step)

        @pl.when(n < LAG - 1)
        def _():
            hand_on(2 * n + 1)
            hand_on(2 * n + 2)

        pl.when(n >= LAG - 1)(lambda: hand_on(n + LAG))

        @pl.when(n == tiles // 2)
        def _():
            come_f(beside).wait_recv()

        for far_by in (2, 4, 6):

            @pl.when(n == tiles // 2 + far_by // 2 - 1)
            def _(far_by=far_by):
                forward_f(lambda n, d: relay_f(n, d).start() if abs(d) == far_by else None)

        @pl.when(n == JOIN)
        def _():
            for d in range(-RADIUS, RADIUS + 1):
                if d != 0:
                    arrives = there(d) if d % 2 == 0 else there(d) & (beside != d)
                    pl.when(arrives)(lambda d=d: come_f(d).wait_recv())
            share_f(col).start()

        @pl.when(n == JOIN + 2)
        def _():
            share_f(col).wait_recv()

        @pl.when(step < tiles - 1)
        def _():
            recv_z(k, step + 1)

        @pl.when(step == 0)
        def _():
            recv_c(k)

        def outer(m, c):
            layer(k, m * (depth - 1), r)
            return c

        lax.fori_loop(0, 2, outer, 0)

        send_z(n + tiles, True)
        send_z(n + tiles - HOLD, False)

        @pl.when((k < SUB - 1) & (step == 0))
        def _():
            copy_y(k + 1).start()

        @pl.when((k < SUB - 1) & (step == tiles - 1))
        def _():
            recv_z(k + 1, 0)
            send_c(k + 1)
            copy_y(k + 1).wait_recv()

        @pl.when(n < SUB * tiles - 1)
        def _():
            within(n + 1)

        turn = n - JOIN - 2
        stress_turn = (turn < 2) | (turn % 2 == 0)

        @pl.when((turn >= 0) & (turn < LAST) & stress_turn)
        def _():
            prepare(jnp.where(turn < 2, turn + 1, turn // 2 + 2))

        @pl.when((turn >= 3) & (turn < LAST) & jnp.logical_not(stress_turn))
        def _():
            shift((turn + 1) // 2)

        @pl.when(turn == LAST)
        def _():
            hand_shift.start()
            hand_pull.start()

        @pl.when(k == SUB - 1)
        def _():
            leave(step).start()

        @pl.when(n == SUB * tiles - 1 - tiles // 2)
        def _():
            activate(other, near)
            each_a(lambda d: copy_a(d, col, 0, near, near).start(), False)
            each_a(lambda d: copy_a(d, other, 1, near, far).start(), True)
            keep_a(0, near).start()

        @pl.when((k == SUB - 1) & (step % 2 == 1) & (step < tiles - 1))
        def _():
            tense(r // 2)

        return c

    lax.fori_loop(0, SUB * tiles, chunk, 0)

    activate(col, far)
    each_a(lambda d: copy_a(d, col, 2, far, far).start(), False)
    keep_a(2, far).start()
    tense(row_of(tiles - 1) // 2)
    share_f(col).wait_send()
    copy_f(0, beside, 0).wait_send()
    for n, d in enumerate(ALONG):
        pl.when(there(d))(lambda n=n, d=d: copy_f(0, d, 1 + n).wait_send())
    forward_f(lambda n, d: relay_f(n, d).wait_send())
    hand_shift.wait()
    hand_pull.wait()
    copy_y(0).wait_send()

    def drain(slot, c):
        both(lambda: copy_c(slot, 0).wait_send(), lambda: copy_c(slot, 1).wait_send())

        @pl.when(slot > 0)
        def _():
            copy_y(slot).wait_send()

        def tile(step, c):
            both(
                lambda: copy_z(slot, 0, step).wait_send(),
                lambda: copy_z(slot, 1, step).wait_send(),
            )
            pl.when(carried(step, others))(lambda: copy_on(slot, step).wait_send())
            return c

        return lax.fori_loop(0, tiles, tile, c)

    lax.fori_loop(0, SUB, drain, 0)

    def left_all(step, c):
        leave(step).wait()
        return c

    lax.fori_loop(0, tiles, left_all, 0)
    each_a(lambda d: copy_a(d, col, 0, near, near).wait_send(), False)
    each_a(lambda d: copy_a(d, other, 1, near, far).wait_send(), True)
    each_a(lambda d: copy_a(d, col, 2, far, far).wait_send(), False)
    for d in range(-REACH, REACH + 1):
        pl.when(jnp.logical_not(there(d)))(lambda d=d: blank_a(d).wait())
    each_a(lambda d: copy_a(-d, col, 0, near, near).wait_recv(), False)
    each_a(lambda d: copy_a(-d, other, 1, near, far).wait_recv(), True)
    each_a(lambda d: copy_a(-d, col, 2, far, far).wait_recv(), False)
    keep_a(0, near).wait()
    keep_a(2, far).wait()


def excite(slabs, states, cond, tension, fiber, disp):
    _, depth, rows, width = states.shape
    tiles = rows // TILE
    full = rows // 4 + TILE
    across = cond.shape[3]
    vmem = pl.BlockSpec(memory_space=pltpu.VMEM)
    hbm = pl.BlockSpec(memory_space=pltpu.HBM)
    window = (2 * REACH + 1, full, across)
    shifts = (3, 2 * REACH - 1, full, across)
    pulls = (6, 2 * REACH + 1, full, across)
    dma = pltpu.SemaphoreType.DMA
    return pl.pallas_call(
        functools.partial(excite_kernel, slabs),
        out_shape=(
            jax.ShapeDtypeStruct(states.shape, F32),
            jax.ShapeDtypeStruct(tension.shape, F32),
            jax.ShapeDtypeStruct(window, F32),
            jax.ShapeDtypeStruct(shifts, F32),
            jax.ShapeDtypeStruct(pulls, F32),
        ),
        in_specs=[hbm, hbm, hbm, hbm, hbm],
        out_specs=(hbm, vmem, hbm, hbm, hbm),
        scratch_shapes=[
            pltpu.VMEM((SUB + 1, depth + 2, rows + 2 * TILE, width), F32),
            pltpu.VMEM(states.shape, F32),
            pltpu.VMEM(cond.shape, F32),
            pltpu.VMEM(tension.shape, F32),
            pltpu.VMEM((7, rows, width), F32),
            pltpu.VMEM((TILE, width), F32),
            pltpu.VMEM(window[1:], F32),
            pltpu.VMEM(window[1:], F32),
            pltpu.VMEM((2 * RADIUS + 1, 4, full, across), F32),
            pltpu.VMEM(fiber.shape, jnp.int32),
            pltpu.VMEM((9, *window), F32),
            pltpu.VMEM(shifts, F32),
            pltpu.VMEM(pulls, F32),
            pltpu.VMEM((width // 256, 4 * TILE, 128), F32),
            dma((6,)),
            dma((tiles,)),
            dma((SUB, 2, tiles)),
            dma((SUB, 2, tiles)),
            dma((SUB, 2)),
            dma((SUB, 2)),
            dma((SUB,)),
            dma((SUB,)),
            dma((2 * REACH + 1, 3)),
            dma((2 * REACH + 1, 3)),
            dma((1 + len(ALONG) + len(BEYOND),)),
            dma((2 * RADIUS + 1,)),
            dma((2,)),
            pltpu.VMEM((SUB, rows, width), F32),
            dma((SUB, tiles)),
            dma((SUB, tiles)),
        ],
        compiler_params=pltpu.CompilerParams(
            collective_id=0, has_side_effects=True, vmem_limit_bytes=61 << 20
        ),
        cost_estimate=pl.CostEstimate(
            flops=200_000_000, bytes_accessed=16 << 20, transcendentals=6_000_000
        ),
        name="excite",
    )(states, cond, tension, fiber, disp)


def mech_kernel(
    slabs, act_hbm, shift_hbm, pull_hbm, ten_in, states_in,
    disp_out, cond_out, ten_out, states_out,
    active, shifted, pull, stress, moved, held, tension, sem,
):
    slab = lax.axis_index("slab")
    first = lax.axis_index("col") == 0
    rows, width = active.shape[1:]
    half = rows - TILE
    load_a = pltpu.make_async_copy(act_hbm, active, sem.at[0])
    load_p = pltpu.make_async_copy(pull_hbm, pull, sem.at[1])
    load_s = pltpu.make_async_copy(shift_hbm, shifted, sem.at[2])
    load_a.start()
    load_p.start()
    load_s.start()
    fetch = [pltpu.make_async_copy(ten_in, tension, sem.at[3])]
    pass_on = [pltpu.make_async_copy(tension, ten_out, sem.at[8])]
    for n in range(4):
        fetch.append(pltpu.make_async_copy(states_in.at[n], held.at[n], sem.at[4 + n]))
        pass_on.append(pltpu.make_async_copy(held.at[n], states_out.at[n], sem.at[9 + n]))
    for copy in fetch:
        copy.start()
    mech = Stencils(rows, width)

    def inside(j):
        zz = slab + j - REACH
        return (zz >= 0) & (zz < slabs)

    def tense(j, c):
        for a in range(3):
            t = active[j] * pull[3 + a, j]
            for i in range(3):
                stress[3 * a + i, j] = t * pull[i, j]
        return c

    def move(field):
        def body(j, c):
            ok = inside(j)
            for i in range(3):
                force = mech.force(lambda n, d: stress[n, j + d], i)
                moved[i, j] = jnp.where(ok, field(i, j) + (MECH_RATE / 128.0) * force, 0.0)
            return c

        return body

    def strain(j, c):
        ok = inside(j)
        f = mech.deformation(lambda i, d: moved[i, j + d])
        pieces = first_piola(f, active[j], [pull[3 + a, j] for a in range(3)])
        for n in range(9):
            stress[n, j] = jnp.where(ok, pieces[n], 0.0)
        return c

    load_a.wait()
    load_p.wait()
    lax.fori_loop(0, 2 * REACH + 1, tense, 0)
    load_s.wait()
    lax.fori_loop(1, 2 * REACH, move(lambda i, j: shifted[i, j - 1]), 0)
    for got, copy in zip(fetch, pass_on):
        got.wait()
        copy.start()
    lax.fori_loop(2, 2 * REACH - 1, strain, 0)
    lax.fori_loop(3, 2 * REACH - 2, move(lambda i, j: moved[i, j]), 0)

    comps = metric(
        mech.deformation(lambda i, d: moved[i, REACH + d]),
        [pull[3 + a, REACH] for a in range(3)],
    )
    for i in range(3):
        whole = moved[i, REACH]
        disp_out[i, 0] = jnp.where(first, whole[:half], whole[TILE:])
    for n in range(6):
        cond_out[n, 0] = jnp.where(first, comps[n][:half], comps[n][TILE:])
    for copy in pass_on:
        copy.wait()


def mechanics(slabs, active, shifted, pull, tension, states):
    _, full, width = active.shape
    rows = full - TILE
    vmem = pl.BlockSpec(memory_space=pltpu.VMEM)
    hbm = pl.BlockSpec(memory_space=pltpu.HBM)
    return pl.pallas_call(
        functools.partial(mech_kernel, slabs),
        out_shape=(
            jax.ShapeDtypeStruct((3, 1, rows, width), F32),
            jax.ShapeDtypeStruct((6, 1, rows, width), F32),
            jax.ShapeDtypeStruct(tension.shape, F32),
            jax.ShapeDtypeStruct(states.shape, F32),
        ),
        in_specs=[hbm, hbm, hbm, hbm, hbm],
        out_specs=(vmem, vmem, hbm, hbm),
        scratch_shapes=[
            pltpu.VMEM(active.shape, F32),
            pltpu.VMEM(shifted.shape, F32),
            pltpu.VMEM(pull.shape, F32),
            pltpu.VMEM((9, 2 * REACH + 1, full, width), F32),
            pltpu.VMEM((3, 2 * REACH + 1, full, width), F32),
            pltpu.VMEM(states.shape, F32),
            pltpu.VMEM(tension.shape, F32),
            pltpu.SemaphoreType.DMA((13,)),
        ],
        compiler_params=pltpu.CompilerParams(vmem_limit_bytes=61 << 20),
        name="mechanics",
    )(active, shifted, pull, tension, states)


def on_device(slabs, states, cond, tension, fiber, disp):
    states_next, tension_next, active, shifted, pull = excite(
        slabs, states, cond, tension, fiber, disp
    )
    disp_next, cond_next, tension_next, states_next = mechanics(
        slabs, active, shifted, pull, tension_next, states_next
    )
    return states_next, tension_next, disp_next, cond_next


def solution(mesh):
    wide = P(None, ("grp", "slab"), "col", None)
    flat = P(("grp", "slab"), "col", None)
    return jax.shard_map(
        functools.partial(on_device, mesh.shape["slab"]),
        mesh=mesh,
        in_specs=(wide, wide, flat, flat, wide),
        out_specs=(wide, flat, wide, wide),
        check_vma=False,
    )
```

```python
import functools

import jax
import jax.numpy as jnp
import numpy as np
from jax import lax
from jax.experimental import pallas as pl
from jax.experimental.pallas import tpu as pltpu
from jax.sharding import PartitionSpec as P

SUB = 4
MECH_STEPS = 2
NFIB = 64
STEP_TIME = 0.05
MECH_RATE = 0.15
SIGMA_LONG = 0.16
SIGMA_TRANS = 0.04
PAIRS = ((0, 0), (1, 1), (2, 2), (0, 1), (0, 2), (1, 2))
MESH = pl.DeviceIdType.MESH
HI = lax.Precision.HIGHEST
F32 = jnp.float32
BF16 = jnp.bfloat16
TILE = 8
LANES = 128
CHUNK = 256
RADIUS = 2 * MECH_STEPS + 1
REACH = RADIUS - 1
ALONG = (-4, -2, 2, 4)
BEYOND = (-6, -4, -2, 2, 4, 6)
PEERS = (-6, -4, -3, -2, -1, 0, 1, 2, 3, 4, 6)
JOIN = 10
LAST = 4 * REACH
LAG = 4
HOLD = 2


def ionic(u, v, w, s):
    per = 2.0 / STEP_TIME
    steep = 50.0 * u
    th_v = jnp.tanh(steep - 50.0 * 0.3)
    th_w = jnp.tanh(steep - 50.0 * 0.13)
    th_o = jnp.tanh(steep - 50.0 * 0.006)
    th_m = jnp.tanh(65.0 * u - 65.0 * 0.03)
    th_s = jnp.tanh(2.0458 * u - 2.0458 * 0.65)
    th_r = jnp.tanh(2.0994 * u - 2.0994 * 0.9087)
    hv2 = 1.0 + th_v
    nv2 = 1.0 - th_v
    hw2 = 1.0 + th_w
    nw2 = 1.0 - th_w
    no = 0.5 - 0.5 * th_o
    rate_v = 1.0 / (605.0 * per + (545.0 * per) * th_o)
    rate_w = 1.0 / (37.5 * per - (22.5 * per) * th_m)
    rate_so = 1.0 / (15.5069 * per - (14.5112 * per) * th_s)
    rate_s = 1.0 / (9.3671 * per + (6.6329 * per) * th_w)
    rate_o = 1.0 / (203.0 * per - (197.0 * per) * th_o)
    lead = STEP_TIME / 0.22
    open_v = hv2 * v
    w_inf = no * (0.06 - u * (1.0 / 0.07)) + 0.94
    du = (
        open_v * ((u - 0.3) * (1.55 * lead - lead * u))
        + hw2 * ((w * s) * (STEP_TIME / 3.775) - rate_so)
        - (u * nw2) * rate_o
    )
    v2 = v - open_v * (STEP_TIME / 2.9012) + (nv2 * rate_v) * (no - v)
    w2 = w - (hw2 * w) * (STEP_TIME / 400.0) + (nw2 * rate_w) * (w_inf - w)
    s2 = s + ((1.0 + th_r) - 2.0 * s) * rate_s
    return du, v2, w2, s2


def iota2(shape, dim):
    return lax.broadcasted_iota(jnp.int32, shape, dim)


def first_piola(f, active=None, fdir=None):
    second = {}
    for a in range(3):
        for b in range(a, 3):
            right = f[0][a] * f[0][b] + f[1][a] * f[1][b] + f[2][a] * f[2][b]
            second[a, b] = 0.5 * (right - (1.0 if a == b else 0.0))
    trace = second[0, 0] + second[1, 1] + second[2, 2]
    for a in range(3):
        if active is not None:
            scaled = 0.5 * active * fdir[a]
            for b in range(a, 3):
                second[a, b] = second[a, b] + scaled * fdir[b]
        second[a, a] = second[a, a] + trace
    for a in range(3):
        for b in range(a):
            second[a, b] = second[b, a]
    return [
        f[i][0] * second[0, a] + f[i][1] * second[1, a] + f[i][2] * second[2, a]
        for a in range(3)
        for i in range(3)
    ]


def metric(f, fdir):
    cof = [[None] * 3 for _ in range(3)]
    for i in range(3):
        for j in range(3):
            cof[i][j] = (
                f[(i + 1) % 3][(j + 1) % 3] * f[(i + 2) % 3][(j + 2) % 3]
                - f[(i + 1) % 3][(j + 2) % 3] * f[(i + 2) % 3][(j + 1) % 3]
            )
    det = f[0][0] * cof[0][0] + f[0][1] * cof[0][1] + f[0][2] * cof[0][2]
    scale = 1.0 / det
    inverse = [[cof[i][j] * scale for i in range(3)] for j in range(3)]
    g = [inverse[a][0] * fdir[0] + inverse[a][1] * fdir[1] + inverse[a][2] * fdir[2] for a in range(3)]
    comps = []
    for a, b in PAIRS:
        inner = (
            inverse[a][0] * inverse[b][0]
            + inverse[a][1] * inverse[b][1]
            + inverse[a][2] * inverse[b][2]
        )
        comps.append(SIGMA_TRANS * inner + (SIGMA_LONG - SIGMA_TRANS) * (g[a] * g[b]))
    return comps


class Stencils:
    def __init__(self, rows, width):
        self.rows, self.width = rows, width
        self.lane = iota2((rows, LANES), 1)
        self.line = iota2((TILE, width), 0)

    def left(self, f):
        parts, before = [], 0.0
        for x in range(0, self.width, LANES):
            here = f[:, x : x + LANES]
            parts.append(pltpu.roll(jnp.where(self.lane == LANES - 1, before, here), 1, 1))
            before = here
        return jnp.concatenate(parts, axis=1)

    def right(self, f):
        parts, after = [], 0.0
        for x in reversed(range(0, self.width, LANES)):
            here = f[:, x : x + LANES]
            parts.append(pltpu.roll(jnp.where(self.lane == 0, after, here), LANES - 1, 1))
            after = here
        return jnp.concatenate(parts[::-1], axis=1)

    def south(self, f):
        parts, before = [], 0.0
        for y in range(0, self.rows, TILE):
            here = f[y : y + TILE]
            parts.append(pltpu.roll(jnp.where(self.line == TILE - 1, before, here), 1, 0))
            before = here
        return jnp.concatenate(parts, axis=0)

    def north(self, f):
        parts, after = [], 0.0
        for y in reversed(range(0, self.rows, TILE)):
            here = f[y : y + TILE]
            parts.append(pltpu.roll(jnp.where(self.line == 0, after, here), TILE - 1, 0))
            after = here
        return jnp.concatenate(parts[::-1], axis=0)


    def sx(self, f):
        return self.left(f) + self.right(f) + 6.0 * f

    def dx(self, f):
        return self.right(f) - self.left(f)

    def sy(self, f):
        return self.south(f) + self.north(f) + 6.0 * f

    def dy(self, f):
        return self.north(f) - self.south(f)

    def deformation(self, field):
        f = []
        for i in range(3):
            low, mid, high = field(i, -1), field(i, 0), field(i, 1)
            zs = low + high + 6.0 * mid
            zd = high - low
            grads = [self.sy(self.sx(zd)), self.dy(self.sx(zs)), self.sy(self.dx(zs))]
            f.append([(1.0 / 128.0) * g for g in grads])
            f[i][i] = f[i][i] + 1.0
        return f

    def force(self, stress, i):
        zd = stress(i, 1) - stress(i, -1)
        ys = stress(3 + i, -1) + stress(3 + i, 1) + 6.0 * stress(3 + i, 0)
        xs = stress(6 + i, -1) + stress(6 + i, 1) + 6.0 * stress(6 + i, 0)
        return self.sy(self.sx(zd) + self.dx(xs)) + self.dy(self.sx(ys))


def sine(x, terms=6):
    y = x * x
    c = 1.0
    for n in range(2 * terms, 0, -2):
        c = 1.0 - y * (1.0 / (n * (n + 1))) * c
    return x * c


def cosine(x):
    y = x * x
    c = 1.0
    for n in (13, 11, 9, 7, 5, 3, 1):
        c = 1.0 - y * (1.0 / (n * (n + 1))) * c
    return c


def directions(index):
    theta = -1.0 + index * (2.0 / (NFIB - 1))
    triple = 3.0 * index
    turns = jnp.floor(triple * (0.5 / np.pi) + 0.5)
    triple = (triple - turns * 6.28125) - turns * (2.0 * np.pi - 6.28125)
    tilt = 0.3 * sine(triple, 10)
    flat = cosine(tilt)
    return [sine(tilt), flat * sine(theta), flat * cosine(theta)]


def halves(x):
    high = x.astype(BF16)
    return high, (x - high.astype(F32)).astype(BF16)


def excite_kernel(
    slabs, states, cond_hbm, ten_hbm, fib_hbm, disp_hbm,
    out_hbm, ten_out, act_hbm, shift_hbm, pull_hbm,
    ubuf, out, cond, tension, coeff, dif, act_win, zeros, fix_win, fiber, passive, shifted, pull, pooled,
    load_sem, store_sem, sz, rz, sc, rc, sy, ry, sa, ra, sf, rf, sg, relay, sv, rv,
):
    grp = lax.axis_index("grp")
    slab = lax.axis_index("slab")
    col = lax.axis_index("col")
    other = 1 - col
    depth, rows, width = out.shape[1:]
    tiles = rows // TILE
    has_up = slab < slabs - 1
    has_dn = slab > 0
    edge_src = rows - (rows - TILE) * col
    edge_dst = (rows + TILE) * col

    load_u = pltpu.make_async_copy(
        states.at[0], ubuf.at[0, pl.ds(1, depth), pl.ds(TILE, rows), :], load_sem.at[0]
    )
    load_g = pltpu.make_async_copy(
        states.at[pl.ds(1, 3)], out.at[pl.ds(1, 3)], load_sem.at[1]
    )
    load_c = pltpu.make_async_copy(cond_hbm, cond, load_sem.at[2])
    load_t = pltpu.make_async_copy(ten_hbm, tension, load_sem.at[3])
    load_u.start()
    load_c.start()
    load_g.start()
    load_t.start()
    half = rows // 4
    span = half + TILE
    own = pl.ds(pl.multiple_of(TILE * col, TILE), half)
    near = pl.ds(TILE, TILE)
    far = pl.ds(pl.multiple_of(2 * TILE * col, TILE), TILE)
    load_d = pltpu.make_async_copy(
        disp_hbm.at[:, 0], fix_win.at[RADIUS, pl.ds(0, 3), own, :], load_sem.at[4]
    )
    load_f = pltpu.make_async_copy(fib_hbm, fiber, load_sem.at[5])
    load_d.start()
    load_f.start()

    barrier = pltpu.get_barrier_semaphore()

    def greet(where):
        pl.semaphore_signal(barrier, inc=1, device_id=where, device_id_type=MESH)

    def there(d):
        return (slab + d >= 0) & (slab + d < slabs)

    peers = 0
    for d in PEERS:
        valid = there(d)
        wide = abs(d) <= REACH
        count = (0 if d == 0 else 1) + (1 if wide else 0)
        peers = peers + count * valid.astype(jnp.int32)

        @pl.when(valid)
        def _(d=d, wide=wide):
            if wide:
                greet((grp, slab + d, other))
            if d != 0:
                greet((grp, slab + d, col))

    zeros[...] = jnp.zeros(zeros.shape, F32)

    def blank_a(d):
        return pltpu.make_async_copy(zeros, act_hbm.at[d + REACH], ra.at[d + REACH, 0])

    for d in range(-RADIUS, RADIUS + 1):

        @pl.when(jnp.logical_not(there(d)))
        def _(d=d):
            fix_win[d + RADIUS] = jnp.zeros(fix_win.shape[1:], F32)
            if abs(d) <= REACH:
                blank_a(d).start()

    blank = jnp.zeros((TILE, width), F32)

    def clear_y(n, c):
        ubuf[n // (depth + 2), n % (depth + 2), pl.ds(pl.multiple_of(edge_dst, TILE), TILE), :] = blank
        return c

    lax.fori_loop(0, SUB * (depth + 2), clear_y, 0)

    def clear_z(layer):
        per = rows // TILE + 2

        def body(n, c):
            ubuf[n // per, layer, pl.ds(pl.multiple_of((n % per) * TILE, TILE), TILE), :] = blank
            return c

        lax.fori_loop(0, SUB * per, body, 0)

    @pl.when(slab == 0)
    def _():
        clear_z(0)

    @pl.when(slab == slabs - 1)
    def _():
        clear_z(depth + 1)

    def row_of(step):
        return jnp.where(col == 1, step, tiles - 1 - step)

    def copy_z(slot, way, step):
        at = pl.ds(pl.multiple_of(TILE + TILE * row_of(step), TILE), TILE)
        src = depth if way == 0 else 1
        dst = 0 if way == 0 else depth + 1
        to = slab + 1 if way == 0 else slab - 1
        return pltpu.make_async_remote_copy(
            src_ref=ubuf.at[slot, src, at, :],
            dst_ref=ubuf.at[slot, dst, at, :],
            send_sem=sz.at[way],
            recv_sem=rz.at[slot, way, step],
            device_id=(grp, to, col),
            device_id_type=MESH,
        )

    def carried(step, count):
        return lax.rem((step + 1) * count, tiles) < count

    beside = 1 - 2 * lax.rem(slab, 2)
    chips = slabs // 2
    upper = tiles * (chips - 1 - slab // 2) // chips
    lower = tiles * (slab // 2) // chips
    even = beside == 1
    mine = jnp.where(even, lower, upper)
    others = jnp.where(even, upper, lower)
    onward = 1 - lax.rem(slab + 1, 2)

    def copy_via(slot, way, step):
        at = pl.ds(pl.multiple_of(TILE + TILE * row_of(step), TILE), TILE)
        to = pl.ds(pl.multiple_of(TILE * row_of(step), TILE), TILE)
        return pltpu.make_async_remote_copy(
            src_ref=ubuf.at[slot, depth if way == 0 else 1, at, :],
            dst_ref=relay.at[slot, to, :],
            send_sem=sz.at[way],
            recv_sem=rv.at[slot, step],
            device_id=(grp, slab + beside, col),
            device_id_type=MESH,
        )

    def copy_on(slot, step):
        at = pl.ds(pl.multiple_of(TILE * row_of(step), TILE), TILE)
        to = pl.ds(pl.multiple_of(TILE + TILE * row_of(step), TILE), TILE)
        return pltpu.make_async_remote_copy(
            src_ref=relay.at[slot, at, :],
            dst_ref=ubuf.at[slot, onward * (depth + 1), to, :],
            send_sem=sv.at[slot, step],
            recv_sem=rz.at[slot, onward, step],
            device_id=(grp, slab + 2 * beside, col),
            device_id_type=MESH,
        )

    def hand_on(n):
        @pl.when((n < SUB * tiles) & carried(n % tiles, others))
        def _():
            copy_via(n // tiles, 0, n % tiles).wait_recv()
            copy_on(n // tiles, n % tiles).start()

    def copy_c(slot, way):
        at = depth + 1 if way == 0 else 0
        return pltpu.make_async_remote_copy(
            src_ref=ubuf.at[slot, at, pl.ds(pl.multiple_of(edge_src, TILE), TILE), :],
            dst_ref=ubuf.at[slot, at, pl.ds(pl.multiple_of(edge_dst, TILE), TILE), :],
            send_sem=sc.at[way],
            recv_sem=rc.at[slot, way],
            device_id=(grp, slab, other),
            device_id_type=MESH,
        )

    def copy_y(slot):
        return pltpu.make_async_remote_copy(
            src_ref=ubuf.at[slot, pl.ds(1, depth), pl.ds(pl.multiple_of(edge_src, TILE), TILE), :],
            dst_ref=ubuf.at[slot, pl.ds(1, depth), pl.ds(pl.multiple_of(edge_dst, TILE), TILE), :],
            send_sem=sy.at[0],
            recv_sem=ry.at[slot],
            device_id=(grp, slab, other),
            device_id_type=MESH,
        )

    def both(do_up, do_dn):
        pl.when(has_up)(do_up)
        pl.when(has_dn)(do_dn)

    def send_z(n, by_partner):
        slot = n // tiles
        step = n % tiles
        via = carried(step, mine)

        def send(way):
            through = via & (jnp.logical_not(even) if way == 0 else even)
            if by_partner:
                pl.when(through)(lambda: copy_via(slot, way, step).start())
            else:
                pl.when(jnp.logical_not(through))(lambda: copy_z(slot, way, step).start())

        @pl.when(n < SUB * tiles)
        def _():
            both(lambda: send(0), lambda: send(1))

    def send_c(slot):
        both(lambda: copy_c(slot, 0).start(), lambda: copy_c(slot, 1).start())

    def recv_z(slot, step):
        both(lambda: copy_z(slot, 1, step).wait_recv(), lambda: copy_z(slot, 0, step).wait_recv())

    def recv_c(slot):
        both(lambda: copy_c(slot, 0).wait_recv(), lambda: copy_c(slot, 1).wait_recv())

    def copy_f(source, d, n):
        slot = RADIUS + source - d
        return pltpu.make_async_remote_copy(
            src_ref=fix_win.at[RADIUS + source, :, own, :],
            dst_ref=fix_win.at[slot, :, own, :],
            send_sem=sf.at[n],
            recv_sem=rf.at[slot],
            device_id=(grp, slab + d, col),
            device_id_type=MESH,
        )

    def come_f(e):
        return pltpu.make_async_remote_copy(
            src_ref=fix_win.at[RADIUS, :, own, :],
            dst_ref=fix_win.at[RADIUS + e, :, own, :],
            send_sem=sf.at[0],
            recv_sem=rf.at[RADIUS + e],
            device_id=(grp, slab + e, col),
            device_id_type=MESH,
        )

    def share_f(whose):
        return pltpu.make_async_remote_copy(
            src_ref=fix_win.at[:, :, near, :],
            dst_ref=fix_win.at[:, :, pl.ds(pl.multiple_of(2 * TILE * whose, TILE), TILE), :],
            send_sem=sg.at[0],
            recv_sem=sg.at[1],
            device_id=(grp, slab, other),
            device_id_type=MESH,
        )

    def forward_f(act):
        for n, d in enumerate(BEYOND):
            ok = there(d) & (jnp.abs(d - beside) <= RADIUS)
            pl.when(ok)(lambda n=n, d=d: act(n, d))

    def relay_f(n, d):
        return copy_f(beside, d, 1 + len(ALONG) + n)

    pl.semaphore_wait(barrier, peers)

    load_u.wait()
    send_z(0, True)
    send_z(0, False)
    copy_y(0).start()
    send_z(1, True)
    send_z(1, False)
    load_d.wait()
    load_f.wait()
    fix_win[RADIUS, 3, own, :] = fiber[0].astype(F32)
    copy_f(0, beside, 0).start()
    for n, d in enumerate(ALONG):
        pl.when(there(d))(lambda n=n, d=d: copy_f(0, d, 1 + n).start())

    def initial(step, c):
        send_z(step, True)
        pl.when(step < tiles - HOLD)(lambda: send_z(step, False))
        return c

    lax.fori_loop(2, tiles, initial, 0)
    load_c.wait()

    spread_x = (iota2((256, 512), 0) % 128 == iota2((256, 512), 1) // 4).astype(BF16)
    spread_y = (iota2((rows, rows // 4), 0) // 4 == iota2((rows, rows // 4), 1)).astype(BF16)
    for c in range(6):
        tall = [
            jnp.dot(spread_y, part, preferred_element_type=F32).astype(BF16)
            for part in halves(cond[c, 0])
        ]
        for h in range(width // 512):
            part = jnp.concatenate([t[:, h * 128 : (h + 1) * 128] for t in tall], axis=1)
            part = jnp.dot(part, spread_x, preferred_element_type=F32)
            coeff[c, :, h * 512 : (h + 1) * 512] = part if c < 3 else 0.5 * part

    def centre_weight(t, c):
        at = pl.ds(pl.multiple_of(TILE * t, TILE), TILE)
        coeff[6, at, :] = 1.0 - 2.0 * (coeff[0, at, :] + coeff[1, at, :] + coeff[2, at, :])
        return c

    lax.fori_loop(0, tiles, centre_weight, 0)

    load_g.wait()
    load_t.wait()

    lane = iota2((TILE, width), 1)

    def left(f):
        return jnp.where(lane == 0, 0.0, pltpu.roll(f, 1, 1))

    def right(f):
        return jnp.where(lane == width - 1, 0.0, pltpu.roll(f, width - 1, 1))

    line = iota2((TILE, width), 0)

    def north_south(tall):
        here = tall[TILE : 2 * TILE]
        return (
            pltpu.roll(jnp.where(line == 0, tall[2 * TILE :], here), TILE - 1, 0),
            pltpu.roll(jnp.where(line == TILE - 1, tall[:TILE], here), 1, 0),
        )

    def layer(k, z, r):
        base = pl.multiple_of(TILE * r, TILE)
        here = pl.ds(base, TILE)
        tall = pl.ds(base, 3 * TILE)
        below = ubuf[k, z, tall, :]
        mid = ubuf[k, z + 1, tall, :]
        above = ubuf[k, z + 2, tall, :]
        odd = above - below
        centre = mid[TILE : 2 * TILE]
        odd0 = odd[TILE : 2 * TILE]
        north, south = north_south(mid)
        odd_north, odd_south = north_south(odd)
        slope = north - south
        total = coeff[6, here, :] * centre
        total = total + coeff[0, here, :] * (above[TILE : 2 * TILE] + below[TILE : 2 * TILE])
        total = total + coeff[1, here, :] * (north + south)
        total = total + coeff[2, here, :] * (right(centre) + left(centre))
        total = total + coeff[3, here, :] * (odd_north - odd_south)
        total = total + coeff[4, here, :] * (right(odd0) - left(odd0))
        total = total + coeff[5, here, :] * (right(slope) - left(slope))
        dif[...] = total
        up = pl.ds(pl.multiple_of(base + TILE, TILE), TILE)
        for x in range(0, width, CHUNK):
            xs = pl.ds(x, CHUNK)
            du, v2, w2, s2 = ionic(
                ubuf[k, z + 1, up, xs], out[1, z, here, xs], out[2, z, here, xs],
                out[3, z, here, xs],
            )
            u2 = dif[:, xs] + du
            ubuf[k + 1, z + 1, up, xs] = u2
            out[0, z, here, xs] = u2
            out[1, z, here, xs] = v2
            out[2, z, here, xs] = w2
            out[3, z, here, xs] = s2

    def leave(step):
        at = pl.ds(pl.multiple_of(TILE * row_of(step), TILE), TILE)
        return pltpu.make_async_copy(
            out.at[:, :, at, :], out_hbm.at[:, :, at, :], store_sem.at[step]
        )

    pair_x = (iota2((256, 128), 0) // 2 == iota2((256, 128), 1)).astype(F32)
    pair_2 = (iota2((512, 128), 0) % 256 // 2 == iota2((512, 128), 1)).astype(BF16)
    pair_y2 = (iota2((half, 2 * half), 0) == iota2((half, 2 * half), 1) // 2).astype(F32)

    def pool_lanes(rows_in, weights, size, chunk):
        parts = halves(rows_in)
        for h in range(width // chunk):
            both_halves = jnp.concatenate(
                [part[:, h * chunk : (h + 1) * chunk] for part in parts], axis=1
            )
            pooled[h, 0:size] = jnp.dot(both_halves, weights, preferred_element_type=F32)

    def tense(p):
        fine = pl.ds(pl.multiple_of(2 * TILE * p, 2 * TILE), 2 * TILE)
        wide = pl.ds(pl.multiple_of(TILE * p, TILE), TILE)
        sums = []
        for q in range(depth // 2):
            layers = out[0, 2 * q, fine, :] + out[0, 2 * q + 1, fine, :]
            sums.append(layers + pltpu.roll(layers, 2 * TILE - 1, 0))
        pool_lanes(0.125 * jnp.concatenate(sums, axis=0), pair_2, TILE * depth, 256)
        for h in range(width // 256):
            xo = slice(h * 128, (h + 1) * 128)
            for q in range(depth // 2):
                mean = pooled[h, pl.ds(2 * TILE * q, TILE, 2), :]
                before = tension[q, wide, xo]
                ten_out[q, wide, xo] = before + 0.5 * (mean - before)

    pool_x = (iota2((1024, 128), 0) % 512 // 4 == iota2((1024, 128), 1)).astype(BF16)

    def activate(part, lines):
        fine = pl.ds(pl.multiple_of(4 * TILE * part, 4 * TILE), 4 * TILE)
        layers = out[0, 0, fine, :]
        for z in range(1, depth):
            layers = layers + out[0, z, fine, :]
        layers = layers + pltpu.roll(layers, 4 * TILE - 1, 0)
        layers = layers + pltpu.roll(layers, 4 * TILE - 2, 0)
        pool_lanes((0.5 / (16 * depth)) * layers, pool_x, 4 * TILE, 512)
        for h in range(width // 512):
            xo = slice(h * 128, (h + 1) * 128)
            act_win[lines, xo] = act_win[lines, xo] + pooled[h, pl.ds(0, TILE, 4), :]

    def copy_a(d, to, kind, lines, at):
        return pltpu.make_async_remote_copy(
            src_ref=act_win.at[lines, :],
            dst_ref=act_hbm.at[REACH - d, at, :],
            send_sem=sa.at[d + REACH, kind],
            recv_sem=ra.at[REACH - d, kind],
            device_id=(grp, slab + d, to),
            device_id_type=MESH,
        )

    def keep_a(kind, lines):
        return pltpu.make_async_copy(
            act_win.at[lines, :], act_hbm.at[REACH, lines, :], sa.at[REACH, kind]
        )

    def each_a(act, centre):
        for d in sorted(range(-REACH, REACH + 1), key=lambda d: -abs(d)):
            if d != 0 or centre:
                pl.when(there(d))(lambda d=d: act(d))

    mech = Stencils(span, fix_win.shape[3])

    def inside(j):
        return there(j - RADIUS)

    def prepare(j):
        ok = inside(j)
        f = mech.deformation(lambda i, d: fix_win[j + d, i])
        fdir = directions(fix_win[j, 3])
        pieces = first_piola(f)
        for n in range(9):
            passive[n, j - 1] = jnp.where(ok, pieces[n], 0.0)
        for i in range(3):
            g = 0.5 * (f[i][0] * fdir[0] + f[i][1] * fdir[1] + f[i][2] * fdir[2])
            pull[i, j - 1] = jnp.where(ok, g, 0.0)
            pull[3 + i, j - 1] = fdir[i]

    def shift(j):
        ok = inside(j)
        for i in range(3):
            force = mech.force(lambda n, d: passive[n, j - 1 + d], i)
            moved = fix_win[j, i] + (MECH_RATE / 128.0) * force
            shifted[i, j - 2] = jnp.where(ok, moved, 0.0)

    hand_shift = pltpu.make_async_copy(shifted, shift_hbm, load_sem.at[0])
    hand_pull = pltpu.make_async_copy(pull, pull_hbm, load_sem.at[1])

    for h in range(width // 512):
        xs = slice(h * 256, (h + 1) * 256)
        layers = tension[0, :, xs] + tension[1, :, xs]
        mean = jnp.dot(layers, pair_x, precision=HI, preferred_element_type=F32)
        mean = 0.0625 * jnp.dot(pair_y2, mean, precision=HI, preferred_element_type=F32)
        act_win[own, h * 128 : (h + 1) * 128] = mean

    def within(n):
        k = n // tiles
        r = row_of(n % tiles)

        def inner(m, c):
            layer(k, m, r)
            return c

        lax.fori_loop(1, depth - 1, inner, 0)

    recv_z(0, 0)
    send_c(0)
    copy_y(0).wait_recv()
    within(0)

    def chunk(n, c):
        k = n // tiles
        step = n % tiles
        r = row_of(step)

        @pl.when(n < LAG - 1)
        def _():
            hand_on(2 * n + 1)
            hand_on(2 * n + 2)

        pl.when(n >= LAG - 1)(lambda: hand_on(n + LAG))

        @pl.when(n == tiles // 2)
        def _():
            come_f(beside).wait_recv()

        for far_by in (2, 4, 6):

            @pl.when(n == tiles // 2 + far_by // 2 - 1)
            def _(far_by=far_by):
                forward_f(lambda n, d: relay_f(n, d).start() if abs(d) == far_by else None)

        @pl.when(n == JOIN)
        def _():
            for d in range(-RADIUS, RADIUS + 1):
                if d != 0:
                    arrives = there(d) if d % 2 == 0 else there(d) & (beside != d)
                    pl.when(arrives)(lambda d=d: come_f(d).wait_recv())
            share_f(col).start()

        @pl.when(n == JOIN + 2)
        def _():
            share_f(col).wait_recv()

        @pl.when(step < tiles - 1)
        def _():
            recv_z(k, step + 1)

        @pl.when(step == 0)
        def _():
            recv_c(k)

        def outer(m, c):
            layer(k, m * (depth - 1), r)
            return c

        lax.fori_loop(0, 2, outer, 0)

        send_z(n + tiles, True)
        send_z(n + tiles - HOLD, False)

        @pl.when((k < SUB - 1) & (step == 0))
        def _():
            copy_y(k + 1).start()

        @pl.when((k < SUB - 1) & (step == tiles - 1))
        def _():
            recv_z(k + 1, 0)
            send_c(k + 1)
            copy_y(k + 1).wait_recv()

        @pl.when(n < SUB * tiles - 1)
        def _():
            within(n + 1)

        turn = n - JOIN - 2
        stress_turn = (turn < 2) | (turn % 2 == 0)

        @pl.when((turn >= 0) & (turn < LAST) & stress_turn)
        def _():
            prepare(jnp.where(turn < 2, turn + 1, turn // 2 + 2))

        @pl.when((turn >= 3) & (turn < LAST) & jnp.logical_not(stress_turn))
        def _():
            shift((turn + 1) // 2)

        @pl.when(turn == LAST)
        def _():
            hand_shift.start()
            hand_pull.start()

        @pl.when(k == SUB - 1)
        def _():
            leave(step).start()

        @pl.when(n == SUB * tiles - 1 - tiles // 2)
        def _():
            activate(other, near)
            each_a(lambda d: copy_a(d, col, 0, near, near).start(), False)
            each_a(lambda d: copy_a(d, other, 1, near, far).start(), True)
            keep_a(0, near).start()

        @pl.when((k == SUB - 1) & (step % 2 == 1) & (step < tiles - 1))
        def _():
            tense(r // 2)

        return c

    lax.fori_loop(0, SUB * tiles, chunk, 0)

    activate(col, far)
    each_a(lambda d: copy_a(d, col, 2, far, far).start(), False)
    keep_a(2, far).start()
    tense(row_of(tiles - 1) // 2)
    share_f(col).wait_send()
    copy_f(0, beside, 0).wait_send()
    for n, d in enumerate(ALONG):
        pl.when(there(d))(lambda n=n, d=d: copy_f(0, d, 1 + n).wait_send())
    forward_f(lambda n, d: relay_f(n, d).wait_send())
    hand_shift.wait()
    hand_pull.wait()
    def sent(what, sem):
        pltpu.make_async_remote_copy(
            src_ref=what, dst_ref=what, send_sem=sem, recv_sem=sg.at[1],
            device_id=(grp, slab, other), device_id_type=MESH,
        ).wait_send()

    both(lambda: sent(relay, sz.at[0]), lambda: sent(relay, sz.at[1]))
    corners = ubuf.at[0, pl.ds(0, SUB), pl.ds(0, TILE), :]
    both(lambda: sent(corners, sc.at[0]), lambda: sent(corners, sc.at[1]))
    sent(ubuf.at[pl.ds(0, SUB), pl.ds(1, depth), pl.ds(0, TILE), :], sy.at[0])

    def drain(n, c):
        pl.when(carried(n % tiles, others))(lambda: copy_on(n // tiles, n % tiles).wait_send())
        return c

    lax.fori_loop(0, SUB * tiles, drain, 0)

    def left_all(step, c):
        leave(step).wait()
        return c

    lax.fori_loop(0, tiles, left_all, 0)
    each_a(lambda d: copy_a(d, col, 0, near, near).wait_send(), False)
    each_a(lambda d: copy_a(d, other, 1, near, far).wait_send(), True)
    each_a(lambda d: copy_a(d, col, 2, far, far).wait_send(), False)
    for d in range(-REACH, REACH + 1):
        pl.when(jnp.logical_not(there(d)))(lambda d=d: blank_a(d).wait())
    each_a(lambda d: copy_a(-d, col, 0, near, near).wait_recv(), False)
    each_a(lambda d: copy_a(-d, other, 1, near, far).wait_recv(), True)
    each_a(lambda d: copy_a(-d, col, 2, far, far).wait_recv(), False)
    keep_a(0, near).wait()
    keep_a(2, far).wait()


def excite(slabs, states, cond, tension, fiber, disp):
    _, depth, rows, width = states.shape
    tiles = rows // TILE
    full = rows // 4 + TILE
    across = cond.shape[3]
    vmem = pl.BlockSpec(memory_space=pltpu.VMEM)
    hbm = pl.BlockSpec(memory_space=pltpu.HBM)
    window = (2 * REACH + 1, full, across)
    shifts = (3, 2 * REACH - 1, full, across)
    pulls = (6, 2 * REACH + 1, full, across)
    dma = pltpu.SemaphoreType.DMA
    return pl.pallas_call(
        functools.partial(excite_kernel, slabs),
        out_shape=(
            jax.ShapeDtypeStruct(states.shape, F32),
            jax.ShapeDtypeStruct(tension.shape, F32),
            jax.ShapeDtypeStruct(window, F32),
            jax.ShapeDtypeStruct(shifts, F32),
            jax.ShapeDtypeStruct(pulls, F32),
        ),
        in_specs=[hbm, hbm, hbm, hbm, hbm],
        out_specs=(hbm, vmem, hbm, hbm, hbm),
        scratch_shapes=[
            pltpu.VMEM((SUB + 1, depth + 2, rows + 2 * TILE, width), F32),
            pltpu.VMEM(states.shape, F32),
            pltpu.VMEM(cond.shape, F32),
            pltpu.VMEM(tension.shape, F32),
            pltpu.VMEM((7, rows, width), F32),
            pltpu.VMEM((TILE, width), F32),
            pltpu.VMEM(window[1:], F32),
            pltpu.VMEM(window[1:], F32),
            pltpu.VMEM((2 * RADIUS + 1, 4, full, across), F32),
            pltpu.VMEM(fiber.shape, jnp.int32),
            pltpu.VMEM((9, *window), F32),
            pltpu.VMEM(shifts, F32),
            pltpu.VMEM(pulls, F32),
            pltpu.VMEM((width // 256, 4 * TILE, 128), F32),
            dma((6,)),
            dma((tiles,)),
            dma((2,)),
            dma((SUB, 2, tiles)),
            dma((2,)),
            dma((SUB, 2)),
            dma((1,)),
            dma((SUB,)),
            dma((2 * REACH + 1, 3)),
            dma((2 * REACH + 1, 3)),
            dma((1 + len(ALONG) + len(BEYOND),)),
            dma((2 * RADIUS + 1,)),
            dma((2,)),
            pltpu.VMEM((SUB, rows, width), F32),
            dma((SUB, tiles)),
            dma((SUB, tiles)),
        ],
        compiler_params=pltpu.CompilerParams(
            collective_id=0, has_side_effects=True, vmem_limit_bytes=61 << 20
        ),
        cost_estimate=pl.CostEstimate(
            flops=200_000_000, bytes_accessed=16 << 20, transcendentals=6_000_000
        ),
        name="excite",
    )(states, cond, tension, fiber, disp)


def mech_kernel(
    slabs, act_hbm, shift_hbm, pull_hbm, ten_in, states_in,
    disp_out, cond_out, ten_out, states_out,
    active, shifted, pull, stress, moved, held, tension, sem,
):
    slab = lax.axis_index("slab")
    first = lax.axis_index("col") == 0
    rows, width = active.shape[1:]
    half = rows - TILE
    load_a = pltpu.make_async_copy(act_hbm, active, sem.at[0])
    load_p = pltpu.make_async_copy(pull_hbm, pull, sem.at[1])
    load_s = pltpu.make_async_copy(shift_hbm, shifted, sem.at[2])
    load_a.start()
    load_p.start()
    load_s.start()
    fetch = [pltpu.make_async_copy(ten_in, tension, sem.at[3])]
    pass_on = [pltpu.make_async_copy(tension, ten_out, sem.at[8])]
    for n in range(4):
        fetch.append(pltpu.make_async_copy(states_in.at[n], held.at[n], sem.at[4 + n]))
        pass_on.append(pltpu.make_async_copy(held.at[n], states_out.at[n], sem.at[9 + n]))
    for copy in fetch:
        copy.start()
    mech = Stencils(rows, width)

    def inside(j):
        zz = slab + j - REACH
        return (zz >= 0) & (zz < slabs)

    def tense(j, c):
        for a in range(3):
            t = active[j] * pull[3 + a, j]
            for i in range(3):
                stress[3 * a + i, j] = t * pull[i, j]
        return c

    def move(field):
        def body(j, c):
            ok = inside(j)
            for i in range(3):
                force = mech.force(lambda n, d: stress[n, j + d], i)
                moved[i, j] = jnp.where(ok, field(i, j) + (MECH_RATE / 128.0) * force, 0.0)
            return c

        return body

    def strain(j, c):
        ok = inside(j)
        f = mech.deformation(lambda i, d: moved[i, j + d])
        pieces = first_piola(f, active[j], [pull[3 + a, j] for a in range(3)])
        for n in range(9):
            stress[n, j] = jnp.where(ok, pieces[n], 0.0)
        return c

    load_a.wait()
    load_p.wait()
    for j in range(2 * REACH + 1):
        tense(j, 0)
    load_s.wait()
    for j in range(1, 2 * REACH):
        move(lambda i, j: shifted[i, j - 1])(j, 0)
    for got, copy in zip(fetch, pass_on):
        got.wait()
        copy.start()
    for j in range(2, 2 * REACH - 1):
        strain(j, 0)
    for j in range(3, 2 * REACH - 2):
        move(lambda i, j: moved[i, j])(j, 0)

    comps = metric(
        mech.deformation(lambda i, d: moved[i, REACH + d]),
        [pull[3 + a, REACH] for a in range(3)],
    )
    for i in range(3):
        whole = moved[i, REACH]
        disp_out[i, 0] = jnp.where(first, whole[:half], whole[TILE:])
    for n in range(6):
        cond_out[n, 0] = jnp.where(first, comps[n][:half], comps[n][TILE:])
    for copy in pass_on:
        copy.wait()


def mechanics(slabs, active, shifted, pull, tension, states):
    _, full, width = active.shape
    rows = full - TILE
    vmem = pl.BlockSpec(memory_space=pltpu.VMEM)
    hbm = pl.BlockSpec(memory_space=pltpu.HBM)
    return pl.pallas_call(
        functools.partial(mech_kernel, slabs),
        out_shape=(
            jax.ShapeDtypeStruct((3, 1, rows, width), F32),
            jax.ShapeDtypeStruct((6, 1, rows, width), F32),
            jax.ShapeDtypeStruct(tension.shape, F32),
            jax.ShapeDtypeStruct(states.shape, F32),
        ),
        in_specs=[hbm, hbm, hbm, hbm, hbm],
        out_specs=(vmem, vmem, hbm, hbm),
        scratch_shapes=[
            pltpu.VMEM(active.shape, F32),
            pltpu.VMEM(shifted.shape, F32),
            pltpu.VMEM(pull.shape, F32),
            pltpu.VMEM((9, 2 * REACH + 1, full, width), F32),
            pltpu.VMEM((3, 2 * REACH + 1, full, width), F32),
            pltpu.VMEM(states.shape, F32),
            pltpu.VMEM(tension.shape, F32),
            pltpu.SemaphoreType.DMA((13,)),
        ],
        compiler_params=pltpu.CompilerParams(vmem_limit_bytes=61 << 20),
        name="mechanics",
    )(active, shifted, pull, tension, states)


def on_device(slabs, states, cond, tension, fiber, disp):
    states_next, tension_next, active, shifted, pull = excite(
        slabs, states, cond, tension, fiber, disp
    )
    disp_next, cond_next, tension_next, states_next = mechanics(
        slabs, active, shifted, pull, tension_next, states_next
    )
    return states_next, tension_next, disp_next, cond_next


def solution(mesh):
    wide = P(None, ("grp", "slab"), "col", None)
    flat = P(("grp", "slab"), "col", None)
    return jax.shard_map(
        functools.partial(on_device, mesh.shape["slab"]),
        mesh=mesh,
        in_specs=(wide, wide, flat, flat, wide),
        out_specs=(wide, flat, wide, wide),
        check_vma=False,
    )
```

```python
import functools

import jax
import jax.numpy as jnp
import numpy as np
from jax import lax
from jax.experimental import pallas as pl
from jax.experimental.pallas import tpu as pltpu
from jax.sharding import PartitionSpec as P

SUB = 4
MECH_STEPS = 2
NFIB = 64
STEP_TIME = 0.05
MECH_RATE = 0.15
SIGMA_LONG = 0.16
SIGMA_TRANS = 0.04
PAIRS = ((0, 0), (1, 1), (2, 2), (0, 1), (0, 2), (1, 2))
MESH = pl.DeviceIdType.MESH
HI = lax.Precision.HIGHEST
F32 = jnp.float32
BF16 = jnp.bfloat16
TILE = 8
LANES = 128
CHUNK = 256
RADIUS = 2 * MECH_STEPS + 1
REACH = RADIUS - 1
ALONG = (-4, -2, 2, 4)
BEYOND = (-6, -4, -2, 2, 4, 6)
PEERS = (-6, -4, -3, -2, -1, 0, 1, 2, 3, 4, 6)
JOIN = 10
LAST = 4 * REACH
LAG = 4
HOLD = 2


def ionic(u, v, w, s):
    per = 2.0 / STEP_TIME
    steep = 50.0 * u
    th_v = jnp.tanh(steep - 50.0 * 0.3)
    th_w = jnp.tanh(steep - 50.0 * 0.13)
    th_o = jnp.tanh(steep - 50.0 * 0.006)
    th_m = jnp.tanh(65.0 * u - 65.0 * 0.03)
    th_s = jnp.tanh(2.0458 * u - 2.0458 * 0.65)
    th_r = jnp.tanh(2.0994 * u - 2.0994 * 0.9087)
    hv2 = 1.0 + th_v
    nv2 = 1.0 - th_v
    hw2 = 1.0 + th_w
    nw2 = 1.0 - th_w
    no = 0.5 - 0.5 * th_o
    rate_v = 1.0 / (605.0 * per + (545.0 * per) * th_o)
    rate_w = 1.0 / (37.5 * per - (22.5 * per) * th_m)
    rate_so = 1.0 / (15.5069 * per - (14.5112 * per) * th_s)
    rate_s = 1.0 / (9.3671 * per + (6.6329 * per) * th_w)
    rate_o = 1.0 / (203.0 * per - (197.0 * per) * th_o)
    lead = STEP_TIME / 0.22
    open_v = hv2 * v
    w_inf = no * (0.06 - u * (1.0 / 0.07)) + 0.94
    du = (
        open_v * ((u - 0.3) * (1.55 * lead - lead * u))
        + hw2 * ((w * s) * (STEP_TIME / 3.775) - rate_so)
        - (u * nw2) * rate_o
    )
    v2 = v - open_v * (STEP_TIME / 2.9012) + (nv2 * rate_v) * (no - v)
    w2 = w - (hw2 * w) * (STEP_TIME / 400.0) + (nw2 * rate_w) * (w_inf - w)
    s2 = s + ((1.0 + th_r) - 2.0 * s) * rate_s
    return du, v2, w2, s2


def iota2(shape, dim):
    return lax.broadcasted_iota(jnp.int32, shape, dim)


def first_piola(f, active=None, fdir=None):
    second = {}
    for a in range(3):
        for b in range(a, 3):
            right = f[0][a] * f[0][b] + f[1][a] * f[1][b] + f[2][a] * f[2][b]
            second[a, b] = 0.5 * (right - (1.0 if a == b else 0.0))
    trace = second[0, 0] + second[1, 1] + second[2, 2]
    for a in range(3):
        if active is not None:
            scaled = 0.5 * active * fdir[a]
            for b in range(a, 3):
                second[a, b] = second[a, b] + scaled * fdir[b]
        second[a, a] = second[a, a] + trace
    for a in range(3):
        for b in range(a):
            second[a, b] = second[b, a]
    return [
        f[i][0] * second[0, a] + f[i][1] * second[1, a] + f[i][2] * second[2, a]
        for a in range(3)
        for i in range(3)
    ]


def metric(f, fdir):
    cof = [[None] * 3 for _ in range(3)]
    for i in range(3):
        for j in range(3):
            cof[i][j] = (
                f[(i + 1) % 3][(j + 1) % 3] * f[(i + 2) % 3][(j + 2) % 3]
                - f[(i + 1) % 3][(j + 2) % 3] * f[(i + 2) % 3][(j + 1) % 3]
            )
    det = f[0][0] * cof[0][0] + f[0][1] * cof[0][1] + f[0][2] * cof[0][2]
    scale = 1.0 / det
    inverse = [[cof[i][j] * scale for i in range(3)] for j in range(3)]
    g = [inverse[a][0] * fdir[0] + inverse[a][1] * fdir[1] + inverse[a][2] * fdir[2] for a in range(3)]
    comps = []
    for a, b in PAIRS:
        inner = (
            inverse[a][0] * inverse[b][0]
            + inverse[a][1] * inverse[b][1]
            + inverse[a][2] * inverse[b][2]
        )
        comps.append(SIGMA_TRANS * inner + (SIGMA_LONG - SIGMA_TRANS) * (g[a] * g[b]))
    return comps


class Stencils:
    def __init__(self, rows, width):
        self.rows, self.width = rows, width
        self.lane = iota2((rows, LANES), 1)
        self.line = iota2((TILE, width), 0)

    def left(self, f):
        parts, before = [], 0.0
        for x in range(0, self.width, LANES):
            here = f[:, x : x + LANES]
            parts.append(pltpu.roll(jnp.where(self.lane == LANES - 1, before, here), 1, 1))
            before = here
        return jnp.concatenate(parts, axis=1)

    def right(self, f):
        parts, after = [], 0.0
        for x in reversed(range(0, self.width, LANES)):
            here = f[:, x : x + LANES]
            parts.append(pltpu.roll(jnp.where(self.lane == 0, after, here), LANES - 1, 1))
            after = here
        return jnp.concatenate(parts[::-1], axis=1)

    def south(self, f):
        parts, before = [], 0.0
        for y in range(0, self.rows, TILE):
            here = f[y : y + TILE]
            parts.append(pltpu.roll(jnp.where(self.line == TILE - 1, before, here), 1, 0))
            before = here
        return jnp.concatenate(parts, axis=0)

    def north(self, f):
        parts, after = [], 0.0
        for y in reversed(range(0, self.rows, TILE)):
            here = f[y : y + TILE]
            parts.append(pltpu.roll(jnp.where(self.line == 0, after, here), TILE - 1, 0))
            after = here
        return jnp.concatenate(parts[::-1], axis=0)


    def sx(self, f):
        return self.left(f) + self.right(f) + 6.0 * f

    def dx(self, f):
        return self.right(f) - self.left(f)

    def sy(self, f):
        return self.south(f) + self.north(f) + 6.0 * f

    def dy(self, f):
        return self.north(f) - self.south(f)

    def deformation(self, field):
        f = []
        for i in range(3):
            low, mid, high = field(i, -1), field(i, 0), field(i, 1)
            zs = low + high + 6.0 * mid
            zd = high - low
            grads = [self.sy(self.sx(zd)), self.dy(self.sx(zs)), self.sy(self.dx(zs))]
            f.append([(1.0 / 128.0) * g for g in grads])
            f[i][i] = f[i][i] + 1.0
        return f

    def force(self, stress, i):
        zd = stress(i, 1) - stress(i, -1)
        ys = stress(3 + i, -1) + stress(3 + i, 1) + 6.0 * stress(3 + i, 0)
        xs = stress(6 + i, -1) + stress(6 + i, 1) + 6.0 * stress(6 + i, 0)
        return self.sy(self.sx(zd) + self.dx(xs)) + self.dy(self.sx(ys))


def sine(x, terms=6):
    y = x * x
    c = 1.0
    for n in range(2 * terms, 0, -2):
        c = 1.0 - y * (1.0 / (n * (n + 1))) * c
    return x * c


def cosine(x):
    y = x * x
    c = 1.0
    for n in (13, 11, 9, 7, 5, 3, 1):
        c = 1.0 - y * (1.0 / (n * (n + 1))) * c
    return c


def directions(index):
    theta = -1.0 + index * (2.0 / (NFIB - 1))
    triple = 3.0 * index
    turns = jnp.floor(triple * (0.5 / np.pi) + 0.5)
    triple = (triple - turns * 6.28125) - turns * (2.0 * np.pi - 6.28125)
    tilt = 0.3 * sine(triple, 10)
    flat = cosine(tilt)
    return [sine(tilt), flat * sine(theta), flat * cosine(theta)]


def halves(x):
    high = x.astype(BF16)
    return high, (x - high.astype(F32)).astype(BF16)


def excite_kernel(
    slabs, states, cond_hbm, ten_hbm, fib_hbm, disp_hbm,
    out_hbm, ten_out, act_hbm, shift_hbm, pull_hbm,
    ubuf, out, cond, tension, coeff, dif, act_win, zeros, fix_win, fiber, passive, shifted, pull, pooled,
    load_sem, store_sem, sz, rz, sc, rc, sy, ry, sa, ra, sf, rf, sg, relay, sv, rv,
):
    grp = lax.axis_index("grp")
    slab = lax.axis_index("slab")
    col = lax.axis_index("col")
    other = 1 - col
    depth, rows, width = out.shape[1:]
    tiles = rows // TILE
    has_up = slab < slabs - 1
    has_dn = slab > 0
    edge_src = rows - (rows - TILE) * col
    edge_dst = (rows + TILE) * col

    load_u = pltpu.make_async_copy(
        states.at[0], ubuf.at[0, pl.ds(1, depth), pl.ds(TILE, rows), :], load_sem.at[0]
    )
    load_g = pltpu.make_async_copy(
        states.at[pl.ds(1, 3)], out.at[pl.ds(1, 3)], load_sem.at[1]
    )
    load_c = pltpu.make_async_copy(cond_hbm, cond, load_sem.at[2])
    load_t = pltpu.make_async_copy(ten_hbm, tension, load_sem.at[3])
    load_u.start()
    load_c.start()
    load_g.start()
    load_t.start()
    half = rows // 4
    span = half + TILE
    own = pl.ds(pl.multiple_of(TILE * col, TILE), half)
    near = pl.ds(TILE, TILE)
    far = pl.ds(pl.multiple_of(2 * TILE * col, TILE), TILE)
    load_d = pltpu.make_async_copy(
        disp_hbm.at[:, 0], fix_win.at[RADIUS, pl.ds(0, 3), own, :], load_sem.at[4]
    )
    load_f = pltpu.make_async_copy(fib_hbm, fiber, load_sem.at[5])
    load_d.start()
    load_f.start()

    barrier = pltpu.get_barrier_semaphore()

    def greet(where):
        pl.semaphore_signal(barrier, inc=1, device_id=where, device_id_type=MESH)

    def there(d):
        return (slab + d >= 0) & (slab + d < slabs)

    peers = 0
    for d in PEERS:
        valid = there(d)
        wide = abs(d) <= REACH
        count = (0 if d == 0 else 1) + (1 if wide else 0)
        peers = peers + count * valid.astype(jnp.int32)

        @pl.when(valid)
        def _(d=d, wide=wide):
            if wide:
                greet((grp, slab + d, other))
            if d != 0:
                greet((grp, slab + d, col))

    zeros[...] = jnp.zeros(zeros.shape, F32)

    def blank_a(d):
        return pltpu.make_async_copy(zeros, act_hbm.at[d + REACH], ra.at[d + REACH, 0])

    for d in range(-RADIUS, RADIUS + 1):

        @pl.when(jnp.logical_not(there(d)))
        def _(d=d):
            fix_win[d + RADIUS] = jnp.zeros(fix_win.shape[1:], F32)
            if abs(d) <= REACH:
                blank_a(d).start()

    blank = jnp.zeros((TILE, width), F32)

    def clear_y(n, c):
        ubuf[n // (depth + 2), n % (depth + 2), pl.ds(pl.multiple_of(edge_dst, TILE), TILE), :] = blank
        return c

    lax.fori_loop(0, SUB * (depth + 2), clear_y, 0)

    def clear_z(layer):
        per = rows // TILE + 2

        def body(n, c):
            ubuf[n // per, layer, pl.ds(pl.multiple_of((n % per) * TILE, TILE), TILE), :] = blank
            return c

        lax.fori_loop(0, SUB * per, body, 0)

    @pl.when(slab == 0)
    def _():
        clear_z(0)

    @pl.when(slab == slabs - 1)
    def _():
        clear_z(depth + 1)

    def row_of(step):
        return jnp.where(col == 1, step, tiles - 1 - step)

    def copy_z(slot, way, step):
        at = pl.ds(pl.multiple_of(TILE + TILE * row_of(step), TILE), TILE)
        src = depth if way == 0 else 1
        dst = 0 if way == 0 else depth + 1
        to = slab + 1 if way == 0 else slab - 1
        return pltpu.make_async_remote_copy(
            src_ref=ubuf.at[slot, src, at, :],
            dst_ref=ubuf.at[slot, dst, at, :],
            send_sem=sz.at[way],
            recv_sem=rz.at[slot, way, step],
            device_id=(grp, to, col),
            device_id_type=MESH,
        )

    def carried(step, count):
        return lax.rem((step + 1) * count, tiles) < count

    beside = 1 - 2 * lax.rem(slab, 2)
    chips = slabs // 2
    upper = tiles * (chips - 1 - slab // 2) // chips
    lower = tiles * (slab // 2) // chips
    even = beside == 1
    mine = jnp.where(even, lower, upper)
    others = jnp.where(even, upper, lower)
    onward = 1 - lax.rem(slab + 1, 2)

    def copy_via(slot, way, step):
        at = pl.ds(pl.multiple_of(TILE + TILE * row_of(step), TILE), TILE)
        to = pl.ds(pl.multiple_of(TILE * row_of(step), TILE), TILE)
        return pltpu.make_async_remote_copy(
            src_ref=ubuf.at[slot, depth if way == 0 else 1, at, :],
            dst_ref=relay.at[slot, to, :],
            send_sem=sz.at[way],
            recv_sem=rv.at[slot, step],
            device_id=(grp, slab + beside, col),
            device_id_type=MESH,
        )

    def copy_on(slot, step):
        at = pl.ds(pl.multiple_of(TILE * row_of(step), TILE), TILE)
        to = pl.ds(pl.multiple_of(TILE + TILE * row_of(step), TILE), TILE)
        return pltpu.make_async_remote_copy(
            src_ref=relay.at[slot, at, :],
            dst_ref=ubuf.at[slot, onward * (depth + 1), to, :],
            send_sem=sv.at[slot, step],
            recv_sem=rz.at[slot, onward, step],
            device_id=(grp, slab + 2 * beside, col),
            device_id_type=MESH,
        )

    def hand_on(n):
        @pl.when((n < SUB * tiles) & carried(n % tiles, others))
        def _():
            copy_via(n // tiles, 0, n % tiles).wait_recv()
            copy_on(n // tiles, n % tiles).start()

    def copy_c(slot, way):
        at = depth + 1 if way == 0 else 0
        return pltpu.make_async_remote_copy(
            src_ref=ubuf.at[slot, at, pl.ds(pl.multiple_of(edge_src, TILE), TILE), :],
            dst_ref=ubuf.at[slot, at, pl.ds(pl.multiple_of(edge_dst, TILE), TILE), :],
            send_sem=sc.at[way],
            recv_sem=rc.at[slot, way],
            device_id=(grp, slab, other),
            device_id_type=MESH,
        )

    def copy_y(slot):
        return pltpu.make_async_remote_copy(
            src_ref=ubuf.at[slot, pl.ds(1, depth), pl.ds(pl.multiple_of(edge_src, TILE), TILE), :],
            dst_ref=ubuf.at[slot, pl.ds(1, depth), pl.ds(pl.multiple_of(edge_dst, TILE), TILE), :],
            send_sem=sy.at[0],
            recv_sem=ry.at[slot],
            device_id=(grp, slab, other),
            device_id_type=MESH,
        )

    def both(do_up, do_dn):
        pl.when(has_up)(do_up)
        pl.when(has_dn)(do_dn)

    def send_z(n, by_partner):
        slot = n // tiles
        step = n % tiles
        via = carried(step, mine)

        def send(way):
            through = via & (jnp.logical_not(even) if way == 0 else even)
            if by_partner:
                pl.when(through)(lambda: copy_via(slot, way, step).start())
            else:
                pl.when(jnp.logical_not(through))(lambda: copy_z(slot, way, step).start())

        @pl.when(n < SUB * tiles)
        def _():
            both(lambda: send(0), lambda: send(1))

    def send_c(slot):
        both(lambda: copy_c(slot, 0).start(), lambda: copy_c(slot, 1).start())

    def recv_z(slot, step):
        both(lambda: copy_z(slot, 1, step).wait_recv(), lambda: copy_z(slot, 0, step).wait_recv())

    def recv_c(slot):
        both(lambda: copy_c(slot, 0).wait_recv(), lambda: copy_c(slot, 1).wait_recv())

    def copy_f(source, d, n):
        slot = RADIUS + source - d
        return pltpu.make_async_remote_copy(
            src_ref=fix_win.at[RADIUS + source, :, own, :],
            dst_ref=fix_win.at[slot, :, own, :],
            send_sem=sf.at[n],
            recv_sem=rf.at[slot],
            device_id=(grp, slab + d, col),
            device_id_type=MESH,
        )

    def come_f(e):
        return pltpu.make_async_remote_copy(
            src_ref=fix_win.at[RADIUS, :, own, :],
            dst_ref=fix_win.at[RADIUS + e, :, own, :],
            send_sem=sf.at[0],
            recv_sem=rf.at[RADIUS + e],
            device_id=(grp, slab + e, col),
            device_id_type=MESH,
        )

    def share_f(whose):
        return pltpu.make_async_remote_copy(
            src_ref=fix_win.at[:, :, near, :],
            dst_ref=fix_win.at[:, :, pl.ds(pl.multiple_of(2 * TILE * whose, TILE), TILE), :],
            send_sem=sg.at[0],
            recv_sem=sg.at[1],
            device_id=(grp, slab, other),
            device_id_type=MESH,
        )

    def forward_f(act):
        for n, d in enumerate(BEYOND):
            ok = there(d) & (jnp.abs(d - beside) <= RADIUS)
            pl.when(ok)(lambda n=n, d=d: act(n, d))

    def relay_f(n, d):
        return copy_f(beside, d, 1 + len(ALONG) + n)

    pl.semaphore_wait(barrier, peers)

    load_u.wait()
    send_z(0, True)
    send_z(0, False)
    copy_y(0).start()
    send_z(1, True)
    send_z(1, False)
    load_d.wait()
    load_f.wait()
    fix_win[RADIUS, 3, own, :] = fiber[0].astype(F32)
    copy_f(0, beside, 0).start()
    for n, d in enumerate(ALONG):
        pl.when(there(d))(lambda n=n, d=d: copy_f(0, d, 1 + n).start())

    def initial(step, c):
        send_z(step, True)
        pl.when(step < tiles - HOLD)(lambda: send_z(step, False))
        return c

    lax.fori_loop(2, tiles, initial, 0)
    load_c.wait()

    spread_x = (iota2((256, 512), 0) % 128 == iota2((256, 512), 1) // 4).astype(BF16)
    spread_y = (iota2((rows, rows // 4), 0) // 4 == iota2((rows, rows // 4), 1)).astype(BF16)
    for c in range(6):
        tall = [
            jnp.dot(spread_y, part, preferred_element_type=F32).astype(BF16)
            for part in halves(cond[c, 0])
        ]
        for h in range(width // 512):
            part = jnp.concatenate([t[:, h * 128 : (h + 1) * 128] for t in tall], axis=1)
            part = jnp.dot(part, spread_x, preferred_element_type=F32)
            coeff[c, :, h * 512 : (h + 1) * 512] = part if c < 3 else 0.5 * part

    def centre_weight(t, c):
        at = pl.ds(pl.multiple_of(TILE * t, TILE), TILE)
        coeff[6, at, :] = 1.0 - 2.0 * (coeff[0, at, :] + coeff[1, at, :] + coeff[2, at, :])
        return c

    lax.fori_loop(0, tiles, centre_weight, 0)

    load_g.wait()
    load_t.wait()

    lane = iota2((TILE, width), 1)

    def left(f):
        return jnp.where(lane == 0, 0.0, pltpu.roll(f, 1, 1))

    def right(f):
        return jnp.where(lane == width - 1, 0.0, pltpu.roll(f, width - 1, 1))

    line = iota2((TILE, width), 0)

    def north_south(tall):
        here = tall[TILE : 2 * TILE]
        return (
            pltpu.roll(jnp.where(line == 0, tall[2 * TILE :], here), TILE - 1, 0),
            pltpu.roll(jnp.where(line == TILE - 1, tall[:TILE], here), 1, 0),
        )

    def layer(k, z, r):
        base = pl.multiple_of(TILE * r, TILE)
        here = pl.ds(base, TILE)
        tall = pl.ds(base, 3 * TILE)
        below = ubuf[k, z, tall, :]
        mid = ubuf[k, z + 1, tall, :]
        above = ubuf[k, z + 2, tall, :]
        odd = above - below
        centre = mid[TILE : 2 * TILE]
        odd0 = odd[TILE : 2 * TILE]
        north, south = north_south(mid)
        odd_north, odd_south = north_south(odd)
        slope = north - south
        total = coeff[6, here, :] * centre
        total = total + coeff[0, here, :] * (above[TILE : 2 * TILE] + below[TILE : 2 * TILE])
        total = total + coeff[1, here, :] * (north + south)
        total = total + coeff[2, here, :] * (right(centre) + left(centre))
        total = total + coeff[3, here, :] * (odd_north - odd_south)
        total = total + coeff[4, here, :] * (right(odd0) - left(odd0))
        total = total + coeff[5, here, :] * (right(slope) - left(slope))
        dif[...] = total
        up = pl.ds(pl.multiple_of(base + TILE, TILE), TILE)
        for x in range(0, width, CHUNK):
            xs = pl.ds(x, CHUNK)
            du, v2, w2, s2 = ionic(
                ubuf[k, z + 1, up, xs], out[1, z, here, xs], out[2, z, here, xs],
                out[3, z, here, xs],
            )
            u2 = dif[:, xs] + du
            ubuf[k + 1, z + 1, up, xs] = u2
            out[0, z, here, xs] = u2
            out[1, z, here, xs] = v2
            out[2, z, here, xs] = w2
            out[3, z, here, xs] = s2

    def leave(step):
        at = pl.ds(pl.multiple_of(TILE * row_of(step), TILE), TILE)
        return pltpu.make_async_copy(
            out.at[:, :, at, :], out_hbm.at[:, :, at, :], store_sem.at[step]
        )

    pair_x = (iota2((256, 128), 0) // 2 == iota2((256, 128), 1)).astype(F32)
    pair_2 = (iota2((512, 128), 0) % 256 // 2 == iota2((512, 128), 1)).astype(BF16)
    pair_y2 = (iota2((half, 2 * half), 0) == iota2((half, 2 * half), 1) // 2).astype(F32)

    def pool_lanes(rows_in, weights, size, chunk):
        parts = halves(rows_in)
        for h in range(width // chunk):
            both_halves = jnp.concatenate(
                [part[:, h * chunk : (h + 1) * chunk] for part in parts], axis=1
            )
            pooled[h, 0:size] = jnp.dot(both_halves, weights, preferred_element_type=F32)

    def tense(p):
        fine = pl.ds(pl.multiple_of(2 * TILE * p, 2 * TILE), 2 * TILE)
        wide = pl.ds(pl.multiple_of(TILE * p, TILE), TILE)
        sums = []
        for q in range(depth // 2):
            layers = out[0, 2 * q, fine, :] + out[0, 2 * q + 1, fine, :]
            sums.append(layers + pltpu.roll(layers, 2 * TILE - 1, 0))
        pool_lanes(0.125 * jnp.concatenate(sums, axis=0), pair_2, TILE * depth, 256)
        for h in range(width // 256):
            xo = slice(h * 128, (h + 1) * 128)
            for q in range(depth // 2):
                mean = pooled[h, pl.ds(2 * TILE * q, TILE, 2), :]
                before = tension[q, wide, xo]
                tension[q, wide, xo] = before + 0.5 * (mean - before)

    pool_x = (iota2((1024, 128), 0) % 512 // 4 == iota2((1024, 128), 1)).astype(BF16)

    def activate(part, lines):
        fine = pl.ds(pl.multiple_of(4 * TILE * part, 4 * TILE), 4 * TILE)
        layers = out[0, 0, fine, :]
        for z in range(1, depth):
            layers = layers + out[0, z, fine, :]
        layers = layers + pltpu.roll(layers, 4 * TILE - 1, 0)
        layers = layers + pltpu.roll(layers, 4 * TILE - 2, 0)
        pool_lanes((0.5 / (16 * depth)) * layers, pool_x, 4 * TILE, 512)
        for h in range(width // 512):
            xo = slice(h * 128, (h + 1) * 128)
            act_win[lines, xo] = act_win[lines, xo] + pooled[h, pl.ds(0, TILE, 4), :]

    def copy_a(d, to, kind, lines, at):
        return pltpu.make_async_remote_copy(
            src_ref=act_win.at[lines, :],
            dst_ref=act_hbm.at[REACH - d, at, :],
            send_sem=sa.at[d + REACH, kind],
            recv_sem=ra.at[REACH - d, kind],
            device_id=(grp, slab + d, to),
            device_id_type=MESH,
        )

    def keep_a(kind, lines):
        return pltpu.make_async_copy(
            act_win.at[lines, :], act_hbm.at[REACH, lines, :], sa.at[REACH, kind]
        )

    def each_a(act, centre):
        for d in sorted(range(-REACH, REACH + 1), key=lambda d: -abs(d)):
            if d != 0 or centre:
                pl.when(there(d))(lambda d=d: act(d))

    mech = Stencils(span, fix_win.shape[3])

    def inside(j):
        return there(j - RADIUS)

    def prepare(j):
        ok = inside(j)
        f = mech.deformation(lambda i, d: fix_win[j + d, i])
        fdir = directions(fix_win[j, 3])
        pieces = first_piola(f)
        for n in range(9):
            passive[n, j - 1] = jnp.where(ok, pieces[n], 0.0)
        for i in range(3):
            g = 0.5 * (f[i][0] * fdir[0] + f[i][1] * fdir[1] + f[i][2] * fdir[2])
            pull[i, j - 1] = jnp.where(ok, g, 0.0)
            pull[3 + i, j - 1] = fdir[i]

    def shift(j):
        ok = inside(j)
        for i in range(3):
            force = mech.force(lambda n, d: passive[n, j - 1 + d], i)
            moved = fix_win[j, i] + (MECH_RATE / 128.0) * force
            shifted[i, j - 2] = jnp.where(ok, moved, 0.0)

    hand_shift = pltpu.make_async_copy(shifted, shift_hbm, load_sem.at[0])
    hand_pull = pltpu.make_async_copy(pull, pull_hbm, load_sem.at[1])

    for h in range(width // 512):
        xs = slice(h * 256, (h + 1) * 256)
        layers = tension[0, :, xs] + tension[1, :, xs]
        mean = jnp.dot(layers, pair_x, precision=HI, preferred_element_type=F32)
        mean = 0.0625 * jnp.dot(pair_y2, mean, precision=HI, preferred_element_type=F32)
        act_win[own, h * 128 : (h + 1) * 128] = mean

    def within(n):
        k = n // tiles
        r = row_of(n % tiles)

        def inner(m, c):
            layer(k, m, r)
            return c

        lax.fori_loop(1, depth - 1, inner, 0)

    recv_z(0, 0)
    send_c(0)
    copy_y(0).wait_recv()
    within(0)

    def chunk(n, c):
        k = n // tiles
        step = n % tiles
        r = row_of(step)

        @pl.when(n < LAG - 1)
        def _():
            hand_on(2 * n + 1)
            hand_on(2 * n + 2)

        pl.when(n >= LAG - 1)(lambda: hand_on(n + LAG))

        @pl.when(n == tiles // 2)
        def _():
            come_f(beside).wait_recv()

        for far_by in (2, 4, 6):

            @pl.when(n == tiles // 2 + far_by // 2 - 1)
            def _(far_by=far_by):
                forward_f(lambda n, d: relay_f(n, d).start() if abs(d) == far_by else None)

        @pl.when(n == JOIN)
        def _():
            for d in range(-RADIUS, RADIUS + 1):
                if d != 0:
                    arrives = there(d) if d % 2 == 0 else there(d) & (beside != d)
                    pl.when(arrives)(lambda d=d: come_f(d).wait_recv())
            share_f(col).start()

        @pl.when(n == JOIN + 2)
        def _():
            share_f(col).wait_recv()

        @pl.when(step < tiles - 1)
        def _():
            recv_z(k, step + 1)

        @pl.when(step == 0)
        def _():
            recv_c(k)

        def outer(m, c):
            layer(k, m * (depth - 1), r)
            return c

        lax.fori_loop(0, 2, outer, 0)

        send_z(n + tiles, True)
        send_z(n + tiles - HOLD, False)

        @pl.when((k < SUB - 1) & (step == 0))
        def _():
            copy_y(k + 1).start()

        @pl.when((k < SUB - 1) & (step == tiles - 1))
        def _():
            recv_z(k + 1, 0)
            send_c(k + 1)
            copy_y(k + 1).wait_recv()

        @pl.when(n < SUB * tiles - 1)
        def _():
            within(n + 1)

        turn = n - JOIN - 2
        stress_turn = (turn < 2) | (turn % 2 == 0)

        @pl.when((turn >= 0) & (turn < LAST) & stress_turn)
        def _():
            prepare(jnp.where(turn < 2, turn + 1, turn // 2 + 2))

        @pl.when((turn >= 3) & (turn < LAST) & jnp.logical_not(stress_turn))
        def _():
            shift((turn + 1) // 2)

        @pl.when(turn == LAST)
        def _():
            hand_shift.start()
            hand_pull.start()

        @pl.when(k == SUB - 1)
        def _():
            leave(step).start()

        @pl.when(n == SUB * tiles - 1 - tiles // 2)
        def _():
            activate(other, near)
            each_a(lambda d: copy_a(d, col, 0, near, near).start(), False)
            each_a(lambda d: copy_a(d, other, 1, near, far).start(), True)
            keep_a(0, near).start()

        @pl.when((k == SUB - 1) & (step % 2 == 1) & (step < tiles - 1))
        def _():
            tense(r // 2)

        return c

    lax.fori_loop(0, SUB * tiles, chunk, 0)

    activate(col, far)
    each_a(lambda d: copy_a(d, col, 2, far, far).start(), False)
    keep_a(2, far).start()
    tense(row_of(tiles - 1) // 2)
    hand_ten = pltpu.make_async_copy(tension, ten_out, load_sem.at[2])
    hand_ten.start()
    share_f(col).wait_send()
    copy_f(0, beside, 0).wait_send()
    for n, d in enumerate(ALONG):
        pl.when(there(d))(lambda n=n, d=d: copy_f(0, d, 1 + n).wait_send())
    forward_f(lambda n, d: relay_f(n, d).wait_send())
    hand_shift.wait()
    hand_pull.wait()
    def sent(what, sem):
        pltpu.make_async_remote_copy(
            src_ref=what, dst_ref=what, send_sem=sem, recv_sem=sg.at[1],
            device_id=(grp, slab, other), device_id_type=MESH,
        ).wait_send()

    both(lambda: sent(relay, sz.at[0]), lambda: sent(relay, sz.at[1]))
    corners = ubuf.at[0, pl.ds(0, SUB), pl.ds(0, TILE), :]
    both(lambda: sent(corners, sc.at[0]), lambda: sent(corners, sc.at[1]))
    sent(ubuf.at[pl.ds(0, SUB), pl.ds(1, depth), pl.ds(0, TILE), :], sy.at[0])

    def drain(n, c):
        pl.when(carried(n % tiles, others))(lambda: copy_on(n // tiles, n % tiles).wait_send())
        return c

    lax.fori_loop(0, SUB * tiles, drain, 0)

    def left_all(step, c):
        leave(step).wait()
        return c

    lax.fori_loop(0, tiles, left_all, 0)
    each_a(lambda d: copy_a(d, col, 0, near, near).wait_send(), False)
    each_a(lambda d: copy_a(d, other, 1, near, far).wait_send(), True)
    each_a(lambda d: copy_a(d, col, 2, far, far).wait_send(), False)
    for d in range(-REACH, REACH + 1):
        pl.when(jnp.logical_not(there(d)))(lambda d=d: blank_a(d).wait())
    each_a(lambda d: copy_a(-d, col, 0, near, near).wait_recv(), False)
    each_a(lambda d: copy_a(-d, other, 1, near, far).wait_recv(), True)
    each_a(lambda d: copy_a(-d, col, 2, far, far).wait_recv(), False)
    hand_ten.wait()
    keep_a(0, near).wait()
    keep_a(2, far).wait()


def excite(slabs, states, cond, tension, fiber, disp):
    _, depth, rows, width = states.shape
    tiles = rows // TILE
    full = rows // 4 + TILE
    across = cond.shape[3]
    hbm = pl.BlockSpec(memory_space=pltpu.HBM)
    window = (2 * REACH + 1, full, across)
    shifts = (3, 2 * REACH - 1, full, across)
    pulls = (6, 2 * REACH + 1, full, across)
    dma = pltpu.SemaphoreType.DMA
    return pl.pallas_call(
        functools.partial(excite_kernel, slabs),
        out_shape=(
            jax.ShapeDtypeStruct(states.shape, F32),
            jax.ShapeDtypeStruct(tension.shape, F32),
            jax.ShapeDtypeStruct(window, F32),
            jax.ShapeDtypeStruct(shifts, F32),
            jax.ShapeDtypeStruct(pulls, F32),
        ),
        in_specs=[hbm, hbm, hbm, hbm, hbm],
        out_specs=(hbm, hbm, hbm, hbm, hbm),
        scratch_shapes=[
            pltpu.VMEM((SUB + 1, depth + 2, rows + 2 * TILE, width), F32),
            pltpu.VMEM(states.shape, F32),
            pltpu.VMEM(cond.shape, F32),
            pltpu.VMEM(tension.shape, F32),
            pltpu.VMEM((7, rows, width), F32),
            pltpu.VMEM((TILE, width), F32),
            pltpu.VMEM(window[1:], F32),
            pltpu.VMEM(window[1:], F32),
            pltpu.VMEM((2 * RADIUS + 1, 4, full, across), F32),
            pltpu.VMEM(fiber.shape, jnp.int32),
            pltpu.VMEM((9, *window), F32),
            pltpu.VMEM(shifts, F32),
            pltpu.VMEM(pulls, F32),
            pltpu.VMEM((width // 256, 4 * TILE, 128), F32),
            dma((6,)),
            dma((tiles,)),
            dma((2,)),
            dma((SUB, 2, tiles)),
            dma((2,)),
            dma((SUB, 2)),
            dma((1,)),
            dma((SUB,)),
            dma((2 * REACH + 1, 3)),
            dma((2 * REACH + 1, 3)),
            dma((1 + len(ALONG) + len(BEYOND),)),
            dma((2 * RADIUS + 1,)),
            dma((2,)),
            pltpu.VMEM((SUB, rows, width), F32),
            dma((SUB, tiles)),
            dma((SUB, tiles)),
        ],
        compiler_params=pltpu.CompilerParams(
            collective_id=0, has_side_effects=True, vmem_limit_bytes=61 << 20
        ),
        cost_estimate=pl.CostEstimate(
            flops=200_000_000, bytes_accessed=16 << 20, transcendentals=6_000_000
        ),
        name="excite",
    )(states, cond, tension, fiber, disp)


def mech_kernel(
    slabs, act_hbm, shift_hbm, pull_hbm, ten_in, states_in,
    disp_hbm, cond_hbm, ten_out, states_out,
    disp_out, cond_out, active, shifted, pull, stress, moved, held, tension, sem,
):
    slab = lax.axis_index("slab")
    first = lax.axis_index("col") == 0
    rows, width = active.shape[1:]
    half = rows - TILE
    load_a = pltpu.make_async_copy(act_hbm, active, sem.at[0])
    load_p = pltpu.make_async_copy(pull_hbm, pull, sem.at[1])
    load_s = pltpu.make_async_copy(shift_hbm, shifted, sem.at[2])
    load_a.start()
    load_p.start()
    load_s.start()
    fetch = [pltpu.make_async_copy(ten_in, tension, sem.at[3])]
    pass_on = [pltpu.make_async_copy(tension, ten_out, sem.at[8])]
    for n in range(4):
        fetch.append(pltpu.make_async_copy(states_in.at[n], held.at[n], sem.at[4 + n]))
        pass_on.append(pltpu.make_async_copy(held.at[n], states_out.at[n], sem.at[9 + n]))
    for copy in fetch:
        copy.start()
    mech = Stencils(rows, width)

    def inside(j):
        zz = slab + j - REACH
        return (zz >= 0) & (zz < slabs)

    def tense(j, c):
        for a in range(3):
            t = active[j] * pull[3 + a, j]
            for i in range(3):
                stress[3 * a + i, j] = t * pull[i, j]
        return c

    def move(field):
        def body(j, c):
            ok = inside(j)
            for i in range(3):
                force = mech.force(lambda n, d: stress[n, j + d], i)
                moved[i, j] = jnp.where(ok, field(i, j) + (MECH_RATE / 128.0) * force, 0.0)
            return c

        return body

    def strain(j, c):
        ok = inside(j)
        f = mech.deformation(lambda i, d: moved[i, j + d])
        pieces = first_piola(f, active[j], [pull[3 + a, j] for a in range(3)])
        for n in range(9):
            stress[n, j] = jnp.where(ok, pieces[n], 0.0)
        return c

    load_a.wait()
    load_p.wait()
    for j in range(2 * REACH + 1):
        tense(j, 0)
    load_s.wait()
    for j in range(1, 2 * REACH):
        move(lambda i, j: shifted[i, j - 1])(j, 0)
    for got, copy in zip(fetch, pass_on):
        got.wait()
        copy.start()
    for j in range(2, 2 * REACH - 1):
        strain(j, 0)
    for j in range(3, 2 * REACH - 2):
        move(lambda i, j: moved[i, j])(j, 0)

    for i in range(3):
        whole = moved[i, REACH]
        disp_out[i, 0] = jnp.where(first, whole[:half], whole[TILE:])
    store_d = pltpu.make_async_copy(disp_out, disp_hbm, sem.at[0])
    store_d.start()
    comps = metric(
        mech.deformation(lambda i, d: moved[i, REACH + d]),
        [pull[3 + a, REACH] for a in range(3)],
    )
    for n in range(6):
        cond_out[n, 0] = jnp.where(first, comps[n][:half], comps[n][TILE:])
    store_c = pltpu.make_async_copy(cond_out, cond_hbm, sem.at[1])
    store_c.start()
    store_d.wait()
    for copy in pass_on:
        copy.wait()
    store_c.wait()


def mechanics(slabs, active, shifted, pull, tension, states):
    _, full, width = active.shape
    rows = full - TILE
    hbm = pl.BlockSpec(memory_space=pltpu.HBM)
    return pl.pallas_call(
        functools.partial(mech_kernel, slabs),
        out_shape=(
            jax.ShapeDtypeStruct((3, 1, rows, width), F32),
            jax.ShapeDtypeStruct((6, 1, rows, width), F32),
            jax.ShapeDtypeStruct(tension.shape, F32),
            jax.ShapeDtypeStruct(states.shape, F32),
        ),
        in_specs=[hbm, hbm, hbm, hbm, hbm],
        out_specs=(hbm, hbm, hbm, hbm),
        scratch_shapes=[
            pltpu.VMEM((3, 1, rows, width), F32),
            pltpu.VMEM((6, 1, rows, width), F32),
            pltpu.VMEM(active.shape, F32),
            pltpu.VMEM(shifted.shape, F32),
            pltpu.VMEM(pull.shape, F32),
            pltpu.VMEM((9, 2 * REACH + 1, full, width), F32),
            pltpu.VMEM((3, 2 * REACH + 1, full, width), F32),
            pltpu.VMEM(states.shape, F32),
            pltpu.VMEM(tension.shape, F32),
            pltpu.SemaphoreType.DMA((13,)),
        ],
        compiler_params=pltpu.CompilerParams(vmem_limit_bytes=61 << 20),
        name="mechanics",
    )(active, shifted, pull, tension, states)


def on_device(slabs, states, cond, tension, fiber, disp):
    states_next, tension_next, active, shifted, pull = excite(
        slabs, states, cond, tension, fiber, disp
    )
    disp_next, cond_next, tension_next, states_next = mechanics(
        slabs, active, shifted, pull, tension_next, states_next
    )
    return states_next, tension_next, disp_next, cond_next


def solution(mesh):
    wide = P(None, ("grp", "slab"), "col", None)
    flat = P(("grp", "slab"), "col", None)
    return jax.shard_map(
        functools.partial(on_device, mesh.shape["slab"]),
        mesh=mesh,
        in_specs=(wide, wide, flat, flat, wide),
        out_specs=(wide, flat, wide, wide),
        check_vma=False,
    )
```

```python
import functools

import jax
import jax.numpy as jnp
import numpy as np
from jax import lax
from jax.experimental import pallas as pl
from jax.experimental.pallas import tpu as pltpu
from jax.sharding import PartitionSpec as P

SUB = 4
MECH_STEPS = 2
NFIB = 64
STEP_TIME = 0.05
MECH_RATE = 0.15
SIGMA_LONG = 0.16
SIGMA_TRANS = 0.04
PAIRS = ((0, 0), (1, 1), (2, 2), (0, 1), (0, 2), (1, 2))
MESH = pl.DeviceIdType.MESH
HI = lax.Precision.HIGHEST
F32 = jnp.float32
BF16 = jnp.bfloat16
TILE = 8
LANES = 128
CHUNK = 256
RADIUS = 2 * MECH_STEPS + 1
REACH = RADIUS - 1
ALONG = (-4, -2, 2, 4)
BEYOND = (-6, -4, -2, 2, 4, 6)
PEERS = (-6, -4, -3, -2, -1, 0, 1, 2, 3, 4, 6)
JOIN = 10
LAST = 4 * REACH
LAG = 4
HOLD = 2


def ionic(u, v, w, s):
    per = 2.0 / STEP_TIME
    steep = 50.0 * u
    th_v = jnp.tanh(steep - 50.0 * 0.3)
    th_w = jnp.tanh(steep - 50.0 * 0.13)
    th_o = jnp.tanh(steep - 50.0 * 0.006)
    th_m = jnp.tanh(65.0 * u - 65.0 * 0.03)
    th_s = jnp.tanh(2.0458 * u - 2.0458 * 0.65)
    th_r = jnp.tanh(2.0994 * u - 2.0994 * 0.9087)
    hv2 = 1.0 + th_v
    nv2 = 1.0 - th_v
    hw2 = 1.0 + th_w
    nw2 = 1.0 - th_w
    no = 0.5 - 0.5 * th_o
    rate_v = 1.0 / (605.0 * per + (545.0 * per) * th_o)
    rate_w = 1.0 / (37.5 * per - (22.5 * per) * th_m)
    rate_so = 1.0 / (15.5069 * per - (14.5112 * per) * th_s)
    rate_s = 1.0 / (9.3671 * per + (6.6329 * per) * th_w)
    rate_o = 1.0 / (203.0 * per - (197.0 * per) * th_o)
    lead = STEP_TIME / 0.22
    open_v = hv2 * v
    w_inf = no * (0.06 - u * (1.0 / 0.07)) + 0.94
    du = (
        open_v * ((u - 0.3) * (1.55 * lead - lead * u))
        + hw2 * ((w * s) * (STEP_TIME / 3.775) - rate_so)
        - (u * nw2) * rate_o
    )
    v2 = v - open_v * (STEP_TIME / 2.9012) + (nv2 * rate_v) * (no - v)
    w2 = w - (hw2 * w) * (STEP_TIME / 400.0) + (nw2 * rate_w) * (w_inf - w)
    s2 = s + ((1.0 + th_r) - 2.0 * s) * rate_s
    return du, v2, w2, s2


def iota2(shape, dim):
    return lax.broadcasted_iota(jnp.int32, shape, dim)


def first_piola(f, active=None, fdir=None):
    second = {}
    for a in range(3):
        for b in range(a, 3):
            right = f[0][a] * f[0][b] + f[1][a] * f[1][b] + f[2][a] * f[2][b]
            second[a, b] = 0.5 * (right - (1.0 if a == b else 0.0))
    trace = second[0, 0] + second[1, 1] + second[2, 2]
    for a in range(3):
        if active is not None:
            scaled = 0.5 * active * fdir[a]
            for b in range(a, 3):
                second[a, b] = second[a, b] + scaled * fdir[b]
        second[a, a] = second[a, a] + trace
    for a in range(3):
        for b in range(a):
            second[a, b] = second[b, a]
    return [
        f[i][0] * second[0, a] + f[i][1] * second[1, a] + f[i][2] * second[2, a]
        for a in range(3)
        for i in range(3)
    ]


def metric(f, fdir):
    cof = [[None] * 3 for _ in range(3)]
    for i in range(3):
        for j in range(3):
            cof[i][j] = (
                f[(i + 1) % 3][(j + 1) % 3] * f[(i + 2) % 3][(j + 2) % 3]
                - f[(i + 1) % 3][(j + 2) % 3] * f[(i + 2) % 3][(j + 1) % 3]
            )
    det = f[0][0] * cof[0][0] + f[0][1] * cof[0][1] + f[0][2] * cof[0][2]
    scale = 1.0 / det
    inverse = [[cof[i][j] * scale for i in range(3)] for j in range(3)]
    g = [inverse[a][0] * fdir[0] + inverse[a][1] * fdir[1] + inverse[a][2] * fdir[2] for a in range(3)]
    comps = []
    for a, b in PAIRS:
        inner = (
            inverse[a][0] * inverse[b][0]
            + inverse[a][1] * inverse[b][1]
            + inverse[a][2] * inverse[b][2]
        )
        comps.append(SIGMA_TRANS * inner + (SIGMA_LONG - SIGMA_TRANS) * (g[a] * g[b]))
    return comps


class Stencils:
    def __init__(self, rows, width):
        self.rows, self.width = rows, width
        self.lane = iota2((rows, LANES), 1)
        self.line = iota2((TILE, width), 0)

    def left(self, f):
        parts, before = [], 0.0
        for x in range(0, self.width, LANES):
            here = f[:, x : x + LANES]
            parts.append(pltpu.roll(jnp.where(self.lane == LANES - 1, before, here), 1, 1))
            before = here
        return jnp.concatenate(parts, axis=1)

    def right(self, f):
        parts, after = [], 0.0
        for x in reversed(range(0, self.width, LANES)):
            here = f[:, x : x + LANES]
            parts.append(pltpu.roll(jnp.where(self.lane == 0, after, here), LANES - 1, 1))
            after = here
        return jnp.concatenate(parts[::-1], axis=1)

    def south(self, f):
        parts, before = [], 0.0
        for y in range(0, self.rows, TILE):
            here = f[y : y + TILE]
            parts.append(pltpu.roll(jnp.where(self.line == TILE - 1, before, here), 1, 0))
            before = here
        return jnp.concatenate(parts, axis=0)

    def north(self, f):
        parts, after = [], 0.0
        for y in reversed(range(0, self.rows, TILE)):
            here = f[y : y + TILE]
            parts.append(pltpu.roll(jnp.where(self.line == 0, after, here), TILE - 1, 0))
            after = here
        return jnp.concatenate(parts[::-1], axis=0)


    def sx(self, f):
        return self.left(f) + self.right(f) + 6.0 * f

    def dx(self, f):
        return self.right(f) - self.left(f)

    def sy(self, f):
        return self.south(f) + self.north(f) + 6.0 * f

    def dy(self, f):
        return self.north(f) - self.south(f)

    def deformation(self, field):
        f = []
        for i in range(3):
            low, mid, high = field(i, -1), field(i, 0), field(i, 1)
            zs = low + high + 6.0 * mid
            zd = high - low
            grads = [self.sy(self.sx(zd)), self.dy(self.sx(zs)), self.sy(self.dx(zs))]
            f.append([(1.0 / 128.0) * g for g in grads])
            f[i][i] = f[i][i] + 1.0
        return f

    def force(self, stress, i):
        zd = stress(i, 1) - stress(i, -1)
        ys = stress(3 + i, -1) + stress(3 + i, 1) + 6.0 * stress(3 + i, 0)
        xs = stress(6 + i, -1) + stress(6 + i, 1) + 6.0 * stress(6 + i, 0)
        return self.sy(self.sx(zd) + self.dx(xs)) + self.dy(self.sx(ys))


def sine(x, terms=6):
    y = x * x
    c = 1.0
    for n in range(2 * terms, 0, -2):
        c = 1.0 - y * (1.0 / (n * (n + 1))) * c
    return x * c


def cosine(x):
    y = x * x
    c = 1.0
    for n in (13, 11, 9, 7, 5, 3, 1):
        c = 1.0 - y * (1.0 / (n * (n + 1))) * c
    return c


def directions(index):
    theta = -1.0 + index * (2.0 / (NFIB - 1))
    triple = 3.0 * index
    turns = jnp.floor(triple * (0.5 / np.pi) + 0.5)
    triple = (triple - turns * 6.28125) - turns * (2.0 * np.pi - 6.28125)
    tilt = 0.3 * sine(triple, 10)
    flat = cosine(tilt)
    return [sine(tilt), flat * sine(theta), flat * cosine(theta)]


def halves(x):
    high = x.astype(BF16)
    return high, (x - high.astype(F32)).astype(BF16)


def excite_kernel(
    slabs, states, cond_hbm, ten_hbm, fib_hbm, disp_hbm,
    out_hbm, ten_out, act_hbm, shift_hbm, pull_hbm,
    ubuf, out, cond, tension, coeff, dif, act_win, zeros, fix_win, fiber, passive, shifted, pull, pooled,
    load_sem, store_sem, sz, rz, sc, rc, sy, ry, sa, ra, sf, rf, sg, relay, sv, rv,
):
    grp = lax.axis_index("grp")
    slab = lax.axis_index("slab")
    col = lax.axis_index("col")
    other = 1 - col
    depth, rows, width = out.shape[1:]
    tiles = rows // TILE
    has_up = slab < slabs - 1
    has_dn = slab > 0
    edge_src = rows - (rows - TILE) * col
    edge_dst = (rows + TILE) * col

    load_u = pltpu.make_async_copy(
        states.at[0], ubuf.at[0, pl.ds(1, depth), pl.ds(TILE, rows), :], load_sem.at[0]
    )
    load_g = pltpu.make_async_copy(
        states.at[pl.ds(1, 3)], out.at[pl.ds(1, 3)], load_sem.at[1]
    )
    load_c = pltpu.make_async_copy(cond_hbm, cond, load_sem.at[2])
    load_t = pltpu.make_async_copy(ten_hbm, tension, load_sem.at[3])
    load_u.start()
    load_c.start()
    load_g.start()
    load_t.start()
    half = rows // 4
    span = half + TILE
    own = pl.ds(pl.multiple_of(TILE * col, TILE), half)
    near = pl.ds(TILE, TILE)
    far = pl.ds(pl.multiple_of(2 * TILE * col, TILE), TILE)
    load_d = pltpu.make_async_copy(
        disp_hbm.at[:, 0], fix_win.at[RADIUS, pl.ds(0, 3), own, :], load_sem.at[4]
    )
    load_f = pltpu.make_async_copy(fib_hbm, fiber, load_sem.at[5])
    load_d.start()
    load_f.start()

    barrier = pltpu.get_barrier_semaphore()

    def greet(where):
        pl.semaphore_signal(barrier, inc=1, device_id=where, device_id_type=MESH)

    def there(d):
        return (slab + d >= 0) & (slab + d < slabs)

    peers = 0
    for d in PEERS:
        valid = there(d)
        wide = abs(d) <= REACH
        count = (0 if d == 0 else 1) + (1 if wide else 0)
        peers = peers + count * valid.astype(jnp.int32)

        @pl.when(valid)
        def _(d=d, wide=wide):
            if wide:
                greet((grp, slab + d, other))
            if d != 0:
                greet((grp, slab + d, col))

    zeros[...] = jnp.zeros(zeros.shape, F32)

    def blank_a(d):
        return pltpu.make_async_copy(zeros, act_hbm.at[d + REACH], ra.at[d + REACH, 0])

    for d in range(-RADIUS, RADIUS + 1):

        @pl.when(jnp.logical_not(there(d)))
        def _(d=d):
            fix_win[d + RADIUS] = jnp.zeros(fix_win.shape[1:], F32)
            if abs(d) <= REACH:
                blank_a(d).start()

    def row_of(step):
        return jnp.where(col == 1, step, tiles - 1 - step)

    def copy_z(slot, way, step):
        at = pl.ds(pl.multiple_of(TILE + TILE * row_of(step), TILE), TILE)
        src = depth if way == 0 else 1
        dst = 0 if way == 0 else depth + 1
        to = slab + 1 if way == 0 else slab - 1
        return pltpu.make_async_remote_copy(
            src_ref=ubuf.at[slot, src, at, :],
            dst_ref=ubuf.at[slot, dst, at, :],
            send_sem=sz.at[way],
            recv_sem=rz.at[slot, way, step],
            device_id=(grp, to, col),
            device_id_type=MESH,
        )

    def carried(step, count):
        return lax.rem((step + 1) * count, tiles) < count

    beside = 1 - 2 * lax.rem(slab, 2)
    chips = slabs // 2
    upper = tiles * (chips - 1 - slab // 2) // chips
    lower = tiles * (slab // 2) // chips
    even = beside == 1
    mine = jnp.where(even, lower, upper)
    others = jnp.where(even, upper, lower)
    onward = 1 - lax.rem(slab + 1, 2)

    def copy_via(slot, way, step):
        at = pl.ds(pl.multiple_of(TILE + TILE * row_of(step), TILE), TILE)
        to = pl.ds(pl.multiple_of(TILE * row_of(step), TILE), TILE)
        return pltpu.make_async_remote_copy(
            src_ref=ubuf.at[slot, depth if way == 0 else 1, at, :],
            dst_ref=relay.at[slot, to, :],
            send_sem=sz.at[way],
            recv_sem=rv.at[slot, step],
            device_id=(grp, slab + beside, col),
            device_id_type=MESH,
        )

    def copy_on(slot, step):
        at = pl.ds(pl.multiple_of(TILE * row_of(step), TILE), TILE)
        to = pl.ds(pl.multiple_of(TILE + TILE * row_of(step), TILE), TILE)
        return pltpu.make_async_remote_copy(
            src_ref=relay.at[slot, at, :],
            dst_ref=ubuf.at[slot, onward * (depth + 1), to, :],
            send_sem=sv.at[slot, step],
            recv_sem=rz.at[slot, onward, step],
            device_id=(grp, slab + 2 * beside, col),
            device_id_type=MESH,
        )

    def hand_on(n):
        @pl.when((n < SUB * tiles) & carried(n % tiles, others))
        def _():
            copy_via(n // tiles, 0, n % tiles).wait_recv()
            copy_on(n // tiles, n % tiles).start()

    def copy_c(slot, way):
        at = depth + 1 if way == 0 else 0
        return pltpu.make_async_remote_copy(
            src_ref=ubuf.at[slot, at, pl.ds(pl.multiple_of(edge_src, TILE), TILE), :],
            dst_ref=ubuf.at[slot, at, pl.ds(pl.multiple_of(edge_dst, TILE), TILE), :],
            send_sem=sc.at[way],
            recv_sem=rc.at[slot, way],
            device_id=(grp, slab, other),
            device_id_type=MESH,
        )

    def copy_y(slot):
        return pltpu.make_async_remote_copy(
            src_ref=ubuf.at[slot, pl.ds(1, depth), pl.ds(pl.multiple_of(edge_src, TILE), TILE), :],
            dst_ref=ubuf.at[slot, pl.ds(1, depth), pl.ds(pl.multiple_of(edge_dst, TILE), TILE), :],
            send_sem=sy.at[0],
            recv_sem=ry.at[slot],
            device_id=(grp, slab, other),
            device_id_type=MESH,
        )

    def both(do_up, do_dn):
        pl.when(has_up)(do_up)
        pl.when(has_dn)(do_dn)

    def send_z(n, by_partner):
        slot = n // tiles
        step = n % tiles
        via = carried(step, mine)

        def send(way):
            through = via & (jnp.logical_not(even) if way == 0 else even)
            if by_partner:
                pl.when(through)(lambda: copy_via(slot, way, step).start())
            else:
                pl.when(jnp.logical_not(through))(lambda: copy_z(slot, way, step).start())

        @pl.when(n < SUB * tiles)
        def _():
            both(lambda: send(0), lambda: send(1))

    def send_c(slot):
        both(lambda: copy_c(slot, 0).start(), lambda: copy_c(slot, 1).start())

    def recv_z(slot, step):
        both(lambda: copy_z(slot, 1, step).wait_recv(), lambda: copy_z(slot, 0, step).wait_recv())

    def recv_c(slot):
        both(lambda: copy_c(slot, 0).wait_recv(), lambda: copy_c(slot, 1).wait_recv())

    def copy_f(source, d, n):
        slot = RADIUS + source - d
        return pltpu.make_async_remote_copy(
            src_ref=fix_win.at[RADIUS + source, :, own, :],
            dst_ref=fix_win.at[slot, :, own, :],
            send_sem=sf.at[n],
            recv_sem=rf.at[slot],
            device_id=(grp, slab + d, col),
            device_id_type=MESH,
        )

    def come_f(e):
        return pltpu.make_async_remote_copy(
            src_ref=fix_win.at[RADIUS, :, own, :],
            dst_ref=fix_win.at[RADIUS + e, :, own, :],
            send_sem=sf.at[0],
            recv_sem=rf.at[RADIUS + e],
            device_id=(grp, slab + e, col),
            device_id_type=MESH,
        )

    def share_f(whose):
        return pltpu.make_async_remote_copy(
            src_ref=fix_win.at[:, :, near, :],
            dst_ref=fix_win.at[:, :, pl.ds(pl.multiple_of(2 * TILE * whose, TILE), TILE), :],
            send_sem=sg.at[0],
            recv_sem=sg.at[1],
            device_id=(grp, slab, other),
            device_id_type=MESH,
        )

    def forward_f(act):
        for n, d in enumerate(BEYOND):
            ok = there(d) & (jnp.abs(d - beside) <= RADIUS)
            pl.when(ok)(lambda n=n, d=d: act(n, d))

    def relay_f(n, d):
        return copy_f(beside, d, 1 + len(ALONG) + n)

    pl.semaphore_wait(barrier, peers)

    load_u.wait()
    send_z(0, True)
    send_z(0, False)
    copy_y(0).start()
    send_z(1, True)
    send_z(1, False)
    load_d.wait()
    load_f.wait()
    fix_win[RADIUS, 3, own, :] = fiber[0].astype(F32)
    copy_f(0, beside, 0).start()
    for n, d in enumerate(ALONG):
        pl.when(there(d))(lambda n=n, d=d: copy_f(0, d, 1 + n).start())

    def initial(step, c):
        send_z(step, True)
        pl.when(step < tiles - HOLD)(lambda: send_z(step, False))
        return c

    lax.fori_loop(2, tiles, initial, 0)

    blank = jnp.zeros((TILE, width), F32)

    def clear_y(n, c):
        ubuf[n // (depth + 2), n % (depth + 2), pl.ds(pl.multiple_of(edge_dst, TILE), TILE), :] = blank
        return c

    lax.fori_loop(0, SUB * (depth + 2), clear_y, 0)

    def clear_z(layer):
        per = rows // TILE + 2

        def body(n, c):
            ubuf[n // per, layer, pl.ds(pl.multiple_of((n % per) * TILE, TILE), TILE), :] = blank
            return c

        lax.fori_loop(0, SUB * per, body, 0)

    @pl.when(slab == 0)
    def _():
        clear_z(0)

    @pl.when(slab == slabs - 1)
    def _():
        clear_z(depth + 1)

    load_c.wait()

    spread_x = (iota2((256, 512), 0) % 128 == iota2((256, 512), 1) // 4).astype(BF16)
    spread_y = (iota2((rows, rows // 4), 0) // 4 == iota2((rows, rows // 4), 1)).astype(BF16)
    for c in range(6):
        tall = [
            jnp.dot(spread_y, part, preferred_element_type=F32).astype(BF16)
            for part in halves(cond[c, 0])
        ]
        for h in range(width // 512):
            part = jnp.concatenate([t[:, h * 128 : (h + 1) * 128] for t in tall], axis=1)
            part = jnp.dot(part, spread_x, preferred_element_type=F32)
            coeff[c, :, h * 512 : (h + 1) * 512] = part if c < 3 else 0.5 * part

    def centre_weight(t, c):
        at = pl.ds(pl.multiple_of(TILE * t, TILE), TILE)
        coeff[6, at, :] = 1.0 - 2.0 * (coeff[0, at, :] + coeff[1, at, :] + coeff[2, at, :])
        return c

    lax.fori_loop(0, tiles, centre_weight, 0)

    load_g.wait()
    load_t.wait()

    lane = iota2((TILE, width), 1)

    def left(f):
        return jnp.where(lane == 0, 0.0, pltpu.roll(f, 1, 1))

    def right(f):
        return jnp.where(lane == width - 1, 0.0, pltpu.roll(f, width - 1, 1))

    line = iota2((TILE, width), 0)

    def north_south(tall):
        here = tall[TILE : 2 * TILE]
        return (
            pltpu.roll(jnp.where(line == 0, tall[2 * TILE :], here), TILE - 1, 0),
            pltpu.roll(jnp.where(line == TILE - 1, tall[:TILE], here), 1, 0),
        )

    def layer(k, z, r):
        base = pl.multiple_of(TILE * r, TILE)
        here = pl.ds(base, TILE)
        tall = pl.ds(base, 3 * TILE)
        below = ubuf[k, z, tall, :]
        mid = ubuf[k, z + 1, tall, :]
        above = ubuf[k, z + 2, tall, :]
        odd = above - below
        centre = mid[TILE : 2 * TILE]
        odd0 = odd[TILE : 2 * TILE]
        north, south = north_south(mid)
        odd_north, odd_south = north_south(odd)
        slope = north - south
        total = coeff[6, here, :] * centre
        total = total + coeff[0, here, :] * (above[TILE : 2 * TILE] + below[TILE : 2 * TILE])
        total = total + coeff[1, here, :] * (north + south)
        total = total + coeff[2, here, :] * (right(centre) + left(centre))
        total = total + coeff[3, here, :] * (odd_north - odd_south)
        total = total + coeff[4, here, :] * (right(odd0) - left(odd0))
        total = total + coeff[5, here, :] * (right(slope) - left(slope))
        dif[...] = total
        up = pl.ds(pl.multiple_of(base + TILE, TILE), TILE)
        for x in range(0, width, CHUNK):
            xs = pl.ds(x, CHUNK)
            du, v2, w2, s2 = ionic(
                ubuf[k, z + 1, up, xs], out[1, z, here, xs], out[2, z, here, xs],
                out[3, z, here, xs],
            )
            u2 = dif[:, xs] + du
            ubuf[k + 1, z + 1, up, xs] = u2
            out[0, z, here, xs] = u2
            out[1, z, here, xs] = v2
            out[2, z, here, xs] = w2
            out[3, z, here, xs] = s2

    def leave(step):
        at = pl.ds(pl.multiple_of(TILE * row_of(step), TILE), TILE)
        return pltpu.make_async_copy(
            out.at[:, :, at, :], out_hbm.at[:, :, at, :], store_sem.at[step]
        )

    pair_x = (iota2((256, 128), 0) // 2 == iota2((256, 128), 1)).astype(F32)
    pair_2 = (iota2((512, 128), 0) % 256 // 2 == iota2((512, 128), 1)).astype(BF16)
    pair_y2 = (iota2((half, 2 * half), 0) == iota2((half, 2 * half), 1) // 2).astype(F32)

    def pool_lanes(rows_in, weights, size, chunk):
        parts = halves(rows_in)
        for h in range(width // chunk):
            both_halves = jnp.concatenate(
                [part[:, h * chunk : (h + 1) * chunk] for part in parts], axis=1
            )
            pooled[h, 0:size] = jnp.dot(both_halves, weights, preferred_element_type=F32)

    def tense(p):
        fine = pl.ds(pl.multiple_of(2 * TILE * p, 2 * TILE), 2 * TILE)
        wide = pl.ds(pl.multiple_of(TILE * p, TILE), TILE)
        sums = []
        for q in range(depth // 2):
            layers = out[0, 2 * q, fine, :] + out[0, 2 * q + 1, fine, :]
            sums.append(layers + pltpu.roll(layers, 2 * TILE - 1, 0))
        pool_lanes(0.125 * jnp.concatenate(sums, axis=0), pair_2, TILE * depth, 256)
        for h in range(width // 256):
            xo = slice(h * 128, (h + 1) * 128)
            for q in range(depth // 2):
                mean = pooled[h, pl.ds(2 * TILE * q, TILE, 2), :]
                before = tension[q, wide, xo]
                tension[q, wide, xo] = before + 0.5 * (mean - before)

    pool_x = (iota2((1024, 128), 0) % 512 // 4 == iota2((1024, 128), 1)).astype(BF16)

    def activate(part, lines):
        fine = pl.ds(pl.multiple_of(4 * TILE * part, 4 * TILE), 4 * TILE)
        layers = out[0, 0, fine, :]
        for z in range(1, depth):
            layers = layers + out[0, z, fine, :]
        layers = layers + pltpu.roll(layers, 4 * TILE - 1, 0)
        layers = layers + pltpu.roll(layers, 4 * TILE - 2, 0)
        pool_lanes((0.5 / (16 * depth)) * layers, pool_x, 4 * TILE, 512)
        for h in range(width // 512):
            xo = slice(h * 128, (h + 1) * 128)
            act_win[lines, xo] = act_win[lines, xo] + pooled[h, pl.ds(0, TILE, 4), :]

    def copy_a(d, to, kind, lines, at):
        return pltpu.make_async_remote_copy(
            src_ref=act_win.at[lines, :],
            dst_ref=act_hbm.at[REACH - d, at, :],
            send_sem=sa.at[d + REACH, kind],
            recv_sem=ra.at[REACH - d, kind],
            device_id=(grp, slab + d, to),
            device_id_type=MESH,
        )

    def keep_a(kind, lines):
        return pltpu.make_async_copy(
            act_win.at[lines, :], act_hbm.at[REACH, lines, :], sa.at[REACH, kind]
        )

    def each_a(act, centre):
        for d in sorted(range(-REACH, REACH + 1), key=lambda d: -abs(d)):
            if d != 0 or centre:
                pl.when(there(d))(lambda d=d: act(d))

    mech = Stencils(span, fix_win.shape[3])

    def inside(j):
        return there(j - RADIUS)

    def prepare(j):
        ok = inside(j)
        f = mech.deformation(lambda i, d: fix_win[j + d, i])
        fdir = directions(fix_win[j, 3])
        pieces = first_piola(f)
        for n in range(9):
            passive[n, j - 1] = jnp.where(ok, pieces[n], 0.0)
        for i in range(3):
            g = 0.5 * (f[i][0] * fdir[0] + f[i][1] * fdir[1] + f[i][2] * fdir[2])
            pull[i, j - 1] = jnp.where(ok, g, 0.0)
            pull[3 + i, j - 1] = fdir[i]

    def shift(j):
        ok = inside(j)
        for i in range(3):
            force = mech.force(lambda n, d: passive[n, j - 1 + d], i)
            moved = fix_win[j, i] + (MECH_RATE / 128.0) * force
            shifted[i, j - 2] = jnp.where(ok, moved, 0.0)

    hand_shift = pltpu.make_async_copy(shifted, shift_hbm, load_sem.at[0])
    hand_pull = pltpu.make_async_copy(pull, pull_hbm, load_sem.at[1])

    for h in range(width // 512):
        xs = slice(h * 256, (h + 1) * 256)
        layers = tension[0, :, xs] + tension[1, :, xs]
        mean = jnp.dot(layers, pair_x, precision=HI, preferred_element_type=F32)
        mean = 0.0625 * jnp.dot(pair_y2, mean, precision=HI, preferred_element_type=F32)
        act_win[own, h * 128 : (h + 1) * 128] = mean

    def within(n):
        k = n // tiles
        r = row_of(n % tiles)

        def inner(m, c):
            layer(k, m, r)
            return c

        lax.fori_loop(1, depth - 1, inner, 0)

    recv_z(0, 0)
    send_c(0)
    copy_y(0).wait_recv()
    within(0)

    def chunk(n, c):
        k = n // tiles
        step = n % tiles
        r = row_of(step)

        @pl.when(n < LAG - 1)
        def _():
            hand_on(2 * n + 1)
            hand_on(2 * n + 2)

        pl.when(n >= LAG - 1)(lambda: hand_on(n + LAG))

        @pl.when(n == tiles // 2)
        def _():
            come_f(beside).wait_recv()

        for far_by in (2, 4, 6):

            @pl.when(n == tiles // 2 + far_by // 2 - 1)
            def _(far_by=far_by):
                forward_f(lambda n, d: relay_f(n, d).start() if abs(d) == far_by else None)

        @pl.when(n == JOIN)
        def _():
            for d in range(-RADIUS, RADIUS + 1):
                if d != 0:
                    arrives = there(d) if d % 2 == 0 else there(d) & (beside != d)
                    pl.when(arrives)(lambda d=d: come_f(d).wait_recv())
            share_f(col).start()

        @pl.when(n == JOIN + 2)
        def _():
            share_f(col).wait_recv()

        @pl.when(step < tiles - 1)
        def _():
            recv_z(k, step + 1)

        @pl.when(step == 0)
        def _():
            recv_c(k)

        def outer(m, c):
            layer(k, m * (depth - 1), r)
            return c

        lax.fori_loop(0, 2, outer, 0)

        send_z(n + tiles, True)
        send_z(n + tiles - HOLD, False)

        @pl.when((k < SUB - 1) & (step == 0))
        def _():
            copy_y(k + 1).start()

        @pl.when((k < SUB - 1) & (step == tiles - 1))
        def _():
            recv_z(k + 1, 0)
            send_c(k + 1)
            copy_y(k + 1).wait_recv()

        @pl.when(n < SUB * tiles - 1)
        def _():
            within(n + 1)

        turn = n - JOIN - 2
        stress_turn = (turn < 2) | (turn % 2 == 0)

        @pl.when((turn >= 0) & (turn < LAST) & stress_turn)
        def _():
            prepare(jnp.where(turn < 2, turn + 1, turn // 2 + 2))

        @pl.when((turn >= 3) & (turn < LAST) & jnp.logical_not(stress_turn))
        def _():
            shift((turn + 1) // 2)

        @pl.when(turn == LAST)
        def _():
            hand_shift.start()
            hand_pull.start()

        @pl.when(k == SUB - 1)
        def _():
            leave(step).start()

        @pl.when(n == SUB * tiles - 1 - tiles // 2)
        def _():
            activate(other, near)
            each_a(lambda d: copy_a(d, col, 0, near, near).start(), False)
            each_a(lambda d: copy_a(d, other, 1, near, far).start(), True)
            keep_a(0, near).start()

        @pl.when((k == SUB - 1) & (step % 2 == 1) & (step < tiles - 1))
        def _():
            tense(r // 2)

        return c

    lax.fori_loop(0, SUB * tiles, chunk, 0)

    activate(col, far)
    each_a(lambda d: copy_a(d, col, 2, far, far).start(), False)
    keep_a(2, far).start()
    tense(row_of(tiles - 1) // 2)
    hand_ten = pltpu.make_async_copy(tension, ten_out, load_sem.at[2])
    hand_ten.start()
    share_f(col).wait_send()
    copy_f(0, beside, 0).wait_send()
    for n, d in enumerate(ALONG):
        pl.when(there(d))(lambda n=n, d=d: copy_f(0, d, 1 + n).wait_send())
    forward_f(lambda n, d: relay_f(n, d).wait_send())
    hand_shift.wait()
    hand_pull.wait()
    def sent(what, sem):
        pltpu.make_async_remote_copy(
            src_ref=what, dst_ref=what, send_sem=sem, recv_sem=sg.at[1],
            device_id=(grp, slab, other), device_id_type=MESH,
        ).wait_send()

    both(lambda: sent(relay, sz.at[0]), lambda: sent(relay, sz.at[1]))
    corners = ubuf.at[0, pl.ds(0, SUB), pl.ds(0, TILE), :]
    both(lambda: sent(corners, sc.at[0]), lambda: sent(corners, sc.at[1]))
    sent(ubuf.at[pl.ds(0, SUB), pl.ds(1, depth), pl.ds(0, TILE), :], sy.at[0])

    def drain(n, c):
        pl.when(carried(n % tiles, others))(lambda: copy_on(n // tiles, n % tiles).wait_send())
        return c

    lax.fori_loop(0, SUB * tiles, drain, 0)

    def left_all(step, c):
        leave(step).wait()
        return c

    lax.fori_loop(0, tiles, left_all, 0)
    each_a(lambda d: copy_a(d, col, 0, near, near).wait_send(), False)
    each_a(lambda d: copy_a(d, other, 1, near, far).wait_send(), True)
    each_a(lambda d: copy_a(d, col, 2, far, far).wait_send(), False)
    for d in range(-REACH, REACH + 1):
        pl.when(jnp.logical_not(there(d)))(lambda d=d: blank_a(d).wait())
    each_a(lambda d: copy_a(-d, col, 0, near, near).wait_recv(), False)
    each_a(lambda d: copy_a(-d, other, 1, near, far).wait_recv(), True)
    each_a(lambda d: copy_a(-d, col, 2, far, far).wait_recv(), False)
    hand_ten.wait()
    keep_a(0, near).wait()
    keep_a(2, far).wait()


def excite(slabs, states, cond, tension, fiber, disp):
    _, depth, rows, width = states.shape
    tiles = rows // TILE
    full = rows // 4 + TILE
    across = cond.shape[3]
    hbm = pl.BlockSpec(memory_space=pltpu.HBM)
    window = (2 * REACH + 1, full, across)
    shifts = (3, 2 * REACH - 1, full, across)
    pulls = (6, 2 * REACH + 1, full, across)
    dma = pltpu.SemaphoreType.DMA
    return pl.pallas_call(
        functools.partial(excite_kernel, slabs),
        out_shape=(
            jax.ShapeDtypeStruct(states.shape, F32),
            jax.ShapeDtypeStruct(tension.shape, F32),
            jax.ShapeDtypeStruct(window, F32),
            jax.ShapeDtypeStruct(shifts, F32),
            jax.ShapeDtypeStruct(pulls, F32),
        ),
        in_specs=[hbm, hbm, hbm, hbm, hbm],
        out_specs=(hbm, hbm, hbm, hbm, hbm),
        scratch_shapes=[
            pltpu.VMEM((SUB + 1, depth + 2, rows + 2 * TILE, width), F32),
            pltpu.VMEM(states.shape, F32),
            pltpu.VMEM(cond.shape, F32),
            pltpu.VMEM(tension.shape, F32),
            pltpu.VMEM((7, rows, width), F32),
            pltpu.VMEM((TILE, width), F32),
            pltpu.VMEM(window[1:], F32),
            pltpu.VMEM(window[1:], F32),
            pltpu.VMEM((2 * RADIUS + 1, 4, full, across), F32),
            pltpu.VMEM(fiber.shape, jnp.int32),
            pltpu.VMEM((9, *window), F32),
            pltpu.VMEM(shifts, F32),
            pltpu.VMEM(pulls, F32),
            pltpu.VMEM((width // 256, 4 * TILE, 128), F32),
            dma((6,)),
            dma((tiles,)),
            dma((2,)),
            dma((SUB, 2, tiles)),
            dma((2,)),
            dma((SUB, 2)),
            dma((1,)),
            dma((SUB,)),
            dma((2 * REACH + 1, 3)),
            dma((2 * REACH + 1, 3)),
            dma((1 + len(ALONG) + len(BEYOND),)),
            dma((2 * RADIUS + 1,)),
            dma((2,)),
            pltpu.VMEM((SUB, rows, width), F32),
            dma((SUB, tiles)),
            dma((SUB, tiles)),
        ],
        compiler_params=pltpu.CompilerParams(
            collective_id=0, has_side_effects=True, vmem_limit_bytes=61 << 20
        ),
        cost_estimate=pl.CostEstimate(
            flops=200_000_000, bytes_accessed=16 << 20, transcendentals=6_000_000
        ),
        name="excite",
    )(states, cond, tension, fiber, disp)


def mech_kernel(
    slabs, act_hbm, shift_hbm, pull_hbm, ten_in, states_in,
    disp_hbm, cond_hbm, ten_out, states_out,
    disp_out, cond_out, active, shifted, pull, stress, moved, held, tension, sem,
):
    slab = lax.axis_index("slab")
    first = lax.axis_index("col") == 0
    rows, width = active.shape[1:]
    half = rows - TILE
    load_a = pltpu.make_async_copy(act_hbm, active, sem.at[0])
    load_p = pltpu.make_async_copy(pull_hbm, pull, sem.at[1])
    load_s = pltpu.make_async_copy(shift_hbm, shifted, sem.at[2])
    load_a.start()
    load_p.start()
    load_s.start()
    fetch = [pltpu.make_async_copy(ten_in, tension, sem.at[3])]
    pass_on = [pltpu.make_async_copy(tension, ten_out, sem.at[8])]
    for n in range(4):
        fetch.append(pltpu.make_async_copy(states_in.at[n], held.at[n], sem.at[4 + n]))
        pass_on.append(pltpu.make_async_copy(held.at[n], states_out.at[n], sem.at[9 + n]))
    for copy in fetch:
        copy.start()
    mech = Stencils(rows, width)

    def inside(j):
        zz = slab + j - REACH
        return (zz >= 0) & (zz < slabs)

    def tense(j, c):
        for a in range(3):
            t = active[j] * pull[3 + a, j]
            for i in range(3):
                stress[3 * a + i, j] = t * pull[i, j]
        return c

    def move(field):
        def body(j, c):
            ok = inside(j)
            for i in range(3):
                force = mech.force(lambda n, d: stress[n, j + d], i)
                moved[i, j] = jnp.where(ok, field(i, j) + (MECH_RATE / 128.0) * force, 0.0)
            return c

        return body

    def strain(j, c):
        ok = inside(j)
        f = mech.deformation(lambda i, d: moved[i, j + d])
        pieces = first_piola(f, active[j], [pull[3 + a, j] for a in range(3)])
        for n in range(9):
            stress[n, j] = jnp.where(ok, pieces[n], 0.0)
        return c

    load_a.wait()
    load_p.wait()
    for j in range(2 * REACH + 1):
        tense(j, 0)
    load_s.wait()
    for j in range(1, 2 * REACH):
        move(lambda i, j: shifted[i, j - 1])(j, 0)
    for got, copy in zip(fetch, pass_on):
        got.wait()
        copy.start()
    for j in range(2, 2 * REACH - 1):
        strain(j, 0)
    for j in range(3, 2 * REACH - 2):
        move(lambda i, j: moved[i, j])(j, 0)

    for i in range(3):
        whole = moved[i, REACH]
        disp_out[i, 0] = jnp.where(first, whole[:half], whole[TILE:])
    store_d = pltpu.make_async_copy(disp_out, disp_hbm, sem.at[0])
    store_d.start()
    comps = metric(
        mech.deformation(lambda i, d: moved[i, REACH + d]),
        [pull[3 + a, REACH] for a in range(3)],
    )
    for n in range(6):
        cond_out[n, 0] = jnp.where(first, comps[n][:half], comps[n][TILE:])
    store_c = pltpu.make_async_copy(cond_out, cond_hbm, sem.at[1])
    store_c.start()
    store_d.wait()
    for copy in pass_on:
        copy.wait()
    store_c.wait()


def mechanics(slabs, active, shifted, pull, tension, states):
    _, full, width = active.shape
    rows = full - TILE
    hbm = pl.BlockSpec(memory_space=pltpu.HBM)
    return pl.pallas_call(
        functools.partial(mech_kernel, slabs),
        out_shape=(
            jax.ShapeDtypeStruct((3, 1, rows, width), F32),
            jax.ShapeDtypeStruct((6, 1, rows, width), F32),
            jax.ShapeDtypeStruct(tension.shape, F32),
            jax.ShapeDtypeStruct(states.shape, F32),
        ),
        in_specs=[hbm, hbm, hbm, hbm, hbm],
        out_specs=(hbm, hbm, hbm, hbm),
        scratch_shapes=[
            pltpu.VMEM((3, 1, rows, width), F32),
            pltpu.VMEM((6, 1, rows, width), F32),
            pltpu.VMEM(active.shape, F32),
            pltpu.VMEM(shifted.shape, F32),
            pltpu.VMEM(pull.shape, F32),
            pltpu.VMEM((9, 2 * REACH + 1, full, width), F32),
            pltpu.VMEM((3, 2 * REACH + 1, full, width), F32),
            pltpu.VMEM(states.shape, F32),
            pltpu.VMEM(tension.shape, F32),
            pltpu.SemaphoreType.DMA((13,)),
        ],
        compiler_params=pltpu.CompilerParams(vmem_limit_bytes=61 << 20),
        name="mechanics",
    )(active, shifted, pull, tension, states)


def on_device(slabs, states, cond, tension, fiber, disp):
    states_next, tension_next, active, shifted, pull = excite(
        slabs, states, cond, tension, fiber, disp
    )
    disp_next, cond_next, tension_next, states_next = mechanics(
        slabs, active, shifted, pull, tension_next, states_next
    )
    return states_next, tension_next, disp_next, cond_next


def solution(mesh):
    wide = P(None, ("grp", "slab"), "col", None)
    flat = P(("grp", "slab"), "col", None)
    return jax.shard_map(
        functools.partial(on_device, mesh.shape["slab"]),
        mesh=mesh,
        in_specs=(wide, wide, flat, flat, wide),
        out_specs=(wide, flat, wide, wide),
        check_vma=False,
    )
```
